256 devices in a mesh: seq: 64 (over y, z, core), tp: 4 (over x).
Axes of the slice: x: 4, y: 4, z: 8, core: 2. Of those that a mesh axis runs over, the one named last changes fastest.
Arguments:
- queries_short: bfloat16 [128, 4, 2304], P('seq', None, 'tp'), may hold values from -4 to 4
- cache_short: bfloat16 [2, 128, 1024, 2304], P(None, 'seq', None, 'tp'), may hold values from -260 to 260
- fresh_short: bfloat16 [2, 128, 4, 2304], P(None, 'seq', None, 'tp'), may hold values from -260 to 260
- short_len: int32 [128], P('seq'), may hold values from 1 to 1024, as said below
- queries_long: bfloat16 [4, 4, 2304], P(None, None, 'tp'), may hold values from -4 to 4
- cache_long: bfloat16 [2, 4, 16384, 2304], P(None, None, 'seq', 'tp'), may hold values from -260 to 260
- fresh_long: bfloat16 [2, 4, 4, 2304], P(None, None, None, 'tp'), may hold values from -260 to 260
- long_len: int32 [4], replicated, may hold values from 8192 to 16384, as said below
- block_live: int32 [4, 128], P(None, 'seq'), may hold values 0 or 1
- out_weight: bfloat16 [2304, 2304], P('tp'), may hold values from -0.125 to 0.125
Outputs:
- short_out: bfloat16 [128, 4, 2304], P('seq', None, 'tp')
- long_out: bfloat16 [4, 4, 2304], P(None, None, 'tp')
The draws below stay inside these ranges and needn't reach their ends.
Inputs may be any that keep to these rules, and one draw needn't show every extreme that they name: `short_len`: some short request fills all 1024 slots. `long_len`: some long request fills all 16384 slots.
All inputs are finite; a program needn't handle non-finite values. No bound on the sum of `block_live` on one device may be relied on, other than what follows from the above.
Results may differ from the reference program's by a relative error of at most 0.011.
Values sent between devices are 32-bit elements; how exact they have to be, the bound alone decides.
A program may use at most 64 MiB of HBM per device.

```python
import math
import jax
import jax.numpy as jnp
from jax import lax

D = 2304
HEADS = 36
HEAD_DIM = 64
NEW = 4
SHORT = 1024
BLOCK = 128
LONG = 4
LONG_DEV = 256
FEAT = 2304
REQ = 128
LONG_LEN = 16384


def aligned_set(key, rows, seg_len, nseg, salt):
    base = jax.random.fold_in(key, salt)
    keys_list = jax.random.split(base, 10)
    root = math.sqrt(HEAD_DIM)
    query = jnp.clip(jax.random.normal(keys_list[0], (rows, NEW, HEADS, HEAD_DIM), jnp.float32), -4.0, 4.0)
    gains = jax.random.uniform(keys_list[2], (rows, NEW, nseg, HEADS), jnp.float32, 2.0, 11.0)
    last_gain = jax.random.uniform(keys_list[9], (rows, NEW, HEADS), jnp.float32, 9.0, 13.0)
    gains = gains.at[:, :, nseg - 1, :].set(last_gain)
    self_gain = jax.random.uniform(keys_list[3], (rows, NEW, HEADS), jnp.float32, 9.0, 13.0)
    slots = jax.random.randint(keys_list[4], (rows, NEW, nseg), 0, seg_len // NEW)
    offsets = slots * NEW + jnp.arange(NEW, dtype=jnp.int32)[None, :, None]
    cache_keys = 0.5 * jnp.clip(jax.random.normal(keys_list[5], (rows, nseg, seg_len, HEADS, HEAD_DIM), jnp.float32), -4.0, 4.0)
    within = jnp.arange(seg_len, dtype=jnp.int32)
    for token in range(NEW):
        hit = (within[None, None, :] == offsets[:, token, :, None]).astype(jnp.float32)
        lifted = query[:, token][:, None, None, :, :] * (gains[:, token][:, :, None, :, None] / root)
        cache_keys = cache_keys + hit[:, :, :, None, None] * lifted
    cache_values = 2.0 * jnp.clip(jax.random.normal(keys_list[6], (rows, nseg * seg_len, HEADS, HEAD_DIM), jnp.float32), -4.0, 4.0)
    fresh_keys = 0.5 * jnp.clip(jax.random.normal(keys_list[7], (rows, NEW, HEADS, HEAD_DIM), jnp.float32), -4.0, 4.0)
    fresh_keys = fresh_keys + query * (self_gain[..., None] / root)
    fresh_values = 2.0 * jnp.clip(jax.random.normal(keys_list[8], (rows, NEW, HEADS, HEAD_DIM), jnp.float32), -4.0, 4.0)
    width = HEADS * HEAD_DIM
    cache = jnp.stack([cache_keys.reshape(rows, nseg * seg_len, width), cache_values.reshape(rows, nseg * seg_len, width)])
    fresh = jnp.stack([fresh_keys.reshape(rows, NEW, width), fresh_values.reshape(rows, NEW, width)])
    return (query.reshape(rows, NEW, width), cache, fresh)


def short_set(key):
    return aligned_set(key, REQ, SHORT // 4, 4, 11)


def long_set(key):
    return aligned_set(key, LONG, LONG_DEV, LONG_LEN // LONG_DEV, 23)


def draw_queries_short(key, part):
    return short_set(key)[0].astype(jnp.bfloat16)


def draw_cache_short(key, part):
    return short_set(key)[1].astype(jnp.bfloat16)


def draw_fresh_short(key, part):
    return short_set(key)[2].astype(jnp.bfloat16)


def draw_queries_long(key, part):
    return long_set(key)[0].astype(jnp.bfloat16)


def draw_cache_long(key, part):
    return long_set(key)[1].astype(jnp.bfloat16)


def draw_fresh_long(key, part):
    return long_set(key)[2].astype(jnp.bfloat16)


def draw_short_len(key, part):
    first, second = jax.random.split(jax.random.fold_in(key, 5))
    lengths = jax.random.randint(first, (REQ,), 1, SHORT + 1)
    chosen = jax.random.randint(second, (), 0, REQ)
    return lengths.at[chosen].set(SHORT).astype(jnp.int32)


def draw_long_len(key, part):
    first, second = jax.random.split(jax.random.fold_in(key, 7))
    lengths = jax.random.randint(first, (LONG,), LONG_LEN // 2, LONG_LEN + 1)
    chosen = jax.random.randint(second, (), 0, LONG)
    return lengths.at[chosen].set(LONG_LEN).astype(jnp.int32)


def plant(result, stream_key, smallest, top_value):
    extent = result.shape
    place = [jax.random.randint(jax.random.fold_in(stream_key, axis), (), 0, extent[axis]) for axis in range(len(extent))]
    result = result.at[tuple(place)].set(smallest)
    longest = extent.index(max(extent))
    place[longest] = (place[longest] + 1) % extent[longest]
    return result.at[tuple(place)].set(top_value)


def block_levels(own_key, dims, shards, low, largest):
    gain = 1.0
    for dim, shards_of in shards:
        draws = jax.random.uniform(jax.random.fold_in(jax.random.fold_in(own_key, 6), dim), (shards_of,), jnp.float32, low / len(shards), largest / len(shards))
        gain = gain * jnp.repeat(jnp.exp(draws), dims[dim] // shards_of).reshape((-1,) + (1,) * (len(dims) - 1 - dim))
    return gain


def bell_draw(own_key, extent, deviation, most, pieces=(), kind=jnp.bfloat16):
    values = jax.random.normal(own_key, extent, jnp.float32) * deviation
    if len(pieces) > 0:
        values = block_levels(own_key, extent, pieces, -0.22, 0.18) * values
    return jnp.clip(values, min=-most, max=most).astype(kind)


def setup_inputs(seed: int = 0) -> dict:
    key_list = jax.random.split(jax.random.key(seed), 11)
    queries_short = draw_queries_short(jax.random.fold_in(key_list[10], 71), 0)
    cache_short = draw_cache_short(jax.random.fold_in(key_list[10], 71), 0)
    fresh_short = draw_fresh_short(jax.random.fold_in(key_list[10], 71), 0)
    short_len = draw_short_len(jax.random.fold_in(key_list[10], 71), 0)
    queries_long = draw_queries_long(jax.random.fold_in(key_list[10], 71), 0)
    cache_long = draw_cache_long(jax.random.fold_in(key_list[10], 71), 0)
    fresh_long = draw_fresh_long(jax.random.fold_in(key_list[10], 71), 0)
    long_len = draw_long_len(jax.random.fold_in(key_list[10], 71), 0)
    block_live = plant((jax.random.randint(key_list[8], (LONG, LONG_LEN // BLOCK), 0, 4) < 3).astype(jnp.int32), jax.random.fold_in(key_list[8], 1), 0, 1)
    out_weight = bell_draw(key_list[9], (FEAT, D), FEAT ** -0.5, 0.125, ((0, 4),))
    return dict(queries_short=queries_short, cache_short=cache_short, fresh_short=fresh_short, short_len=short_len, queries_long=queries_long, cache_long=cache_long, fresh_long=fresh_long, long_len=long_len, block_live=block_live, out_weight=out_weight)


NEGATIVE = -1e+30

def attend(query, keys, values, usable, fresh_keys, fresh_values):
    count = query.shape[0]
    heads = query.shape[1] // HEAD_DIM
    scale = 1.0 / math.sqrt(HEAD_DIM)
    query_heads = query.astype(jnp.float32).reshape(count, heads, HEAD_DIM)
    key_heads = keys.astype(jnp.float32).reshape(-1, heads, HEAD_DIM)
    value_heads = values.astype(jnp.float32).reshape(-1, heads, HEAD_DIM)
    fresh_key_heads = fresh_keys.astype(jnp.float32).reshape(count, heads, HEAD_DIM)
    fresh_value_heads = fresh_values.astype(jnp.float32).reshape(count, heads, HEAD_DIM)
    scores = jnp.einsum('jhd,phd->hjp', query_heads, key_heads, precision=lax.Precision.HIGHEST) * scale
    scores = jnp.where(usable[None, None, :], scores, NEGATIVE)
    fresh_scores = jnp.einsum('jhd,ihd->hji', query_heads, fresh_key_heads, precision=lax.Precision.HIGHEST) * scale
    causal = (jnp.arange(count)[:, None] >= jnp.arange(count)[None, :])[None]
    fresh_scores = jnp.where(causal, fresh_scores, NEGATIVE)
    highest = jnp.maximum(lax.optimization_barrier(jnp.max(scores, axis=-1)), lax.optimization_barrier(jnp.max(fresh_scores, axis=-1)))
    expo = jnp.where(usable[None, None, :], jnp.exp(scores - highest[..., None]), 0.0)
    fresh_expo = jnp.where(causal, jnp.exp(fresh_scores - highest[..., None]), 0.0)
    totals = lax.optimization_barrier(jnp.sum(expo, axis=-1)) + lax.optimization_barrier(jnp.sum(fresh_expo, axis=-1))
    weights = lax.optimization_barrier(expo.astype(jnp.bfloat16)).astype(jnp.float32)
    fresh_weights = lax.optimization_barrier(fresh_expo.astype(jnp.bfloat16)).astype(jnp.float32)
    summed = jnp.einsum('hjp,phd->hjd', weights, value_heads, precision=lax.Precision.HIGHEST)
    summed = summed + jnp.einsum('hji,ihd->hjd', fresh_weights, fresh_value_heads, precision=lax.Precision.HIGHEST)
    normed = (summed / totals[..., None]).astype(jnp.bfloat16)
    return jnp.transpose(normed, (1, 0, 2)).reshape(count, heads * HEAD_DIM)

def attend_tuple(items):
    return attend(items[0], items[1], items[2], items[3], items[4], items[5])

def reference(queries_short, cache_short, fresh_short, short_len, queries_long, cache_long, fresh_long, long_len, block_live, out_weight):
    short_usable = jnp.arange(SHORT, dtype=jnp.int32)[None, :] < short_len[:, None]
    short_att = lax.map(attend_tuple, (queries_short, cache_short[0], cache_short[1], short_usable, fresh_short[0], fresh_short[1]))
    live = jnp.repeat(block_live, BLOCK, axis=1) == 1
    long_usable = (jnp.arange(LONG_LEN, dtype=jnp.int32)[None, :] < long_len[:, None]) & live
    long_att = lax.map(attend_tuple, (queries_long, cache_long[0], cache_long[1], long_usable, fresh_long[0], fresh_long[1]))
    short_out = jnp.dot(short_att.reshape(-1, FEAT), out_weight, preferred_element_type=jnp.float32).astype(jnp.bfloat16)
    long_out = jnp.dot(long_att.reshape(-1, FEAT), out_weight, preferred_element_type=jnp.float32).astype(jnp.bfloat16)
    return (short_out.reshape(REQ, NEW, D), long_out.reshape(LONG, NEW, D))
```

```python
import functools
import math

import jax
import jax.numpy as jnp
from jax import lax
from jax.experimental import pallas as pl
from jax.experimental.pallas import tpu as pltpu
from jax.sharding import PartitionSpec as P

HEAD_DIM = 64
MESH = pl.DeviceIdType.MESH
LANES = 128


NEGATIVE = -1e30


def split_heads(tensor):
    return tensor.reshape(tensor.shape[0], tensor.shape[1], tensor.shape[2] // HEAD_DIM, HEAD_DIM)


def partial_softmax(query_heads, key_heads, value_heads, usable):
    scores = jnp.einsum(
        "rjhd,rphd->rhjp", query_heads, key_heads, preferred_element_type=jnp.float32
    ) * (1.0 / math.sqrt(HEAD_DIM))
    scores = jnp.where(usable, scores, NEGATIVE)
    highest = jnp.max(scores, axis=-1)
    expo = jnp.where(usable, jnp.exp(scores - highest[..., None]), 0.0)
    totals = jnp.sum(expo, axis=-1)
    summed = jnp.einsum(
        "rhjp,rphd->rhjd",
        expo.astype(jnp.bfloat16),
        value_heads,
        preferred_element_type=jnp.float32,
    )
    return (highest, totals, summed)


def combine_parts(first, second):
    highest = jnp.maximum(first[0], second[0])
    scale_first = jnp.exp(first[0] - highest)
    scale_second = jnp.exp(second[0] - highest)
    totals = first[1] * scale_first + second[1] * scale_second
    summed = first[2] * scale_first[..., None] + second[2] * scale_second[..., None]
    return (highest, totals, summed)


def finish(parts):
    normed = (parts[2] / parts[1][..., None]).astype(jnp.bfloat16)
    normed = jnp.transpose(normed, (0, 2, 1, 3))
    return normed.reshape(normed.shape[0], normed.shape[1], normed.shape[2] * normed.shape[3])


def fresh_part(queries, fresh):
    count = queries.shape[1]
    causal = (jnp.arange(count)[:, None] >= jnp.arange(count)[None, :])[None, None]
    return partial_softmax(
        split_heads(queries), split_heads(fresh[0]), split_heads(fresh[1]), causal
    )


def merge_states(low, high):
    lane = lax.broadcasted_iota(jnp.int32, low.shape, 1)
    top_low = low[:, HEAD_DIM : HEAD_DIM + 1]
    top_high = high[:, HEAD_DIM : HEAD_DIM + 1]
    top = jnp.maximum(top_low, top_high)
    mixed = low * jnp.exp(top_low - top) + high * jnp.exp(top_high - top)
    return jnp.where(lane == HEAD_DIM, top, mixed)


def butterfly_kernel(rounds, x_ref, o_ref, state, recv, send_sem, recv_sem):
    me = lax.axis_index("seq")
    column = lax.axis_index("tp")
    partners = []
    for k in range(rounds):
        step = 1 << k
        bit = (me // step) % 2
        partners.append((me + step - 2 * step * bit, bit))
    barrier = pltpu.get_barrier_semaphore()
    for partner, _ in partners:
        pl.semaphore_signal(
            barrier, inc=1, device_id=(partner, column), device_id_type=MESH
        )
    pl.semaphore_wait(barrier, rounds)
    for k in range(rounds):
        partner, bit = partners[k]
        source = x_ref if k == 0 else state.at[k - 1]
        copy = pltpu.make_async_remote_copy(
            src_ref=source,
            dst_ref=recv.at[k],
            send_sem=send_sem.at[k],
            recv_sem=recv_sem.at[k],
            device_id=(partner, column),
            device_id_type=MESH,
        )
        copy.start()
        copy.wait()
        mine = source[...]
        theirs = recv[k]
        first = bit == 0
        merged = merge_states(
            jnp.where(first, mine, theirs), jnp.where(first, theirs, mine)
        )
        if k == rounds - 1:
            o_ref[...] = merged
        else:
            state[k] = merged


def seq_allreduce(packed, devices):
    rounds = devices.bit_length() - 1
    rows = packed.shape[0]
    return pl.pallas_call(
        functools.partial(butterfly_kernel, rounds),
        out_shape=jax.ShapeDtypeStruct(packed.shape, jnp.float32),
        in_specs=[pl.BlockSpec(memory_space=pltpu.VMEM)],
        out_specs=pl.BlockSpec(memory_space=pltpu.VMEM),
        scratch_shapes=[
            pltpu.VMEM((max(rounds - 1, 1), rows, LANES), jnp.float32),
            pltpu.VMEM((rounds, rows, LANES), jnp.float32),
            pltpu.SemaphoreType.DMA((rounds,)),
            pltpu.SemaphoreType.DMA((rounds,)),
        ],
        compiler_params=pltpu.CompilerParams(collective_id=0, has_side_effects=True),
        cost_estimate=pl.CostEstimate(
            flops=8 * rows * LANES * rounds,
            transcendentals=2 * rows * rounds,
            bytes_accessed=2 * rows * LANES * 4 * rounds,
        ),
    )(packed)


def per_device(
    queries_short,
    cache_short,
    fresh_short,
    short_len,
    queries_long,
    cache_long,
    fresh_long,
    long_len,
    block_live,
    out_weight,
):
    short_query = split_heads(queries_short)
    request_count = queries_short.shape[0]
    token_count = queries_short.shape[1]
    positions = cache_short.shape[2]
    usable = (jnp.arange(positions, dtype=jnp.int32)[None, :] < short_len[:, None])[
        :, None, None, :
    ]
    short_parts = partial_softmax(
        short_query, split_heads(cache_short[0]), split_heads(cache_short[1]), usable
    )
    short_att = finish(combine_parts(short_parts, fresh_part(queries_short, fresh_short)))
    local_len = cache_long.shape[2]
    spots = lax.axis_index("seq") * local_len + jnp.arange(local_len, dtype=jnp.int32)
    live = jnp.repeat(block_live, local_len // block_live.shape[1], axis=1) == 1
    long_usable = ((spots[None, :] < long_len[:, None]) & live)[:, None, None, :]
    long_parts = partial_softmax(
        split_heads(queries_long),
        split_heads(cache_long[0]),
        split_heads(cache_long[1]),
        long_usable,
    )
    highest_long, totals_long, summed_long = long_parts
    shape = highest_long.shape
    rows = highest_long.size
    packed = jnp.concatenate(
        [
            summed_long.reshape(rows, HEAD_DIM),
            highest_long.reshape(rows, 1),
            totals_long.reshape(rows, 1),
            jnp.zeros((rows, LANES - HEAD_DIM - 2), jnp.float32),
        ],
        axis=1,
    )
    reduced = seq_allreduce(packed, lax.axis_size("seq"))
    merged = (
        reduced[:, HEAD_DIM].reshape(shape),
        reduced[:, HEAD_DIM + 1].reshape(shape),
        reduced[:, :HEAD_DIM].reshape(shape + (HEAD_DIM,)),
    )
    long_att = finish(combine_parts(merged, fresh_part(queries_long, fresh_long)))
    short_term = jnp.dot(
        short_att.reshape(-1, short_att.shape[2]), out_weight, preferred_element_type=jnp.float32
    )
    long_term = jnp.dot(
        long_att.reshape(-1, long_att.shape[2]), out_weight, preferred_element_type=jnp.float32
    )
    short_cols = lax.psum_scatter(short_term, "tp", scatter_dimension=1, tiled=True)
    long_cols = lax.psum_scatter(long_term, "tp", scatter_dimension=1, tiled=True)
    short_out = short_cols.astype(jnp.bfloat16).reshape(
        request_count, token_count, short_cols.shape[1]
    )
    long_out = long_cols.astype(jnp.bfloat16).reshape(
        long_att.shape[0], long_att.shape[1], long_cols.shape[1]
    )
    return (short_out, long_out)


def solution(mesh):
    in_specs = (
        P("seq", None, "tp"),
        P(None, "seq", None, "tp"),
        P(None, "seq", None, "tp"),
        P("seq"),
        P(None, None, "tp"),
        P(None, None, "seq", "tp"),
        P(None, None, None, "tp"),
        P(),
        P(None, "seq"),
        P("tp", None),
    )
    out_specs = (P("seq", None, "tp"), P(None, None, "tp"))
    return jax.shard_map(
        per_device, mesh=mesh, in_specs=in_specs, out_specs=out_specs, check_vma=False
    )
```

```python
import functools
import math

import jax
import jax.numpy as jnp
from jax import lax
from jax.experimental import pallas as pl
from jax.experimental.pallas import tpu as pltpu
from jax.sharding import PartitionSpec as P

HEAD_DIM = 64
MESH = pl.DeviceIdType.MESH
LANES = 128


NEGATIVE = -1e30


def split_heads(tensor):
    return tensor.reshape(tensor.shape[0], tensor.shape[1], tensor.shape[2] // HEAD_DIM, HEAD_DIM)


def partial_softmax(query_heads, key_heads, value_heads, usable):
    scores = jnp.einsum(
        "rjhd,rphd->rhjp", query_heads, key_heads, preferred_element_type=jnp.float32
    ) * (1.0 / math.sqrt(HEAD_DIM))
    scores = jnp.where(usable, scores, NEGATIVE)
    highest = jnp.max(scores, axis=-1)
    expo = jnp.where(usable, jnp.exp(scores - highest[..., None]), 0.0)
    totals = jnp.sum(expo, axis=-1)
    summed = jnp.einsum(
        "rhjp,rphd->rhjd",
        expo.astype(jnp.bfloat16),
        value_heads,
        preferred_element_type=jnp.float32,
    )
    return (highest, totals, summed)


def combine_parts(first, second):
    highest = jnp.maximum(first[0], second[0])
    scale_first = jnp.exp(first[0] - highest)
    scale_second = jnp.exp(second[0] - highest)
    totals = first[1] * scale_first + second[1] * scale_second
    summed = first[2] * scale_first[..., None] + second[2] * scale_second[..., None]
    return (highest, totals, summed)


def finish(parts):
    normed = (parts[2] / parts[1][..., None]).astype(jnp.bfloat16)
    normed = jnp.transpose(normed, (0, 2, 1, 3))
    return normed.reshape(normed.shape[0], normed.shape[1], normed.shape[2] * normed.shape[3])


def fresh_part(queries, fresh):
    count = queries.shape[1]
    causal = (jnp.arange(count)[:, None] >= jnp.arange(count)[None, :])[None, None]
    return partial_softmax(
        split_heads(queries), split_heads(fresh[0]), split_heads(fresh[1]), causal
    )


def merge_states(low, high):
    lane = lax.broadcasted_iota(jnp.int32, low.shape, 1)
    top_low = low[:, HEAD_DIM : HEAD_DIM + 1]
    top_high = high[:, HEAD_DIM : HEAD_DIM + 1]
    top = jnp.maximum(top_low, top_high)
    mixed = low * jnp.exp(top_low - top) + high * jnp.exp(top_high - top)
    return jnp.where(lane == HEAD_DIM, top, mixed)


def butterfly_kernel(rounds, x_ref, o_ref, state, recv, send_sem, recv_sem):
    me = lax.axis_index("seq")
    column = lax.axis_index("tp")
    partners = []
    for k in range(rounds):
        step = 1 << k
        bit = (me // step) % 2
        partners.append((me + step - 2 * step * bit, bit))
    barrier = pltpu.get_barrier_semaphore()
    for partner, _ in partners:
        pl.semaphore_signal(
            barrier, inc=1, device_id=(partner, column), device_id_type=MESH
        )
    pl.semaphore_wait(barrier, rounds)
    for k in range(rounds):
        partner, bit = partners[k]
        source = x_ref if k == 0 else state.at[k - 1]
        copy = pltpu.make_async_remote_copy(
            src_ref=source,
            dst_ref=recv.at[k],
            send_sem=send_sem.at[k],
            recv_sem=recv_sem.at[k],
            device_id=(partner, column),
            device_id_type=MESH,
        )
        copy.start()
        copy.wait()
        mine = source[...]
        theirs = recv[k]
        first = bit == 0
        merged = merge_states(
            jnp.where(first, mine, theirs), jnp.where(first, theirs, mine)
        )
        if k == rounds - 1:
            o_ref[...] = merged
        else:
            state[k] = merged


def seq_allreduce(packed, devices):
    rounds = devices.bit_length() - 1
    rows = packed.shape[0]
    return pl.pallas_call(
        functools.partial(butterfly_kernel, rounds),
        out_shape=jax.ShapeDtypeStruct(packed.shape, jnp.float32),
        in_specs=[pl.BlockSpec(memory_space=pltpu.VMEM)],
        out_specs=pl.BlockSpec(memory_space=pltpu.VMEM),
        scratch_shapes=[
            pltpu.VMEM((max(rounds - 1, 1), rows, LANES), jnp.float32),
            pltpu.VMEM((rounds, rows, LANES), jnp.float32),
            pltpu.SemaphoreType.DMA((rounds,)),
            pltpu.SemaphoreType.DMA((rounds,)),
        ],
        compiler_params=pltpu.CompilerParams(collective_id=0, has_side_effects=True),
        cost_estimate=pl.CostEstimate(
            flops=8 * rows * LANES * rounds,
            transcendentals=2 * rows * rounds,
            bytes_accessed=2 * rows * LANES * 4 * rounds,
        ),
    )(packed)


def scatter_kernel(parts, x_ref, o_ref, recv, local_sem, send_sem, recv_sem):
    me = lax.axis_index("tp")
    row = lax.axis_index("seq")
    barrier = pltpu.get_barrier_semaphore()
    for d in range(1, parts):
        pl.semaphore_signal(
            barrier, inc=1, device_id=(row, (me + d) % parts), device_id_type=MESH
        )
    pl.semaphore_wait(barrier, parts - 1)
    own = pltpu.make_async_copy(x_ref.at[me], recv.at[me], local_sem)
    own.start()
    copies = []
    for d in range(1, parts):
        copy = pltpu.make_async_remote_copy(
            src_ref=x_ref.at[(me + d) % parts],
            dst_ref=recv.at[me],
            send_sem=send_sem.at[d - 1],
            recv_sem=recv_sem.at[d - 1],
            device_id=(row, (me + d) % parts),
            device_id_type=MESH,
        )
        copy.start()
        copies.append(copy)
    own.wait()
    for d in range(1, parts):
        copies[d - 1].wait_send()
        pltpu.make_async_remote_copy(
            src_ref=x_ref.at[0],
            dst_ref=recv.at[(me + parts - d) % parts],
            send_sem=send_sem.at[d - 1],
            recv_sem=recv_sem.at[d - 1],
            device_id=(row, (me + parts - d) % parts),
            device_id_type=MESH,
        ).wait_recv()
    total = recv[0]
    for s in range(1, parts):
        total = total + recv[s]
    o_ref[...] = total


def tp_reduce_scatter(term, parts):
    rows, width = term.shape
    cols = width // parts
    blocks = jnp.transpose(term.reshape(rows, parts, cols), (1, 0, 2))
    return pl.pallas_call(
        functools.partial(scatter_kernel, parts),
        out_shape=jax.ShapeDtypeStruct((rows, cols), jnp.float32),
        in_specs=[pl.BlockSpec(memory_space=pltpu.VMEM)],
        out_specs=pl.BlockSpec(memory_space=pltpu.VMEM),
        scratch_shapes=[
            pltpu.VMEM((parts, rows, cols), jnp.float32),
            pltpu.SemaphoreType.DMA(()),
            pltpu.SemaphoreType.DMA((parts - 1,)),
            pltpu.SemaphoreType.DMA((parts - 1,)),
        ],
        compiler_params=pltpu.CompilerParams(collective_id=1, has_side_effects=True),
        cost_estimate=pl.CostEstimate(
            flops=rows * width,
            transcendentals=0,
            bytes_accessed=3 * rows * width * 4,
        ),
    )(blocks)


def per_device(
    queries_short,
    cache_short,
    fresh_short,
    short_len,
    queries_long,
    cache_long,
    fresh_long,
    long_len,
    block_live,
    out_weight,
):
    short_query = split_heads(queries_short)
    request_count = queries_short.shape[0]
    token_count = queries_short.shape[1]
    positions = cache_short.shape[2]
    usable = (jnp.arange(positions, dtype=jnp.int32)[None, :] < short_len[:, None])[
        :, None, None, :
    ]
    short_parts = partial_softmax(
        short_query, split_heads(cache_short[0]), split_heads(cache_short[1]), usable
    )
    short_att = finish(combine_parts(short_parts, fresh_part(queries_short, fresh_short)))
    local_len = cache_long.shape[2]
    spots = lax.axis_index("seq") * local_len + jnp.arange(local_len, dtype=jnp.int32)
    live = jnp.repeat(block_live, local_len // block_live.shape[1], axis=1) == 1
    long_usable = ((spots[None, :] < long_len[:, None]) & live)[:, None, None, :]
    long_parts = partial_softmax(
        split_heads(queries_long),
        split_heads(cache_long[0]),
        split_heads(cache_long[1]),
        long_usable,
    )
    highest_long, totals_long, summed_long = long_parts
    shape = highest_long.shape
    rows = highest_long.size
    packed = jnp.concatenate(
        [
            summed_long.reshape(rows, HEAD_DIM),
            highest_long.reshape(rows, 1),
            totals_long.reshape(rows, 1),
            jnp.zeros((rows, LANES - HEAD_DIM - 2), jnp.float32),
        ],
        axis=1,
    )
    reduced = seq_allreduce(packed, lax.axis_size("seq"))
    merged = (
        reduced[:, HEAD_DIM].reshape(shape),
        reduced[:, HEAD_DIM + 1].reshape(shape),
        reduced[:, :HEAD_DIM].reshape(shape + (HEAD_DIM,)),
    )
    long_att = finish(combine_parts(merged, fresh_part(queries_long, fresh_long)))
    short_term = jnp.dot(
        short_att.reshape(-1, short_att.shape[2]), out_weight, preferred_element_type=jnp.float32
    )
    long_term = jnp.dot(
        long_att.reshape(-1, long_att.shape[2]), out_weight, preferred_element_type=jnp.float32
    )
    short_cols = lax.psum_scatter(short_term, "tp", scatter_dimension=1, tiled=True)
    long_cols = tp_reduce_scatter(long_term, lax.axis_size("tp"))
    short_out = short_cols.astype(jnp.bfloat16).reshape(
        request_count, token_count, short_cols.shape[1]
    )
    long_out = long_cols.astype(jnp.bfloat16).reshape(
        long_att.shape[0], long_att.shape[1], long_cols.shape[1]
    )
    return (short_out, long_out)


def solution(mesh):
    in_specs = (
        P("seq", None, "tp"),
        P(None, "seq", None, "tp"),
        P(None, "seq", None, "tp"),
        P("seq"),
        P(None, None, "tp"),
        P(None, None, "seq", "tp"),
        P(None, None, None, "tp"),
        P(),
        P(None, "seq"),
        P("tp", None),
    )
    out_specs = (P("seq", None, "tp"), P(None, None, "tp"))
    return jax.shard_map(
        per_device, mesh=mesh, in_specs=in_specs, out_specs=out_specs, check_vma=False
    )
```

```python
import functools
import math

import jax
import jax.numpy as jnp
from jax import lax
from jax.experimental import pallas as pl
from jax.experimental.pallas import tpu as pltpu
from jax.sharding import PartitionSpec as P

HEAD_DIM = 64
MESH = pl.DeviceIdType.MESH
LANES = 128


NEGATIVE = -1e30


def split_heads(tensor):
    return tensor.reshape(tensor.shape[0], tensor.shape[1], tensor.shape[2] // HEAD_DIM, HEAD_DIM)


def partial_softmax(query_heads, key_heads, value_heads, usable):
    scores = jnp.einsum(
        "rjhd,rphd->rhjp", query_heads, key_heads, preferred_element_type=jnp.float32
    ) * (1.0 / math.sqrt(HEAD_DIM))
    scores = jnp.where(usable, scores, NEGATIVE)
    highest = jnp.max(scores, axis=-1)
    expo = jnp.where(usable, jnp.exp(scores - highest[..., None]), 0.0)
    totals = jnp.sum(expo, axis=-1)
    summed = jnp.einsum(
        "rhjp,rphd->rhjd",
        expo.astype(jnp.bfloat16),
        value_heads,
        preferred_element_type=jnp.float32,
    )
    return (highest, totals, summed)


def combine_parts(first, second):
    highest = jnp.maximum(first[0], second[0])
    scale_first = jnp.exp(first[0] - highest)
    scale_second = jnp.exp(second[0] - highest)
    totals = first[1] * scale_first + second[1] * scale_second
    summed = first[2] * scale_first[..., None] + second[2] * scale_second[..., None]
    return (highest, totals, summed)


def finish(parts):
    normed = (parts[2] / parts[1][..., None]).astype(jnp.bfloat16)
    normed = jnp.transpose(normed, (0, 2, 1, 3))
    return normed.reshape(normed.shape[0], normed.shape[1], normed.shape[2] * normed.shape[3])


def fresh_part(queries, fresh):
    count = queries.shape[1]
    causal = (jnp.arange(count)[:, None] >= jnp.arange(count)[None, :])[None, None]
    return partial_softmax(
        split_heads(queries), split_heads(fresh[0]), split_heads(fresh[1]), causal
    )


def merge_states(low, high):
    lane = lax.broadcasted_iota(jnp.int32, low.shape, 1)
    top_low = low[:, HEAD_DIM : HEAD_DIM + 1]
    top_high = high[:, HEAD_DIM : HEAD_DIM + 1]
    top = jnp.maximum(top_low, top_high)
    mixed = low * jnp.exp(top_low - top) + high * jnp.exp(top_high - top)
    return jnp.where(lane == HEAD_DIM, top, mixed)


def butterfly_kernel(rounds, x_ref, o_ref, state, recv, send_sem, recv_sem):
    me = lax.axis_index("seq")
    column = lax.axis_index("tp")
    partners = []
    for k in range(rounds):
        step = 1 << k
        bit = (me // step) % 2
        partners.append((me + step - 2 * step * bit, bit))
    barrier = pltpu.get_barrier_semaphore()
    for partner, _ in partners:
        pl.semaphore_signal(
            barrier, inc=1, device_id=(partner, column), device_id_type=MESH
        )
    pl.semaphore_wait(barrier, rounds)
    for k in range(rounds):
        partner, bit = partners[k]
        source = x_ref if k == 0 else state.at[k - 1]
        copy = pltpu.make_async_remote_copy(
            src_ref=source,
            dst_ref=recv.at[k],
            send_sem=send_sem.at[k],
            recv_sem=recv_sem.at[k],
            device_id=(partner, column),
            device_id_type=MESH,
        )
        copy.start()
        copy.wait()
        mine = source[...]
        theirs = recv[k]
        first = bit == 0
        merged = merge_states(
            jnp.where(first, mine, theirs), jnp.where(first, theirs, mine)
        )
        if k == rounds - 1:
            o_ref[...] = merged
        else:
            state[k] = merged


def seq_allreduce(packed, devices):
    rounds = devices.bit_length() - 1
    rows = packed.shape[0]
    return pl.pallas_call(
        functools.partial(butterfly_kernel, rounds),
        out_shape=jax.ShapeDtypeStruct(packed.shape, jnp.float32),
        in_specs=[pl.BlockSpec(memory_space=pltpu.VMEM)],
        out_specs=pl.BlockSpec(memory_space=pltpu.VMEM),
        scratch_shapes=[
            pltpu.VMEM((max(rounds - 1, 1), rows, LANES), jnp.float32),
            pltpu.VMEM((rounds, rows, LANES), jnp.float32),
            pltpu.SemaphoreType.DMA((rounds,)),
            pltpu.SemaphoreType.DMA((rounds,)),
        ],
        compiler_params=pltpu.CompilerParams(collective_id=0, has_side_effects=True),
        cost_estimate=pl.CostEstimate(
            flops=8 * rows * LANES * rounds,
            transcendentals=2 * rows * rounds,
            bytes_accessed=2 * rows * LANES * 4 * rounds,
        ),
    )(packed)


def scatter_kernel(parts, x_ref, o_ref, recv, local_sem, send_sem, recv_sem):
    me = lax.axis_index("tp")
    row = lax.axis_index("seq")
    barrier = pltpu.get_barrier_semaphore()
    for d in range(1, parts):
        pl.semaphore_signal(
            barrier, inc=1, device_id=(row, (me + d) % parts), device_id_type=MESH
        )
    pl.semaphore_wait(barrier, parts - 1)
    own = pltpu.make_async_copy(x_ref.at[me], recv.at[me], local_sem)
    own.start()
    copies = []
    for d in range(1, parts):
        copy = pltpu.make_async_remote_copy(
            src_ref=x_ref.at[(me + d) % parts],
            dst_ref=recv.at[me],
            send_sem=send_sem.at[d - 1],
            recv_sem=recv_sem.at[d - 1],
            device_id=(row, (me + d) % parts),
            device_id_type=MESH,
        )
        copy.start()
        copies.append(copy)
    own.wait()
    for d in range(1, parts):
        copies[d - 1].wait_send()
        pltpu.make_async_remote_copy(
            src_ref=x_ref.at[0],
            dst_ref=recv.at[(me + parts - d) % parts],
            send_sem=send_sem.at[d - 1],
            recv_sem=recv_sem.at[d - 1],
            device_id=(row, (me + parts - d) % parts),
            device_id_type=MESH,
        ).wait_recv()
    total = recv[0]
    for s in range(1, parts):
        total = total + recv[s]
    o_ref[...] = total


def tp_reduce_scatter(term, parts):
    rows, width = term.shape
    cols = width // parts
    blocks = jnp.transpose(term.reshape(rows, parts, cols), (1, 0, 2))
    return pl.pallas_call(
        functools.partial(scatter_kernel, parts),
        out_shape=jax.ShapeDtypeStruct((rows, cols), jnp.float32),
        in_specs=[pl.BlockSpec(memory_space=pltpu.VMEM)],
        out_specs=pl.BlockSpec(memory_space=pltpu.VMEM),
        scratch_shapes=[
            pltpu.VMEM((parts, rows, cols), jnp.float32),
            pltpu.SemaphoreType.DMA(()),
            pltpu.SemaphoreType.DMA((parts - 1,)),
            pltpu.SemaphoreType.DMA((parts - 1,)),
        ],
        compiler_params=pltpu.CompilerParams(collective_id=1, has_side_effects=True),
        cost_estimate=pl.CostEstimate(
            flops=rows * width,
            transcendentals=0,
            bytes_accessed=3 * rows * width * 4,
        ),
    )(blocks)


def per_device(
    queries_short,
    cache_short,
    fresh_short,
    short_len,
    queries_long,
    cache_long,
    fresh_long,
    long_len,
    block_live,
    out_weight,
):
    short_query = split_heads(queries_short)
    request_count = queries_short.shape[0]
    token_count = queries_short.shape[1]
    positions = cache_short.shape[2]
    usable = (jnp.arange(positions, dtype=jnp.int32)[None, :] < short_len[:, None])[
        :, None, None, :
    ]
    short_parts = partial_softmax(
        short_query, split_heads(cache_short[0]), split_heads(cache_short[1]), usable
    )
    short_att = finish(combine_parts(short_parts, fresh_part(queries_short, fresh_short)))
    local_len = cache_long.shape[2]
    spots = lax.axis_index("seq") * local_len + jnp.arange(local_len, dtype=jnp.int32)
    live = jnp.repeat(block_live, local_len // block_live.shape[1], axis=1) == 1
    long_usable = ((spots[None, :] < long_len[:, None]) & live)[:, None, None, :]
    long_parts = partial_softmax(
        split_heads(queries_long),
        split_heads(cache_long[0]),
        split_heads(cache_long[1]),
        long_usable,
    )
    highest_long, totals_long, summed_long = long_parts
    shape = highest_long.shape
    rows = highest_long.size
    packed = jnp.concatenate(
        [
            summed_long.reshape(rows, HEAD_DIM),
            highest_long.reshape(rows, 1),
            totals_long.reshape(rows, 1),
            jnp.zeros((rows, LANES - HEAD_DIM - 2), jnp.float32),
        ],
        axis=1,
    )
    reduced = seq_allreduce(packed, lax.axis_size("seq"))
    merged = (
        reduced[:, HEAD_DIM].reshape(shape),
        reduced[:, HEAD_DIM + 1].reshape(shape),
        reduced[:, :HEAD_DIM].reshape(shape + (HEAD_DIM,)),
    )
    long_att = finish(combine_parts(merged, fresh_part(queries_long, fresh_long)))
    short_rows = short_att.reshape(-1, short_att.shape[2])
    both = jnp.concatenate([short_rows, long_att.reshape(-1, long_att.shape[2])], axis=0)
    term = jnp.dot(both, out_weight, preferred_element_type=jnp.float32)
    cols = tp_reduce_scatter(term, lax.axis_size("tp")).astype(jnp.bfloat16)
    short_out = cols[: short_rows.shape[0]].reshape(request_count, token_count, cols.shape[1])
    long_out = cols[short_rows.shape[0] :].reshape(
        long_att.shape[0], long_att.shape[1], cols.shape[1]
    )
    return (short_out, long_out)


def solution(mesh):
    in_specs = (
        P("seq", None, "tp"),
        P(None, "seq", None, "tp"),
        P(None, "seq", None, "tp"),
        P("seq"),
        P(None, None, "tp"),
        P(None, None, "seq", "tp"),
        P(None, None, None, "tp"),
        P(),
        P(None, "seq"),
        P("tp", None),
    )
    out_specs = (P("seq", None, "tp"), P(None, None, "tp"))
    return jax.shard_map(
        per_device, mesh=mesh, in_specs=in_specs, out_specs=out_specs, check_vma=False
    )
```

```python
import functools
import math

import jax
import jax.numpy as jnp
from jax import lax
from jax.experimental import pallas as pl
from jax.experimental.pallas import tpu as pltpu
from jax.sharding import PartitionSpec as P

HEAD_DIM = 64
MESH = pl.DeviceIdType.MESH
LANES = 128


NEGATIVE = -1e30


def split_heads(tensor):
    return tensor.reshape(tensor.shape[0], tensor.shape[1], tensor.shape[2] // HEAD_DIM, HEAD_DIM)


def partial_softmax(query_heads, key_heads, value_heads, usable):
    scores = jnp.einsum(
        "rjhd,rphd->rhjp", query_heads, key_heads, preferred_element_type=jnp.float32
    ) * (1.0 / math.sqrt(HEAD_DIM))
    scores = jnp.where(usable, scores, NEGATIVE)
    highest = jnp.max(scores, axis=-1)
    expo = jnp.where(usable, jnp.exp(scores - highest[..., None]), 0.0)
    totals = jnp.sum(expo, axis=-1)
    summed = jnp.einsum(
        "rhjp,rphd->rhjd",
        expo.astype(jnp.bfloat16),
        value_heads,
        preferred_element_type=jnp.float32,
    )
    return (highest, totals, summed)


def combine_parts(first, second):
    highest = jnp.maximum(first[0], second[0])
    scale_first = jnp.exp(first[0] - highest)
    scale_second = jnp.exp(second[0] - highest)
    totals = first[1] * scale_first + second[1] * scale_second
    summed = first[2] * scale_first[..., None] + second[2] * scale_second[..., None]
    return (highest, totals, summed)


def finish(parts):
    normed = (parts[2] / parts[1][..., None]).astype(jnp.bfloat16)
    normed = jnp.transpose(normed, (0, 2, 1, 3))
    return normed.reshape(normed.shape[0], normed.shape[1], normed.shape[2] * normed.shape[3])


def fresh_part(queries, fresh):
    count = queries.shape[1]
    causal = (jnp.arange(count)[:, None] >= jnp.arange(count)[None, :])[None, None]
    return partial_softmax(
        split_heads(queries), split_heads(fresh[0]), split_heads(fresh[1]), causal
    )


def merge_states(low, high):
    lane = lax.broadcasted_iota(jnp.int32, low.shape, 1)
    top_low = low[:, HEAD_DIM : HEAD_DIM + 1]
    top_high = high[:, HEAD_DIM : HEAD_DIM + 1]
    top = jnp.maximum(top_low, top_high)
    mixed = low * jnp.exp(top_low - top) + high * jnp.exp(top_high - top)
    return jnp.where(lane == HEAD_DIM, top, mixed)


def butterfly_kernel(rounds, x_ref, o_ref, state, recv, send_sem, recv_sem):
    me = lax.axis_index("seq")
    column = lax.axis_index("tp")
    partners = []
    for k in range(rounds):
        step = 1 << k
        bit = (me // step) % 2
        partners.append((me + step - 2 * step * bit, bit))
    barrier = pltpu.get_barrier_semaphore()
    for partner, _ in partners:
        pl.semaphore_signal(
            barrier, inc=1, device_id=(partner, column), device_id_type=MESH
        )
    pl.semaphore_wait(barrier, rounds)
    for k in range(rounds):
        partner, bit = partners[k]
        source = x_ref if k == 0 else state.at[k - 1]
        copy = pltpu.make_async_remote_copy(
            src_ref=source,
            dst_ref=recv.at[k],
            send_sem=send_sem.at[k],
            recv_sem=recv_sem.at[k],
            device_id=(partner, column),
            device_id_type=MESH,
        )
        copy.start()
        copy.wait()
        mine = source[...]
        theirs = recv[k]
        first = bit == 0
        merged = merge_states(
            jnp.where(first, mine, theirs), jnp.where(first, theirs, mine)
        )
        if k == rounds - 1:
            o_ref[...] = merged
        else:
            state[k] = merged


def seq_allreduce(packed, devices):
    rounds = devices.bit_length() - 1
    rows = packed.shape[0]
    return pl.pallas_call(
        functools.partial(butterfly_kernel, rounds),
        out_shape=jax.ShapeDtypeStruct(packed.shape, jnp.float32),
        in_specs=[pl.BlockSpec(memory_space=pltpu.VMEM)],
        out_specs=pl.BlockSpec(memory_space=pltpu.VMEM),
        scratch_shapes=[
            pltpu.VMEM((max(rounds - 1, 1), rows, LANES), jnp.float32),
            pltpu.VMEM((rounds, rows, LANES), jnp.float32),
            pltpu.SemaphoreType.DMA((rounds,)),
            pltpu.SemaphoreType.DMA((rounds,)),
        ],
        compiler_params=pltpu.CompilerParams(collective_id=0, has_side_effects=True),
        cost_estimate=pl.CostEstimate(
            flops=8 * rows * LANES * rounds,
            transcendentals=2 * rows * rounds,
            bytes_accessed=2 * rows * LANES * 4 * rounds,
        ),
    )(packed)


def scatter_kernel(parts, x_ref, o_ref, recv, local_sem, send_sem, recv_sem):
    me = lax.axis_index("tp")
    row = lax.axis_index("seq")
    barrier = pltpu.get_barrier_semaphore()
    for d in range(1, parts):
        pl.semaphore_signal(
            barrier, inc=1, device_id=(row, (me + d) % parts), device_id_type=MESH
        )
    pl.semaphore_wait(barrier, parts - 1)
    own = pltpu.make_async_copy(x_ref.at[me], recv.at[me], local_sem)
    own.start()
    copies = []
    for d in range(1, parts):
        copy = pltpu.make_async_remote_copy(
            src_ref=x_ref.at[(me + d) % parts],
            dst_ref=recv.at[me],
            send_sem=send_sem.at[d - 1],
            recv_sem=recv_sem.at[d - 1],
            device_id=(row, (me + d) % parts),
            device_id_type=MESH,
        )
        copy.start()
        copies.append(copy)
    own.wait()
    for d in range(1, parts):
        copies[d - 1].wait_send()
        pltpu.make_async_remote_copy(
            src_ref=x_ref.at[0],
            dst_ref=recv.at[(me + parts - d) % parts],
            send_sem=send_sem.at[d - 1],
            recv_sem=recv_sem.at[d - 1],
            device_id=(row, (me + parts - d) % parts),
            device_id_type=MESH,
        ).wait_recv()
    total = recv[0]
    for s in range(1, parts):
        total = total + recv[s]
    o_ref[...] = total


def tp_reduce_scatter(term, parts):
    rows, width = term.shape
    cols = width // parts
    blocks = jnp.transpose(term.reshape(rows, parts, cols), (1, 0, 2))
    return pl.pallas_call(
        functools.partial(scatter_kernel, parts),
        out_shape=jax.ShapeDtypeStruct((rows, cols), jnp.float32),
        in_specs=[pl.BlockSpec(memory_space=pltpu.VMEM)],
        out_specs=pl.BlockSpec(memory_space=pltpu.VMEM),
        scratch_shapes=[
            pltpu.VMEM((parts, rows, cols), jnp.float32),
            pltpu.SemaphoreType.DMA(()),
            pltpu.SemaphoreType.DMA((parts - 1,)),
            pltpu.SemaphoreType.DMA((parts - 1,)),
        ],
        compiler_params=pltpu.CompilerParams(collective_id=1, has_side_effects=True),
        cost_estimate=pl.CostEstimate(
            flops=rows * width,
            transcendentals=0,
            bytes_accessed=3 * rows * width * 4,
        ),
    )(blocks)


def attention_kernel(with_fresh, q_ref, k_ref, v_ref, mask_ref, *rest):
    tokens, width = q_ref.shape[1], q_ref.shape[2]
    rows = (width // HEAD_DIM) * tokens
    pick = (
        lax.broadcasted_iota(jnp.int32, (rows, tokens), 0) % tokens
        == lax.broadcasted_iota(jnp.int32, (rows, tokens), 1)
    ).astype(jnp.bfloat16)
    head_lanes = (
        lax.broadcasted_iota(jnp.int32, (rows, width), 0) // tokens
        == lax.broadcasted_iota(jnp.int32, (rows, width), 1) // HEAD_DIM
    )
    spread = jnp.dot(pick, q_ref[0], preferred_element_type=jnp.float32)
    query = jnp.where(head_lanes, spread, 0.0).astype(jnp.bfloat16)
    contract = (((1,), (1,)), ((), ()))
    scale = 1.0 / math.sqrt(HEAD_DIM)
    scores = lax.dot_general(
        query, k_ref[0, 0], contract, preferred_element_type=jnp.float32
    ) * scale
    usable = mask_ref[0] != 0
    scores = jnp.where(usable, scores, NEGATIVE)
    highest = jnp.max(scores, axis=1, keepdims=True)
    if with_fresh:
        fk_ref, fv_ref, o_ref = rest
        fresh_scores = lax.dot_general(
            query, fk_ref[0, 0], contract, preferred_element_type=jnp.float32
        ) * scale
        causal = lax.broadcasted_iota(jnp.int32, (rows, tokens), 1) <= (
            lax.broadcasted_iota(jnp.int32, (rows, tokens), 0) % tokens
        )
        fresh_scores = jnp.where(causal, fresh_scores, NEGATIVE)
        highest = jnp.maximum(highest, jnp.max(fresh_scores, axis=1, keepdims=True))
    expo = jnp.where(usable, jnp.exp(scores - highest), 0.0)
    totals = jnp.sum(expo, axis=1, keepdims=True)
    summed = jnp.dot(
        expo.astype(jnp.bfloat16), v_ref[0, 0], preferred_element_type=jnp.float32
    )
    if with_fresh:
        fresh_expo = jnp.where(causal, jnp.exp(fresh_scores - highest), 0.0)
        totals = totals + jnp.sum(fresh_expo, axis=1, keepdims=True)
        summed = summed + jnp.dot(
            fresh_expo.astype(jnp.bfloat16), fv_ref[0, 0], preferred_element_type=jnp.float32
        )
        normed = jnp.where(head_lanes, (summed / totals).astype(jnp.bfloat16), 0.0)
        gather = (
            lax.broadcasted_iota(jnp.int32, (tokens, rows), 1) % tokens
            == lax.broadcasted_iota(jnp.int32, (tokens, rows), 0)
        ).astype(jnp.bfloat16)
        o_ref[0] = jnp.dot(
            gather, normed.astype(jnp.bfloat16), preferred_element_type=jnp.float32
        ).astype(o_ref.dtype)
    else:
        sum_ref, top_ref, total_ref = rest
        sum_ref[0] = summed
        top_ref[0] = highest
        total_ref[0] = totals


def attention(queries, cache, mask, fresh=None):
    count, tokens, width = queries.shape
    positions = cache.shape[2]
    rows = (width // HEAD_DIM) * tokens
    specs = [
        pl.BlockSpec((1, tokens, width), lambda r: (r, 0, 0)),
        pl.BlockSpec((1, 1, positions, width), lambda r: (0, r, 0, 0)),
        pl.BlockSpec((1, 1, positions, width), lambda r: (1, r, 0, 0)),
        pl.BlockSpec((1, 1, positions), lambda r: (r, 0, 0)),
    ]
    operands = [queries, cache, cache, mask]
    if fresh is not None:
        specs += [
            pl.BlockSpec((1, 1, tokens, width), lambda r: (0, r, 0, 0)),
            pl.BlockSpec((1, 1, tokens, width), lambda r: (1, r, 0, 0)),
        ]
        operands += [fresh, fresh]
        out_shape = jax.ShapeDtypeStruct((count, tokens, width), jnp.bfloat16)
        out_specs = pl.BlockSpec((1, tokens, width), lambda r: (r, 0, 0))
    else:
        out_shape = (
            jax.ShapeDtypeStruct((count, rows, width), jnp.float32),
            jax.ShapeDtypeStruct((count, rows, 1), jnp.float32),
            jax.ShapeDtypeStruct((count, rows, 1), jnp.float32),
        )
        out_specs = (
            pl.BlockSpec((1, rows, width), lambda r: (r, 0, 0)),
            pl.BlockSpec((1, rows, 1), lambda r: (r, 0, 0)),
            pl.BlockSpec((1, rows, 1), lambda r: (r, 0, 0)),
        )
    return pl.pallas_call(
        functools.partial(attention_kernel, fresh is not None),
        out_shape=out_shape,
        grid=(count,),
        in_specs=specs,
        out_specs=out_specs,
        cost_estimate=pl.CostEstimate(
            flops=4 * count * rows * positions * width,
            transcendentals=count * rows * positions,
            bytes_accessed=2 * count * positions * width * 2,
        ),
    )(*operands)


def per_device(
    queries_short,
    cache_short,
    fresh_short,
    short_len,
    queries_long,
    cache_long,
    fresh_long,
    long_len,
    block_live,
    out_weight,
):
    request_count = queries_short.shape[0]
    token_count = queries_short.shape[1]
    positions = cache_short.shape[2]
    usable = jnp.arange(positions, dtype=jnp.int32)[None, :] < short_len[:, None]
    short_att = attention(
        queries_short, cache_short, usable.astype(jnp.int32)[:, None, :], fresh_short
    )
    local_len = cache_long.shape[2]
    spots = lax.axis_index("seq") * local_len + jnp.arange(local_len, dtype=jnp.int32)
    live = jnp.repeat(block_live, local_len // block_live.shape[1], axis=1) == 1
    long_usable = (spots[None, :] < long_len[:, None]) & live
    long_sum, long_top, long_total = attention(
        queries_long, cache_long, long_usable.astype(jnp.int32)[:, None, :]
    )
    long_count = queries_long.shape[0]
    heads = queries_long.shape[2] // HEAD_DIM
    diagonal = jnp.eye(heads, dtype=jnp.float32)[None, :, None, :, None]
    long_parts = (
        long_top.reshape(long_count, heads, token_count),
        long_total.reshape(long_count, heads, token_count),
        jnp.sum(
            long_sum.reshape(long_count, heads, token_count, heads, HEAD_DIM) * diagonal,
            axis=3,
        ),
    )
    highest_long, totals_long, summed_long = long_parts
    shape = highest_long.shape
    rows = highest_long.size
    packed = jnp.concatenate(
        [
            summed_long.reshape(rows, HEAD_DIM),
            highest_long.reshape(rows, 1),
            totals_long.reshape(rows, 1),
            jnp.zeros((rows, LANES - HEAD_DIM - 2), jnp.float32),
        ],
        axis=1,
    )
    reduced = seq_allreduce(packed, lax.axis_size("seq"))
    merged = (
        reduced[:, HEAD_DIM].reshape(shape),
        reduced[:, HEAD_DIM + 1].reshape(shape),
        reduced[:, :HEAD_DIM].reshape(shape + (HEAD_DIM,)),
    )
    long_att = finish(combine_parts(merged, fresh_part(queries_long, fresh_long)))
    short_rows = short_att.reshape(-1, short_att.shape[2])
    both = jnp.concatenate([short_rows, long_att.reshape(-1, long_att.shape[2])], axis=0)
    term = jnp.dot(both, out_weight, preferred_element_type=jnp.float32)
    cols = tp_reduce_scatter(term, lax.axis_size("tp")).astype(jnp.bfloat16)
    short_out = cols[: short_rows.shape[0]].reshape(request_count, token_count, cols.shape[1])
    long_out = cols[short_rows.shape[0] :].reshape(
        long_att.shape[0], long_att.shape[1], cols.shape[1]
    )
    return (short_out, long_out)


def solution(mesh):
    in_specs = (
        P("seq", None, "tp"),
        P(None, "seq", None, "tp"),
        P(None, "seq", None, "tp"),
        P("seq"),
        P(None, None, "tp"),
        P(None, None, "seq", "tp"),
        P(None, None, None, "tp"),
        P(),
        P(None, "seq"),
        P("tp", None),
    )
    out_specs = (P("seq", None, "tp"), P(None, None, "tp"))
    return jax.shard_map(
        per_device, mesh=mesh, in_specs=in_specs, out_specs=out_specs, check_vma=False
    )
```

```python
import functools
import math

import jax
import jax.numpy as jnp
from jax import lax
from jax.experimental import pallas as pl
from jax.experimental.pallas import tpu as pltpu
from jax.sharding import PartitionSpec as P

HEAD_DIM = 64
MESH = pl.DeviceIdType.MESH
LANES = 128


NEGATIVE = -1e30


def split_heads(tensor):
    return tensor.reshape(tensor.shape[0], tensor.shape[1], tensor.shape[2] // HEAD_DIM, HEAD_DIM)


def partial_softmax(query_heads, key_heads, value_heads, usable):
    scores = jnp.einsum(
        "rjhd,rphd->rhjp", query_heads, key_heads, preferred_element_type=jnp.float32
    ) * (1.0 / math.sqrt(HEAD_DIM))
    scores = jnp.where(usable, scores, NEGATIVE)
    highest = jnp.max(scores, axis=-1)
    expo = jnp.where(usable, jnp.exp(scores - highest[..., None]), 0.0)
    totals = jnp.sum(expo, axis=-1)
    summed = jnp.einsum(
        "rhjp,rphd->rhjd",
        expo.astype(jnp.bfloat16),
        value_heads,
        preferred_element_type=jnp.float32,
    )
    return (highest, totals, summed)


def combine_parts(first, second):
    highest = jnp.maximum(first[0], second[0])
    scale_first = jnp.exp(first[0] - highest)
    scale_second = jnp.exp(second[0] - highest)
    totals = first[1] * scale_first + second[1] * scale_second
    summed = first[2] * scale_first[..., None] + second[2] * scale_second[..., None]
    return (highest, totals, summed)


def finish(parts):
    normed = (parts[2] / parts[1][..., None]).astype(jnp.bfloat16)
    normed = jnp.transpose(normed, (0, 2, 1, 3))
    return normed.reshape(normed.shape[0], normed.shape[1], normed.shape[2] * normed.shape[3])


def fresh_part(queries, fresh):
    count = queries.shape[1]
    causal = (jnp.arange(count)[:, None] >= jnp.arange(count)[None, :])[None, None]
    return partial_softmax(
        split_heads(queries), split_heads(fresh[0]), split_heads(fresh[1]), causal
    )


def merge_states(low, high):
    lane = lax.broadcasted_iota(jnp.int32, low.shape, 1)
    top_low = low[:, HEAD_DIM : HEAD_DIM + 1]
    top_high = high[:, HEAD_DIM : HEAD_DIM + 1]
    top = jnp.maximum(top_low, top_high)
    mixed = low * jnp.exp(top_low - top) + high * jnp.exp(top_high - top)
    return jnp.where(lane == HEAD_DIM, top, mixed)


def butterfly_kernel(rounds, x_ref, o_ref, state, recv, send_sem, recv_sem):
    me = lax.axis_index("seq")
    column = lax.axis_index("tp")
    partners = []
    for k in range(rounds):
        step = 1 << k
        bit = (me // step) % 2
        partners.append((me + step - 2 * step * bit, bit))
    barrier = pltpu.get_barrier_semaphore()
    for partner, _ in partners:
        pl.semaphore_signal(
            barrier, inc=1, device_id=(partner, column), device_id_type=MESH
        )
    pl.semaphore_wait(barrier, rounds)
    for k in range(rounds):
        partner, bit = partners[k]
        source = x_ref if k == 0 else state.at[k - 1]
        copy = pltpu.make_async_remote_copy(
            src_ref=source,
            dst_ref=recv.at[k],
            send_sem=send_sem.at[k],
            recv_sem=recv_sem.at[k],
            device_id=(partner, column),
            device_id_type=MESH,
        )
        copy.start()
        copy.wait()
        mine = source[...]
        theirs = recv[k]
        first = bit == 0
        merged = merge_states(
            jnp.where(first, mine, theirs), jnp.where(first, theirs, mine)
        )
        if k == rounds - 1:
            o_ref[...] = merged
        else:
            state[k] = merged


def seq_allreduce(packed, devices):
    rounds = devices.bit_length() - 1
    rows = packed.shape[0]
    return pl.pallas_call(
        functools.partial(butterfly_kernel, rounds),
        out_shape=jax.ShapeDtypeStruct(packed.shape, jnp.float32),
        in_specs=[pl.BlockSpec(memory_space=pltpu.VMEM)],
        out_specs=pl.BlockSpec(memory_space=pltpu.VMEM),
        scratch_shapes=[
            pltpu.VMEM((max(rounds - 1, 1), rows, LANES), jnp.float32),
            pltpu.VMEM((rounds, rows, LANES), jnp.float32),
            pltpu.SemaphoreType.DMA((rounds,)),
            pltpu.SemaphoreType.DMA((rounds,)),
        ],
        compiler_params=pltpu.CompilerParams(collective_id=0, has_side_effects=True),
        cost_estimate=pl.CostEstimate(
            flops=8 * rows * LANES * rounds,
            transcendentals=2 * rows * rounds,
            bytes_accessed=2 * rows * LANES * 4 * rounds,
        ),
    )(packed)


def scatter_kernel(parts, x_ref, o_ref, recv, local_sem, send_sem, recv_sem):
    me = lax.axis_index("tp")
    row = lax.axis_index("seq")
    barrier = pltpu.get_barrier_semaphore()
    for d in range(1, parts):
        pl.semaphore_signal(
            barrier, inc=1, device_id=(row, (me + d) % parts), device_id_type=MESH
        )
    pl.semaphore_wait(barrier, parts - 1)
    own = pltpu.make_async_copy(x_ref.at[me], recv.at[me], local_sem)
    own.start()
    copies = []
    for d in range(1, parts):
        copy = pltpu.make_async_remote_copy(
            src_ref=x_ref.at[(me + d) % parts],
            dst_ref=recv.at[me],
            send_sem=send_sem.at[d - 1],
            recv_sem=recv_sem.at[d - 1],
            device_id=(row, (me + d) % parts),
            device_id_type=MESH,
        )
        copy.start()
        copies.append(copy)
    own.wait()
    for d in range(1, parts):
        copies[d - 1].wait_send()
        pltpu.make_async_remote_copy(
            src_ref=x_ref.at[0],
            dst_ref=recv.at[(me + parts - d) % parts],
            send_sem=send_sem.at[d - 1],
            recv_sem=recv_sem.at[d - 1],
            device_id=(row, (me + parts - d) % parts),
            device_id_type=MESH,
        ).wait_recv()
    total = recv[0]
    for s in range(1, parts):
        total = total + recv[s]
    o_ref[...] = total


def tp_reduce_scatter(term, parts):
    rows, width = term.shape
    cols = width // parts
    blocks = jnp.transpose(term.reshape(rows, parts, cols), (1, 0, 2))
    return pl.pallas_call(
        functools.partial(scatter_kernel, parts),
        out_shape=jax.ShapeDtypeStruct((rows, cols), jnp.float32),
        in_specs=[pl.BlockSpec(memory_space=pltpu.VMEM)],
        out_specs=pl.BlockSpec(memory_space=pltpu.VMEM),
        scratch_shapes=[
            pltpu.VMEM((parts, rows, cols), jnp.float32),
            pltpu.SemaphoreType.DMA(()),
            pltpu.SemaphoreType.DMA((parts - 1,)),
            pltpu.SemaphoreType.DMA((parts - 1,)),
        ],
        compiler_params=pltpu.CompilerParams(collective_id=1, has_side_effects=True),
        cost_estimate=pl.CostEstimate(
            flops=rows * width,
            transcendentals=0,
            bytes_accessed=3 * rows * width * 4,
        ),
    )(blocks)


def attention_kernel(with_fresh, len_ref, live_ref, off_ref, q_ref, k_ref, v_ref, *rest):
    tokens, width = q_ref.shape[1], q_ref.shape[2]
    positions = k_ref.shape[3]
    rows = (width // HEAD_DIM) * tokens
    request = pl.program_id(0)
    spot = lax.broadcasted_iota(jnp.int32, (1, positions), 1)
    blocks = live_ref.shape[1]
    alive = spot < 0
    for b in range(blocks):
        alive = alive | ((spot // (positions // blocks) == b) & (live_ref[request, b] == 1))
    usable = alive & (spot + off_ref[0] < len_ref[request])
    pick = (
        lax.broadcasted_iota(jnp.int32, (rows, tokens), 0) % tokens
        == lax.broadcasted_iota(jnp.int32, (rows, tokens), 1)
    ).astype(jnp.bfloat16)
    head_lanes = (
        lax.broadcasted_iota(jnp.int32, (rows, width), 0) // tokens
        == lax.broadcasted_iota(jnp.int32, (rows, width), 1) // HEAD_DIM
    )
    spread = jnp.dot(pick, q_ref[0], preferred_element_type=jnp.float32)
    query = jnp.where(head_lanes, spread, 0.0).astype(jnp.bfloat16)
    contract = (((1,), (1,)), ((), ()))
    scale = 1.0 / math.sqrt(HEAD_DIM)
    scores = jnp.dot(query, k_ref[0, 0], preferred_element_type=jnp.float32) * scale
    scores = jnp.where(usable, scores, NEGATIVE)
    highest = jnp.max(scores, axis=1, keepdims=True)
    if with_fresh:
        fk_ref, fv_ref, o_ref = rest
        fresh_scores = lax.dot_general(
            query, fk_ref[0, 0], contract, preferred_element_type=jnp.float32
        ) * scale
        causal = lax.broadcasted_iota(jnp.int32, (rows, tokens), 1) <= (
            lax.broadcasted_iota(jnp.int32, (rows, tokens), 0) % tokens
        )
        fresh_scores = jnp.where(causal, fresh_scores, NEGATIVE)
        highest = jnp.maximum(highest, jnp.max(fresh_scores, axis=1, keepdims=True))
    expo = jnp.where(usable, jnp.exp(scores - highest), 0.0)
    totals = jnp.sum(expo, axis=1, keepdims=True)
    summed = lax.dot_general(
        expo.astype(jnp.bfloat16), v_ref[0, 0], contract, preferred_element_type=jnp.float32
    )
    if with_fresh:
        fresh_expo = jnp.where(causal, jnp.exp(fresh_scores - highest), 0.0)
        totals = totals + jnp.sum(fresh_expo, axis=1, keepdims=True)
        summed = summed + jnp.dot(
            fresh_expo.astype(jnp.bfloat16), fv_ref[0, 0], preferred_element_type=jnp.float32
        )
        normed = jnp.where(head_lanes, (summed / totals).astype(jnp.bfloat16), 0.0)
        gather = (
            lax.broadcasted_iota(jnp.int32, (tokens, rows), 1) % tokens
            == lax.broadcasted_iota(jnp.int32, (tokens, rows), 0)
        ).astype(jnp.bfloat16)
        o_ref[0] = jnp.dot(
            gather, normed.astype(jnp.bfloat16), preferred_element_type=jnp.float32
        ).astype(o_ref.dtype)
    else:
        sum_ref, top_ref, total_ref = rest
        sum_ref[0] = summed
        top_ref[0] = highest
        total_ref[0] = totals


def attention(queries, cache, lengths, live, offset, fresh=None):
    count, tokens, width = queries.shape
    positions = cache.shape[2]
    rows = (width // HEAD_DIM) * tokens
    flipped = jnp.swapaxes(cache, 2, 3)
    specs = [
        pl.BlockSpec((1, tokens, width), lambda r, *_: (r, 0, 0)),
        pl.BlockSpec((1, 1, width, positions), lambda r, *_: (0, r, 0, 0)),
        pl.BlockSpec((1, 1, width, positions), lambda r, *_: (1, r, 0, 0)),
    ]
    operands = [lengths, live, offset, queries, flipped, flipped]
    if fresh is not None:
        specs += [
            pl.BlockSpec((1, 1, tokens, width), lambda r, *_: (0, r, 0, 0)),
            pl.BlockSpec((1, 1, tokens, width), lambda r, *_: (1, r, 0, 0)),
        ]
        operands += [fresh, fresh]
        out_shape = jax.ShapeDtypeStruct((count, tokens, width), jnp.bfloat16)
        out_specs = pl.BlockSpec((1, tokens, width), lambda r, *_: (r, 0, 0))
    else:
        out_shape = (
            jax.ShapeDtypeStruct((count, rows, width), jnp.float32),
            jax.ShapeDtypeStruct((count, rows, 1), jnp.float32),
            jax.ShapeDtypeStruct((count, rows, 1), jnp.float32),
        )
        out_specs = (
            pl.BlockSpec((1, rows, width), lambda r, *_: (r, 0, 0)),
            pl.BlockSpec((1, rows, 1), lambda r, *_: (r, 0, 0)),
            pl.BlockSpec((1, rows, 1), lambda r, *_: (r, 0, 0)),
        )
    return pl.pallas_call(
        functools.partial(attention_kernel, fresh is not None),
        out_shape=out_shape,
        grid_spec=pltpu.PrefetchScalarGridSpec(
            num_scalar_prefetch=3, grid=(count,), in_specs=specs, out_specs=out_specs
        ),
        cost_estimate=pl.CostEstimate(
            flops=4 * count * rows * positions * width,
            transcendentals=count * rows * positions,
            bytes_accessed=2 * count * positions * width * 2,
        ),
    )(*operands)


def per_device(
    queries_short,
    cache_short,
    fresh_short,
    short_len,
    queries_long,
    cache_long,
    fresh_long,
    long_len,
    block_live,
    out_weight,
):
    request_count = queries_short.shape[0]
    token_count = queries_short.shape[1]
    short_att = attention(
        queries_short,
        cache_short,
        short_len,
        jnp.ones((request_count, 1), jnp.int32),
        jnp.zeros((1,), jnp.int32),
        fresh_short,
    )
    local_len = cache_long.shape[2]
    long_sum, long_top, long_total = attention(
        queries_long,
        cache_long,
        long_len,
        block_live,
        (lax.axis_index("seq") * local_len).astype(jnp.int32).reshape(1),
    )
    long_count = queries_long.shape[0]
    heads = queries_long.shape[2] // HEAD_DIM
    diagonal = jnp.eye(heads, dtype=jnp.float32)[None, :, None, :, None]
    long_parts = (
        long_top.reshape(long_count, heads, token_count),
        long_total.reshape(long_count, heads, token_count),
        jnp.sum(
            long_sum.reshape(long_count, heads, token_count, heads, HEAD_DIM) * diagonal,
            axis=3,
        ),
    )
    highest_long, totals_long, summed_long = long_parts
    shape = highest_long.shape
    rows = highest_long.size
    packed = jnp.concatenate(
        [
            summed_long.reshape(rows, HEAD_DIM),
            highest_long.reshape(rows, 1),
            totals_long.reshape(rows, 1),
            jnp.zeros((rows, LANES - HEAD_DIM - 2), jnp.float32),
        ],
        axis=1,
    )
    reduced = seq_allreduce(packed, lax.axis_size("seq"))
    merged = (
        reduced[:, HEAD_DIM].reshape(shape),
        reduced[:, HEAD_DIM + 1].reshape(shape),
        reduced[:, :HEAD_DIM].reshape(shape + (HEAD_DIM,)),
    )
    long_att = finish(combine_parts(merged, fresh_part(queries_long, fresh_long)))
    short_rows = short_att.reshape(-1, short_att.shape[2])
    both = jnp.concatenate([short_rows, long_att.reshape(-1, long_att.shape[2])], axis=0)
    term = jnp.dot(both, out_weight, preferred_element_type=jnp.float32)
    cols = tp_reduce_scatter(term, lax.axis_size("tp")).astype(jnp.bfloat16)
    short_out = cols[: short_rows.shape[0]].reshape(request_count, token_count, cols.shape[1])
    long_out = cols[short_rows.shape[0] :].reshape(
        long_att.shape[0], long_att.shape[1], cols.shape[1]
    )
    return (short_out, long_out)


def solution(mesh):
    in_specs = (
        P("seq", None, "tp"),
        P(None, "seq", None, "tp"),
        P(None, "seq", None, "tp"),
        P("seq"),
        P(None, None, "tp"),
        P(None, None, "seq", "tp"),
        P(None, None, None, "tp"),
        P(),
        P(None, "seq"),
        P("tp", None),
    )
    out_specs = (P("seq", None, "tp"), P(None, None, "tp"))
    return jax.shard_map(
        per_device, mesh=mesh, in_specs=in_specs, out_specs=out_specs, check_vma=False
    )
```

```python
import functools
import math

import jax
import jax.numpy as jnp
from jax import lax
from jax.experimental import pallas as pl
from jax.experimental.pallas import tpu as pltpu
from jax.sharding import PartitionSpec as P

HEAD_DIM = 64
MESH = pl.DeviceIdType.MESH
LANES = 128


NEGATIVE = -1e30


def split_heads(tensor):
    return tensor.reshape(tensor.shape[0], tensor.shape[1], tensor.shape[2] // HEAD_DIM, HEAD_DIM)


def partial_softmax(query_heads, key_heads, value_heads, usable):
    scores = jnp.einsum(
        "rjhd,rphd->rhjp", query_heads, key_heads, preferred_element_type=jnp.float32
    ) * (1.0 / math.sqrt(HEAD_DIM))
    scores = jnp.where(usable, scores, NEGATIVE)
    highest = jnp.max(scores, axis=-1)
    expo = jnp.where(usable, jnp.exp(scores - highest[..., None]), 0.0)
    totals = jnp.sum(expo, axis=-1)
    summed = jnp.einsum(
        "rhjp,rphd->rhjd",
        expo.astype(jnp.bfloat16),
        value_heads,
        preferred_element_type=jnp.float32,
    )
    return (highest, totals, summed)


def combine_parts(first, second):
    highest = jnp.maximum(first[0], second[0])
    scale_first = jnp.exp(first[0] - highest)
    scale_second = jnp.exp(second[0] - highest)
    totals = first[1] * scale_first + second[1] * scale_second
    summed = first[2] * scale_first[..., None] + second[2] * scale_second[..., None]
    return (highest, totals, summed)


def finish(parts):
    normed = (parts[2] / parts[1][..., None]).astype(jnp.bfloat16)
    normed = jnp.transpose(normed, (0, 2, 1, 3))
    return normed.reshape(normed.shape[0], normed.shape[1], normed.shape[2] * normed.shape[3])


def fresh_part(queries, fresh):
    count = queries.shape[1]
    causal = (jnp.arange(count)[:, None] >= jnp.arange(count)[None, :])[None, None]
    return partial_softmax(
        split_heads(queries), split_heads(fresh[0]), split_heads(fresh[1]), causal
    )


def merge_states(low, high):
    lane = lax.broadcasted_iota(jnp.int32, low.shape, low.ndim - 1)
    top_low = low[..., HEAD_DIM : HEAD_DIM + 1]
    top_high = high[..., HEAD_DIM : HEAD_DIM + 1]
    top = jnp.maximum(top_low, top_high)
    mixed = low * jnp.exp(top_low - top) + high * jnp.exp(top_high - top)
    return jnp.where(lane == HEAD_DIM, top, mixed)


def butterfly_kernel(rounds, x_ref, o_ref, state, recv, send_sem, recv_sem):
    me = lax.axis_index("seq")
    column = lax.axis_index("tp")
    partners = []
    for k in range(rounds):
        step = 1 << k
        bit = (me // step) % 2
        partners.append((me + step - 2 * step * bit, bit))
    barrier = pltpu.get_barrier_semaphore()
    for partner, _ in partners:
        pl.semaphore_signal(
            barrier, inc=1, device_id=(partner, column), device_id_type=MESH
        )
    pl.semaphore_wait(barrier, rounds)
    for k in range(rounds):
        partner, bit = partners[k]
        source = x_ref if k == 0 else state.at[k - 1]
        copy = pltpu.make_async_remote_copy(
            src_ref=source,
            dst_ref=recv.at[k],
            send_sem=send_sem.at[k],
            recv_sem=recv_sem.at[k],
            device_id=(partner, column),
            device_id_type=MESH,
        )
        copy.start()
        copy.wait()
        mine = source[...]
        theirs = recv[k]
        first = bit == 0
        merged = merge_states(
            jnp.where(first, mine, theirs), jnp.where(first, theirs, mine)
        )
        if k == rounds - 1:
            o_ref[...] = merged
        else:
            state[k] = merged


def seq_allreduce(packed, devices):
    rounds = devices.bit_length() - 1
    rows = packed.size // LANES
    return pl.pallas_call(
        functools.partial(butterfly_kernel, rounds),
        out_shape=jax.ShapeDtypeStruct(packed.shape, jnp.float32),
        in_specs=[pl.BlockSpec(memory_space=pltpu.VMEM)],
        out_specs=pl.BlockSpec(memory_space=pltpu.VMEM),
        scratch_shapes=[
            pltpu.VMEM((max(rounds - 1, 1),) + packed.shape, jnp.float32),
            pltpu.VMEM((rounds,) + packed.shape, jnp.float32),
            pltpu.SemaphoreType.DMA((rounds,)),
            pltpu.SemaphoreType.DMA((rounds,)),
        ],
        compiler_params=pltpu.CompilerParams(collective_id=0, has_side_effects=True),
        cost_estimate=pl.CostEstimate(
            flops=8 * rows * LANES * rounds,
            transcendentals=2 * rows * rounds,
            bytes_accessed=2 * rows * LANES * 4 * rounds,
        ),
    )(packed)


def scatter_kernel(parts, x_ref, o_ref, recv, local_sem, send_sem, recv_sem):
    me = lax.axis_index("tp")
    row = lax.axis_index("seq")
    barrier = pltpu.get_barrier_semaphore()
    for d in range(1, parts):
        pl.semaphore_signal(
            barrier, inc=1, device_id=(row, (me + d) % parts), device_id_type=MESH
        )
    pl.semaphore_wait(barrier, parts - 1)
    own = pltpu.make_async_copy(x_ref.at[me], recv.at[me], local_sem)
    own.start()
    copies = []
    for d in range(1, parts):
        copy = pltpu.make_async_remote_copy(
            src_ref=x_ref.at[(me + d) % parts],
            dst_ref=recv.at[me],
            send_sem=send_sem.at[d - 1],
            recv_sem=recv_sem.at[d - 1],
            device_id=(row, (me + d) % parts),
            device_id_type=MESH,
        )
        copy.start()
        copies.append(copy)
    own.wait()
    for d in range(1, parts):
        copies[d - 1].wait_send()
        pltpu.make_async_remote_copy(
            src_ref=x_ref.at[0],
            dst_ref=recv.at[(me + parts - d) % parts],
            send_sem=send_sem.at[d - 1],
            recv_sem=recv_sem.at[d - 1],
            device_id=(row, (me + parts - d) % parts),
            device_id_type=MESH,
        ).wait_recv()
    total = recv[0]
    for s in range(1, parts):
        total = total + recv[s]
    o_ref[...] = total


def tp_reduce_scatter(term, parts):
    rows, width = term.shape
    cols = width // parts
    blocks = jnp.transpose(term.reshape(rows, parts, cols), (1, 0, 2))
    return pl.pallas_call(
        functools.partial(scatter_kernel, parts),
        out_shape=jax.ShapeDtypeStruct((rows, cols), jnp.float32),
        in_specs=[pl.BlockSpec(memory_space=pltpu.VMEM)],
        out_specs=pl.BlockSpec(memory_space=pltpu.VMEM),
        scratch_shapes=[
            pltpu.VMEM((parts, rows, cols), jnp.float32),
            pltpu.SemaphoreType.DMA(()),
            pltpu.SemaphoreType.DMA((parts - 1,)),
            pltpu.SemaphoreType.DMA((parts - 1,)),
        ],
        compiler_params=pltpu.CompilerParams(collective_id=1, has_side_effects=True),
        cost_estimate=pl.CostEstimate(
            flops=rows * width,
            transcendentals=0,
            bytes_accessed=3 * rows * width * 4,
        ),
    )(blocks)


def attention_kernel(with_fresh, len_ref, live_ref, off_ref, q_ref, k_ref, v_ref, *rest):
    tokens, width = q_ref.shape[1], q_ref.shape[2]
    positions = k_ref.shape[3]
    rows = (width // HEAD_DIM) * tokens
    request = pl.program_id(0)
    spot = lax.broadcasted_iota(jnp.int32, (1, positions), 1)
    usable = spot + off_ref[0] < len_ref[request]
    if not with_fresh:
        blocks = live_ref.shape[0]
        alive = spot < 0
        for b in range(blocks):
            alive = alive | (
                (spot // (positions // blocks) == b) & (live_ref[b, request] == 1)
            )
        usable = usable & alive
    pick = (
        lax.broadcasted_iota(jnp.int32, (rows, tokens), 0) % tokens
        == lax.broadcasted_iota(jnp.int32, (rows, tokens), 1)
    ).astype(jnp.bfloat16)
    head_lanes = (
        lax.broadcasted_iota(jnp.int32, (rows, width), 0) // tokens
        == lax.broadcasted_iota(jnp.int32, (rows, width), 1) // HEAD_DIM
    )
    spread = jnp.dot(pick, q_ref[0], preferred_element_type=jnp.float32)
    query = jnp.where(head_lanes, spread, 0.0).astype(jnp.bfloat16)
    contract = (((1,), (1,)), ((), ()))
    scale = 1.0 / math.sqrt(HEAD_DIM)
    scores = jnp.dot(query, k_ref[0, 0], preferred_element_type=jnp.float32) * scale
    scores = jnp.where(usable, scores, NEGATIVE)
    highest = jnp.max(scores, axis=1, keepdims=True)
    if with_fresh:
        fk_ref, fv_ref, o_ref = rest
        fresh_scores = lax.dot_general(
            query, fk_ref[0, 0], contract, preferred_element_type=jnp.float32
        ) * scale
        causal = lax.broadcasted_iota(jnp.int32, (rows, tokens), 1) <= (
            lax.broadcasted_iota(jnp.int32, (rows, tokens), 0) % tokens
        )
        fresh_scores = jnp.where(causal, fresh_scores, NEGATIVE)
        highest = jnp.maximum(highest, jnp.max(fresh_scores, axis=1, keepdims=True))
    expo = jnp.where(usable, jnp.exp(scores - highest), 0.0)
    totals = jnp.sum(expo, axis=1, keepdims=True)
    summed = lax.dot_general(
        expo.astype(jnp.bfloat16), v_ref[0, 0], contract, preferred_element_type=jnp.float32
    )
    if with_fresh:
        fresh_expo = jnp.where(causal, jnp.exp(fresh_scores - highest), 0.0)
        totals = totals + jnp.sum(fresh_expo, axis=1, keepdims=True)
        summed = summed + jnp.dot(
            fresh_expo.astype(jnp.bfloat16), fv_ref[0, 0], preferred_element_type=jnp.float32
        )
        normed = jnp.where(head_lanes, (summed / totals).astype(jnp.bfloat16), 0.0)
        gather = (
            lax.broadcasted_iota(jnp.int32, (tokens, rows), 1) % tokens
            == lax.broadcasted_iota(jnp.int32, (tokens, rows), 0)
        ).astype(jnp.bfloat16)
        o_ref[0] = jnp.dot(
            gather, normed.astype(jnp.bfloat16), preferred_element_type=jnp.float32
        ).astype(o_ref.dtype)
    else:
        (out_ref,) = rest
        masked = jnp.where(head_lanes, summed, 0.0)
        folded = masked[:, 0:HEAD_DIM]
        for g in range(1, width // HEAD_DIM):
            folded = folded + masked[:, g * HEAD_DIM : (g + 1) * HEAD_DIM]
        out_ref[0] = jnp.concatenate(
            [
                folded,
                highest,
                totals,
                jnp.zeros((rows, LANES - HEAD_DIM - 2), jnp.float32),
            ],
            axis=1,
        )


def attention(queries, cache, lengths, live, offset, fresh=None):
    count, tokens, width = queries.shape
    positions = cache.shape[2]
    rows = (width // HEAD_DIM) * tokens
    flipped = jnp.swapaxes(cache, 2, 3)
    specs = [
        pl.BlockSpec((1, tokens, width), lambda r, *_: (r, 0, 0)),
        pl.BlockSpec((1, 1, width, positions), lambda r, *_: (0, r, 0, 0)),
        pl.BlockSpec((1, 1, width, positions), lambda r, *_: (1, r, 0, 0)),
    ]
    operands = [lengths, live, offset, queries, flipped, flipped]
    if fresh is not None:
        specs += [
            pl.BlockSpec((1, 1, tokens, width), lambda r, *_: (0, r, 0, 0)),
            pl.BlockSpec((1, 1, tokens, width), lambda r, *_: (1, r, 0, 0)),
        ]
        operands += [fresh, fresh]
        out_shape = jax.ShapeDtypeStruct((count, tokens, width), jnp.bfloat16)
        out_specs = pl.BlockSpec((1, tokens, width), lambda r, *_: (r, 0, 0))
    else:
        out_shape = jax.ShapeDtypeStruct((count, rows, LANES), jnp.float32)
        out_specs = pl.BlockSpec((1, rows, LANES), lambda r, *_: (r, 0, 0))
    return pl.pallas_call(
        functools.partial(attention_kernel, fresh is not None),
        out_shape=out_shape,
        grid_spec=pltpu.PrefetchScalarGridSpec(
            num_scalar_prefetch=3, grid=(count,), in_specs=specs, out_specs=out_specs
        ),
        cost_estimate=pl.CostEstimate(
            flops=4 * count * rows * positions * width,
            transcendentals=count * rows * positions,
            bytes_accessed=2 * count * positions * width * 2,
        ),
    )(*operands)


def per_device(
    queries_short,
    cache_short,
    fresh_short,
    short_len,
    queries_long,
    cache_long,
    fresh_long,
    long_len,
    block_live,
    out_weight,
):
    request_count = queries_short.shape[0]
    token_count = queries_short.shape[1]
    short_att = attention(
        queries_short,
        cache_short,
        short_len,
        jnp.zeros((1, 1), jnp.int32),
        jnp.zeros((1,), jnp.int32),
        fresh_short,
    )
    local_len = cache_long.shape[2]
    packed = attention(
        queries_long,
        cache_long,
        long_len,
        block_live.T,
        (lax.axis_index("seq") * local_len).astype(jnp.int32).reshape(1),
    )
    heads = queries_long.shape[2] // HEAD_DIM
    shape = (queries_long.shape[0], heads, token_count)
    reduced = seq_allreduce(packed, lax.axis_size("seq"))
    merged = (
        reduced[..., HEAD_DIM].reshape(shape),
        reduced[..., HEAD_DIM + 1].reshape(shape),
        reduced[..., :HEAD_DIM].reshape(shape + (HEAD_DIM,)),
    )
    long_att = finish(combine_parts(merged, fresh_part(queries_long, fresh_long)))
    short_rows = short_att.reshape(-1, short_att.shape[2])
    both = jnp.concatenate([short_rows, long_att.reshape(-1, long_att.shape[2])], axis=0)
    term = jnp.dot(both, out_weight, preferred_element_type=jnp.float32)
    cols = tp_reduce_scatter(term, lax.axis_size("tp")).astype(jnp.bfloat16)
    short_out = cols[: short_rows.shape[0]].reshape(request_count, token_count, cols.shape[1])
    long_out = cols[short_rows.shape[0] :].reshape(
        long_att.shape[0], long_att.shape[1], cols.shape[1]
    )
    return (short_out, long_out)


def solution(mesh):
    in_specs = (
        P("seq", None, "tp"),
        P(None, "seq", None, "tp"),
        P(None, "seq", None, "tp"),
        P("seq"),
        P(None, None, "tp"),
        P(None, None, "seq", "tp"),
        P(None, None, None, "tp"),
        P(),
        P(None, "seq"),
        P("tp", None),
    )
    out_specs = (P("seq", None, "tp"), P(None, None, "tp"))
    return jax.shard_map(
        per_device, mesh=mesh, in_specs=in_specs, out_specs=out_specs, check_vma=False
    )
```

```python
import functools
import math

import jax
import jax.numpy as jnp
from jax import lax
from jax.experimental import pallas as pl
from jax.experimental.pallas import tpu as pltpu
from jax.sharding import PartitionSpec as P

HEAD_DIM = 64
MESH = pl.DeviceIdType.MESH
LANES = 128


NEGATIVE = -1e30


def split_heads(tensor):
    return tensor.reshape(tensor.shape[0], tensor.shape[1], tensor.shape[2] // HEAD_DIM, HEAD_DIM)


def partial_softmax(query_heads, key_heads, value_heads, usable):
    scores = jnp.einsum(
        "rjhd,rphd->rhjp", query_heads, key_heads, preferred_element_type=jnp.float32
    ) * (1.0 / math.sqrt(HEAD_DIM))
    scores = jnp.where(usable, scores, NEGATIVE)
    highest = jnp.max(scores, axis=-1)
    expo = jnp.where(usable, jnp.exp(scores - highest[..., None]), 0.0)
    totals = jnp.sum(expo, axis=-1)
    summed = jnp.einsum(
        "rhjp,rphd->rhjd",
        expo.astype(jnp.bfloat16),
        value_heads,
        preferred_element_type=jnp.float32,
    )
    return (highest, totals, summed)


def combine_parts(first, second):
    highest = jnp.maximum(first[0], second[0])
    scale_first = jnp.exp(first[0] - highest)
    scale_second = jnp.exp(second[0] - highest)
    totals = first[1] * scale_first + second[1] * scale_second
    summed = first[2] * scale_first[..., None] + second[2] * scale_second[..., None]
    return (highest, totals, summed)


def finish(parts):
    normed = (parts[2] / parts[1][..., None]).astype(jnp.bfloat16)
    normed = jnp.transpose(normed, (0, 2, 1, 3))
    return normed.reshape(normed.shape[0], normed.shape[1], normed.shape[2] * normed.shape[3])


def fresh_part(queries, fresh):
    count = queries.shape[1]
    causal = (jnp.arange(count)[:, None] >= jnp.arange(count)[None, :])[None, None]
    return partial_softmax(
        split_heads(queries), split_heads(fresh[0]), split_heads(fresh[1]), causal
    )


def merge_states(low, high):
    lane = lax.broadcasted_iota(jnp.int32, low.shape, low.ndim - 1)
    top_low = low[..., HEAD_DIM : HEAD_DIM + 1]
    top_high = high[..., HEAD_DIM : HEAD_DIM + 1]
    top = jnp.maximum(top_low, top_high)
    mixed = low * jnp.exp(top_low - top) + high * jnp.exp(top_high - top)
    return jnp.where(lane == HEAD_DIM, top, mixed)


def short_request(q, k_view, v_view, usable, fk, fv):
    tokens, width = q.shape
    rows = (width // HEAD_DIM) * tokens
    pick = (
        lax.broadcasted_iota(jnp.int32, (rows, tokens), 0) % tokens
        == lax.broadcasted_iota(jnp.int32, (rows, tokens), 1)
    ).astype(jnp.bfloat16)
    head_lanes = (
        lax.broadcasted_iota(jnp.int32, (rows, width), 0) // tokens
        == lax.broadcasted_iota(jnp.int32, (rows, width), 1) // HEAD_DIM
    )
    spread = jnp.dot(pick, q, preferred_element_type=jnp.float32)
    query = jnp.where(head_lanes, spread, 0.0).astype(jnp.bfloat16)
    contract = (((1,), (1,)), ((), ()))
    scale = 1.0 / math.sqrt(HEAD_DIM)
    scores = jnp.dot(query, k_view[...], preferred_element_type=jnp.float32) * scale
    scores = jnp.where(usable, scores, NEGATIVE)
    fresh_scores = lax.dot_general(query, fk, contract, preferred_element_type=jnp.float32) * scale
    causal = lax.broadcasted_iota(jnp.int32, (rows, tokens), 1) <= (
        lax.broadcasted_iota(jnp.int32, (rows, tokens), 0) % tokens
    )
    fresh_scores = jnp.where(causal, fresh_scores, NEGATIVE)
    highest = jnp.maximum(
        jnp.max(scores, axis=1, keepdims=True), jnp.max(fresh_scores, axis=1, keepdims=True)
    )
    expo = jnp.where(usable, jnp.exp(scores - highest), 0.0)
    fresh_expo = jnp.where(causal, jnp.exp(fresh_scores - highest), 0.0)
    totals = jnp.sum(expo, axis=1, keepdims=True) + jnp.sum(fresh_expo, axis=1, keepdims=True)
    summed = lax.dot_general(
        expo.astype(jnp.bfloat16), v_view[...], contract, preferred_element_type=jnp.float32
    ) + jnp.dot(fresh_expo.astype(jnp.bfloat16), fv, preferred_element_type=jnp.float32)
    normed = jnp.where(head_lanes, (summed / totals).astype(jnp.bfloat16), 0.0)
    gather = (
        lax.broadcasted_iota(jnp.int32, (tokens, rows), 1) % tokens
        == lax.broadcasted_iota(jnp.int32, (tokens, rows), 0)
    ).astype(jnp.bfloat16)
    return jnp.dot(gather, normed.astype(jnp.bfloat16), preferred_element_type=jnp.float32)


def butterfly_kernel(
    rounds, len_ref, x_ref, q_ref, f_ref, cache_ref, o_ref, att_ref,
    state, recv, send_sem, recv_sem, kv_buf, kv_sem,
):
    me = lax.axis_index("seq")
    column = lax.axis_index("tp")
    count = q_ref.shape[0]
    loads = []
    for r in range(count):
        pair = []
        for kv in range(2):
            load = pltpu.make_async_copy(
                cache_ref.at[kv, r], kv_buf.at[kv, r], kv_sem.at[kv, r]
            )
            load.start()
            pair.append(load)
        loads.append(pair)

    def short_step(r):
        for load in loads[r]:
            load.wait()
        spot = lax.broadcasted_iota(jnp.int32, (1, kv_buf.shape[3]), 1)
        att_ref[r] = short_request(
            q_ref[r], kv_buf.at[0, r], kv_buf.at[1, r], spot < len_ref[r],
            f_ref[0, r], f_ref[1, r],
        ).astype(att_ref.dtype)

    partners = []
    for k in range(rounds):
        step = 1 << k
        bit = (me // step) % 2
        partners.append((me + step - 2 * step * bit, bit))
    barrier = pltpu.get_barrier_semaphore()
    for partner, _ in partners:
        pl.semaphore_signal(
            barrier, inc=1, device_id=(partner, column), device_id_type=MESH
        )
    pl.semaphore_wait(barrier, rounds)
    for k in range(rounds):
        partner, bit = partners[k]
        source = x_ref if k == 0 else state.at[k - 1]
        copy = pltpu.make_async_remote_copy(
            src_ref=source,
            dst_ref=recv.at[k],
            send_sem=send_sem.at[k],
            recv_sem=recv_sem.at[k],
            device_id=(partner, column),
            device_id_type=MESH,
        )
        copy.start()
        if k < count:
            short_step(k)
        copy.wait()
        mine = source[...]
        theirs = recv[k]
        first = bit == 0
        merged = merge_states(
            jnp.where(first, mine, theirs), jnp.where(first, theirs, mine)
        )
        if k == rounds - 1:
            o_ref[...] = merged
        else:
            state[k] = merged
    for r in range(rounds, count):
        short_step(r)


def seq_allreduce(packed, devices, lengths, queries, fresh, cache):
    rounds = devices.bit_length() - 1
    rows = packed.size // LANES
    flipped = jnp.swapaxes(cache, 2, 3)
    vmem = pl.BlockSpec(memory_space=pltpu.VMEM)
    return pl.pallas_call(
        functools.partial(butterfly_kernel, rounds),
        out_shape=(
            jax.ShapeDtypeStruct(packed.shape, jnp.float32),
            jax.ShapeDtypeStruct(queries.shape, jnp.bfloat16),
        ),
        in_specs=[
            pl.BlockSpec(memory_space=pltpu.SMEM),
            vmem,
            vmem,
            vmem,
            pl.BlockSpec(memory_space=pl.ANY),
        ],
        out_specs=(vmem, vmem),
        scratch_shapes=[
            pltpu.VMEM((max(rounds - 1, 1),) + packed.shape, jnp.float32),
            pltpu.VMEM((rounds,) + packed.shape, jnp.float32),
            pltpu.SemaphoreType.DMA((rounds,)),
            pltpu.SemaphoreType.DMA((rounds,)),
            pltpu.VMEM(flipped.shape, flipped.dtype),
            pltpu.SemaphoreType.DMA(flipped.shape[:2]),
        ],
        compiler_params=pltpu.CompilerParams(
            collective_id=0, has_side_effects=True, vmem_limit_bytes=48 * 1024 * 1024
        ),
        cost_estimate=pl.CostEstimate(
            flops=8 * rows * LANES * rounds + 4 * 36 * queries.shape[0] * cache.size // 2,
            transcendentals=2 * rows * rounds,
            bytes_accessed=2 * rows * LANES * 4 * rounds + cache.size * 2,
        ),
    )(lengths, packed, queries, fresh, flipped)


def scatter_kernel(parts, x_ref, o_ref, recv, local_sem, send_sem, recv_sem):
    me = lax.axis_index("tp")
    row = lax.axis_index("seq")
    barrier = pltpu.get_barrier_semaphore()
    for d in range(1, parts):
        pl.semaphore_signal(
            barrier, inc=1, device_id=(row, (me + d) % parts), device_id_type=MESH
        )
    pl.semaphore_wait(barrier, parts - 1)
    own = pltpu.make_async_copy(x_ref.at[me], recv.at[me], local_sem)
    own.start()
    copies = []
    for d in range(1, parts):
        copy = pltpu.make_async_remote_copy(
            src_ref=x_ref.at[(me + d) % parts],
            dst_ref=recv.at[me],
            send_sem=send_sem.at[d - 1],
            recv_sem=recv_sem.at[d - 1],
            device_id=(row, (me + d) % parts),
            device_id_type=MESH,
        )
        copy.start()
        copies.append(copy)
    own.wait()
    for d in range(1, parts):
        copies[d - 1].wait_send()
        pltpu.make_async_remote_copy(
            src_ref=x_ref.at[0],
            dst_ref=recv.at[(me + parts - d) % parts],
            send_sem=send_sem.at[d - 1],
            recv_sem=recv_sem.at[d - 1],
            device_id=(row, (me + parts - d) % parts),
            device_id_type=MESH,
        ).wait_recv()
    total = recv[0]
    for s in range(1, parts):
        total = total + recv[s]
    o_ref[...] = total


def tp_reduce_scatter(term, parts):
    rows, width = term.shape
    cols = width // parts
    blocks = jnp.transpose(term.reshape(rows, parts, cols), (1, 0, 2))
    return pl.pallas_call(
        functools.partial(scatter_kernel, parts),
        out_shape=jax.ShapeDtypeStruct((rows, cols), jnp.float32),
        in_specs=[pl.BlockSpec(memory_space=pltpu.VMEM)],
        out_specs=pl.BlockSpec(memory_space=pltpu.VMEM),
        scratch_shapes=[
            pltpu.VMEM((parts, rows, cols), jnp.float32),
            pltpu.SemaphoreType.DMA(()),
            pltpu.SemaphoreType.DMA((parts - 1,)),
            pltpu.SemaphoreType.DMA((parts - 1,)),
        ],
        compiler_params=pltpu.CompilerParams(collective_id=1, has_side_effects=True),
        cost_estimate=pl.CostEstimate(
            flops=rows * width,
            transcendentals=0,
            bytes_accessed=3 * rows * width * 4,
        ),
    )(blocks)


def attention_kernel(with_fresh, len_ref, live_ref, off_ref, q_ref, k_ref, v_ref, *rest):
    tokens, width = q_ref.shape[1], q_ref.shape[2]
    positions = k_ref.shape[3]
    rows = (width // HEAD_DIM) * tokens
    request = pl.program_id(0)
    spot = lax.broadcasted_iota(jnp.int32, (1, positions), 1)
    usable = spot + off_ref[0] < len_ref[request]
    if not with_fresh:
        blocks = live_ref.shape[0]
        alive = spot < 0
        for b in range(blocks):
            alive = alive | (
                (spot // (positions // blocks) == b) & (live_ref[b, request] == 1)
            )
        usable = usable & alive
    pick = (
        lax.broadcasted_iota(jnp.int32, (rows, tokens), 0) % tokens
        == lax.broadcasted_iota(jnp.int32, (rows, tokens), 1)
    ).astype(jnp.bfloat16)
    head_lanes = (
        lax.broadcasted_iota(jnp.int32, (rows, width), 0) // tokens
        == lax.broadcasted_iota(jnp.int32, (rows, width), 1) // HEAD_DIM
    )
    spread = jnp.dot(pick, q_ref[0], preferred_element_type=jnp.float32)
    query = jnp.where(head_lanes, spread, 0.0).astype(jnp.bfloat16)
    contract = (((1,), (1,)), ((), ()))
    scale = 1.0 / math.sqrt(HEAD_DIM)
    scores = jnp.dot(query, k_ref[0, 0], preferred_element_type=jnp.float32) * scale
    scores = jnp.where(usable, scores, NEGATIVE)
    highest = jnp.max(scores, axis=1, keepdims=True)
    if with_fresh:
        fk_ref, fv_ref, o_ref = rest
        fresh_scores = lax.dot_general(
            query, fk_ref[0, 0], contract, preferred_element_type=jnp.float32
        ) * scale
        causal = lax.broadcasted_iota(jnp.int32, (rows, tokens), 1) <= (
            lax.broadcasted_iota(jnp.int32, (rows, tokens), 0) % tokens
        )
        fresh_scores = jnp.where(causal, fresh_scores, NEGATIVE)
        highest = jnp.maximum(highest, jnp.max(fresh_scores, axis=1, keepdims=True))
    expo = jnp.where(usable, jnp.exp(scores - highest), 0.0)
    totals = jnp.sum(expo, axis=1, keepdims=True)
    summed = lax.dot_general(
        expo.astype(jnp.bfloat16), v_ref[0, 0], contract, preferred_element_type=jnp.float32
    )
    if with_fresh:
        fresh_expo = jnp.where(causal, jnp.exp(fresh_scores - highest), 0.0)
        totals = totals + jnp.sum(fresh_expo, axis=1, keepdims=True)
        summed = summed + jnp.dot(
            fresh_expo.astype(jnp.bfloat16), fv_ref[0, 0], preferred_element_type=jnp.float32
        )
        normed = jnp.where(head_lanes, (summed / totals).astype(jnp.bfloat16), 0.0)
        gather = (
            lax.broadcasted_iota(jnp.int32, (tokens, rows), 1) % tokens
            == lax.broadcasted_iota(jnp.int32, (tokens, rows), 0)
        ).astype(jnp.bfloat16)
        o_ref[0] = jnp.dot(
            gather, normed.astype(jnp.bfloat16), preferred_element_type=jnp.float32
        ).astype(o_ref.dtype)
    else:
        (out_ref,) = rest
        masked = jnp.where(head_lanes, summed, 0.0)
        folded = masked[:, 0:HEAD_DIM]
        for g in range(1, width // HEAD_DIM):
            folded = folded + masked[:, g * HEAD_DIM : (g + 1) * HEAD_DIM]
        out_ref[0] = jnp.concatenate(
            [
                folded,
                highest,
                totals,
                jnp.zeros((rows, LANES - HEAD_DIM - 2), jnp.float32),
            ],
            axis=1,
        )


def attention(queries, cache, lengths, live, offset, fresh=None):
    count, tokens, width = queries.shape
    positions = cache.shape[2]
    rows = (width // HEAD_DIM) * tokens
    flipped = jnp.swapaxes(cache, 2, 3)
    specs = [
        pl.BlockSpec((1, tokens, width), lambda r, *_: (r, 0, 0)),
        pl.BlockSpec((1, 1, width, positions), lambda r, *_: (0, r, 0, 0)),
        pl.BlockSpec((1, 1, width, positions), lambda r, *_: (1, r, 0, 0)),
    ]
    operands = [lengths, live, offset, queries, flipped, flipped]
    if fresh is not None:
        specs += [
            pl.BlockSpec((1, 1, tokens, width), lambda r, *_: (0, r, 0, 0)),
            pl.BlockSpec((1, 1, tokens, width), lambda r, *_: (1, r, 0, 0)),
        ]
        operands += [fresh, fresh]
        out_shape = jax.ShapeDtypeStruct((count, tokens, width), jnp.bfloat16)
        out_specs = pl.BlockSpec((1, tokens, width), lambda r, *_: (r, 0, 0))
    else:
        out_shape = jax.ShapeDtypeStruct((count, rows, LANES), jnp.float32)
        out_specs = pl.BlockSpec((1, rows, LANES), lambda r, *_: (r, 0, 0))
    return pl.pallas_call(
        functools.partial(attention_kernel, fresh is not None),
        out_shape=out_shape,
        grid_spec=pltpu.PrefetchScalarGridSpec(
            num_scalar_prefetch=3, grid=(count,), in_specs=specs, out_specs=out_specs
        ),
        cost_estimate=pl.CostEstimate(
            flops=4 * count * rows * positions * width,
            transcendentals=count * rows * positions,
            bytes_accessed=2 * count * positions * width * 2,
        ),
    )(*operands)


def per_device(
    queries_short,
    cache_short,
    fresh_short,
    short_len,
    queries_long,
    cache_long,
    fresh_long,
    long_len,
    block_live,
    out_weight,
):
    request_count = queries_short.shape[0]
    token_count = queries_short.shape[1]
    local_len = cache_long.shape[2]
    packed = attention(
        queries_long,
        cache_long,
        long_len,
        block_live.T,
        (lax.axis_index("seq") * local_len).astype(jnp.int32).reshape(1),
    )
    heads = queries_long.shape[2] // HEAD_DIM
    shape = (queries_long.shape[0], heads, token_count)
    reduced, short_att = seq_allreduce(
        packed, lax.axis_size("seq"), short_len, queries_short, fresh_short, cache_short
    )
    merged = (
        reduced[..., HEAD_DIM].reshape(shape),
        reduced[..., HEAD_DIM + 1].reshape(shape),
        reduced[..., :HEAD_DIM].reshape(shape + (HEAD_DIM,)),
    )
    long_att = finish(combine_parts(merged, fresh_part(queries_long, fresh_long)))
    short_rows = short_att.reshape(-1, short_att.shape[2])
    both = jnp.concatenate([short_rows, long_att.reshape(-1, long_att.shape[2])], axis=0)
    term = jnp.dot(both, out_weight, preferred_element_type=jnp.float32)
    cols = tp_reduce_scatter(term, lax.axis_size("tp")).astype(jnp.bfloat16)
    short_out = cols[: short_rows.shape[0]].reshape(request_count, token_count, cols.shape[1])
    long_out = cols[short_rows.shape[0] :].reshape(
        long_att.shape[0], long_att.shape[1], cols.shape[1]
    )
    return (short_out, long_out)


def solution(mesh):
    in_specs = (
        P("seq", None, "tp"),
        P(None, "seq", None, "tp"),
        P(None, "seq", None, "tp"),
        P("seq"),
        P(None, None, "tp"),
        P(None, None, "seq", "tp"),
        P(None, None, None, "tp"),
        P(),
        P(None, "seq"),
        P("tp", None),
    )
    out_specs = (P("seq", None, "tp"), P(None, None, "tp"))
    return jax.shard_map(
        per_device, mesh=mesh, in_specs=in_specs, out_specs=out_specs, check_vma=False
    )
```

```python
import functools
import math

import jax
import jax.numpy as jnp
from jax import lax
from jax.experimental import pallas as pl
from jax.experimental.pallas import tpu as pltpu
from jax.sharding import PartitionSpec as P

HEAD_DIM = 64
MESH = pl.DeviceIdType.MESH
LANES = 128


NEGATIVE = -1e30


def split_heads(tensor):
    return tensor.reshape(tensor.shape[0], tensor.shape[1], tensor.shape[2] // HEAD_DIM, HEAD_DIM)


def partial_softmax(query_heads, key_heads, value_heads, usable):
    scores = jnp.einsum(
        "rjhd,rphd->rhjp", query_heads, key_heads, preferred_element_type=jnp.float32
    ) * (1.0 / math.sqrt(HEAD_DIM))
    scores = jnp.where(usable, scores, NEGATIVE)
    highest = jnp.max(scores, axis=-1)
    expo = jnp.where(usable, jnp.exp(scores - highest[..., None]), 0.0)
    totals = jnp.sum(expo, axis=-1)
    summed = jnp.einsum(
        "rhjp,rphd->rhjd",
        expo.astype(jnp.bfloat16),
        value_heads,
        preferred_element_type=jnp.float32,
    )
    return (highest, totals, summed)


def combine_parts(first, second):
    highest = jnp.maximum(first[0], second[0])
    scale_first = jnp.exp(first[0] - highest)
    scale_second = jnp.exp(second[0] - highest)
    totals = first[1] * scale_first + second[1] * scale_second
    summed = first[2] * scale_first[..., None] + second[2] * scale_second[..., None]
    return (highest, totals, summed)


def finish(parts):
    normed = (parts[2] / parts[1][..., None]).astype(jnp.bfloat16)
    normed = jnp.transpose(normed, (0, 2, 1, 3))
    return normed.reshape(normed.shape[0], normed.shape[1], normed.shape[2] * normed.shape[3])


def fresh_part(queries, fresh):
    count = queries.shape[1]
    causal = (jnp.arange(count)[:, None] >= jnp.arange(count)[None, :])[None, None]
    return partial_softmax(
        split_heads(queries), split_heads(fresh[0]), split_heads(fresh[1]), causal
    )


def merge_states(low, high):
    lane = lax.broadcasted_iota(jnp.int32, low.shape, low.ndim - 1)
    top_low = low[..., HEAD_DIM : HEAD_DIM + 1]
    top_high = high[..., HEAD_DIM : HEAD_DIM + 1]
    top = jnp.maximum(top_low, top_high)
    mixed = low * jnp.exp(top_low - top) + high * jnp.exp(top_high - top)
    return jnp.where(lane == HEAD_DIM, top, mixed)


def short_request(q, k_view, v_view, usable, fk, fv):
    tokens, width = q.shape
    rows = (width // HEAD_DIM) * tokens
    pick = (
        lax.broadcasted_iota(jnp.int32, (rows, tokens), 0) % tokens
        == lax.broadcasted_iota(jnp.int32, (rows, tokens), 1)
    ).astype(jnp.bfloat16)
    head_lanes = (
        lax.broadcasted_iota(jnp.int32, (rows, width), 0) // tokens
        == lax.broadcasted_iota(jnp.int32, (rows, width), 1) // HEAD_DIM
    )
    spread = jnp.dot(pick, q, preferred_element_type=jnp.float32)
    query = jnp.where(head_lanes, spread, 0.0).astype(jnp.bfloat16)
    contract = (((1,), (1,)), ((), ()))
    scale = 1.0 / math.sqrt(HEAD_DIM)
    scores = jnp.dot(query, k_view[...], preferred_element_type=jnp.float32) * scale
    scores = jnp.where(usable, scores, NEGATIVE)
    fresh_scores = lax.dot_general(query, fk, contract, preferred_element_type=jnp.float32) * scale
    causal = lax.broadcasted_iota(jnp.int32, (rows, tokens), 1) <= (
        lax.broadcasted_iota(jnp.int32, (rows, tokens), 0) % tokens
    )
    fresh_scores = jnp.where(causal, fresh_scores, NEGATIVE)
    highest = jnp.maximum(
        jnp.max(scores, axis=1, keepdims=True), jnp.max(fresh_scores, axis=1, keepdims=True)
    )
    expo = jnp.where(usable, jnp.exp(scores - highest), 0.0)
    fresh_expo = jnp.where(causal, jnp.exp(fresh_scores - highest), 0.0)
    totals = jnp.sum(expo, axis=1, keepdims=True) + jnp.sum(fresh_expo, axis=1, keepdims=True)
    summed = lax.dot_general(
        expo.astype(jnp.bfloat16), v_view[...], contract, preferred_element_type=jnp.float32
    ) + jnp.dot(fresh_expo.astype(jnp.bfloat16), fv, preferred_element_type=jnp.float32)
    normed = jnp.where(head_lanes, (summed / totals).astype(jnp.bfloat16), 0.0)
    gather = (
        lax.broadcasted_iota(jnp.int32, (tokens, rows), 1) % tokens
        == lax.broadcasted_iota(jnp.int32, (tokens, rows), 0)
    ).astype(jnp.bfloat16)
    return jnp.dot(gather, normed.astype(jnp.bfloat16), preferred_element_type=jnp.float32)


def butterfly_kernel(
    rounds, len_ref, x_ref, q_ref, f_ref, cache_ref, o_ref, att_ref,
    state, recv, send_sem, recv_sem, kv_buf, kv_sem,
):
    me = lax.axis_index("seq")
    column = lax.axis_index("tp")
    count = q_ref.shape[0]
    loads = []
    for r in range(count):
        pair = []
        for kv in range(2):
            load = pltpu.make_async_copy(
                cache_ref.at[kv, r], kv_buf.at[kv, r], kv_sem.at[kv, r]
            )
            load.start()
            pair.append(load)
        loads.append(pair)

    def short_step(r):
        for load in loads[r]:
            load.wait()
        spot = lax.broadcasted_iota(jnp.int32, (1, kv_buf.shape[3]), 1)
        att_ref[r] = short_request(
            q_ref[r], kv_buf.at[0, r], kv_buf.at[1, r], spot < len_ref[r],
            f_ref[0, r], f_ref[1, r],
        ).astype(att_ref.dtype)

    partners = []
    for k in range(rounds):
        step = 1 << k
        bit = (me // step) % 2
        partners.append((me + step - 2 * step * bit, bit))
    barrier = pltpu.get_barrier_semaphore()
    for partner, _ in partners:
        pl.semaphore_signal(
            barrier, inc=1, device_id=(partner, column), device_id_type=MESH
        )
    pl.semaphore_wait(barrier, rounds)
    for k in range(rounds):
        partner, bit = partners[k]
        source = x_ref if k == 0 else state.at[k - 1]
        copy = pltpu.make_async_remote_copy(
            src_ref=source,
            dst_ref=recv.at[k],
            send_sem=send_sem.at[k],
            recv_sem=recv_sem.at[k],
            device_id=(partner, column),
            device_id_type=MESH,
        )
        copy.start()
        if k < count:
            short_step(k)
        copy.wait()
        mine = source[...]
        theirs = recv[k]
        first = bit == 0
        merged = merge_states(
            jnp.where(first, mine, theirs), jnp.where(first, theirs, mine)
        )
        if k == rounds - 1:
            o_ref[...] = merged
        else:
            state[k] = merged
    for r in range(rounds, count):
        short_step(r)


def seq_allreduce(packed, devices, lengths, queries, fresh, cache):
    rounds = devices.bit_length() - 1
    rows = packed.size // LANES
    flipped = jnp.swapaxes(cache, 2, 3)
    vmem = pl.BlockSpec(memory_space=pltpu.VMEM)
    return pl.pallas_call(
        functools.partial(butterfly_kernel, rounds),
        out_shape=(
            jax.ShapeDtypeStruct(packed.shape, jnp.float32),
            jax.ShapeDtypeStruct(queries.shape, jnp.bfloat16),
        ),
        in_specs=[
            pl.BlockSpec(memory_space=pltpu.SMEM),
            vmem,
            vmem,
            vmem,
            pl.BlockSpec(memory_space=pl.ANY),
        ],
        out_specs=(vmem, vmem),
        scratch_shapes=[
            pltpu.VMEM((max(rounds - 1, 1),) + packed.shape, jnp.float32),
            pltpu.VMEM((rounds,) + packed.shape, jnp.float32),
            pltpu.SemaphoreType.DMA((rounds,)),
            pltpu.SemaphoreType.DMA((rounds,)),
            pltpu.VMEM(flipped.shape, flipped.dtype),
            pltpu.SemaphoreType.DMA(flipped.shape[:2]),
        ],
        compiler_params=pltpu.CompilerParams(collective_id=0, has_side_effects=True),
        cost_estimate=pl.CostEstimate(
            flops=8 * rows * LANES * rounds + 4 * 36 * queries.shape[0] * cache.size // 2,
            transcendentals=2 * rows * rounds,
            bytes_accessed=2 * rows * LANES * 4 * rounds + cache.size * 2,
        ),
    )(lengths, packed, queries, fresh, flipped)


def scatter_kernel(parts, x_ref, o_ref, recv, local_sem, send_sem, recv_sem):
    me = lax.axis_index("tp")
    row = lax.axis_index("seq")
    barrier = pltpu.get_barrier_semaphore()
    for d in range(1, parts):
        pl.semaphore_signal(
            barrier, inc=1, device_id=(row, (me + d) % parts), device_id_type=MESH
        )
    pl.semaphore_wait(barrier, parts - 1)
    own = pltpu.make_async_copy(x_ref.at[me], recv.at[me], local_sem)
    own.start()
    copies = []
    for d in range(1, parts):
        copy = pltpu.make_async_remote_copy(
            src_ref=x_ref.at[(me + d) % parts],
            dst_ref=recv.at[me],
            send_sem=send_sem.at[d - 1],
            recv_sem=recv_sem.at[d - 1],
            device_id=(row, (me + d) % parts),
            device_id_type=MESH,
        )
        copy.start()
        copies.append(copy)
    own.wait()
    for d in range(1, parts):
        copies[d - 1].wait_send()
        pltpu.make_async_remote_copy(
            src_ref=x_ref.at[0],
            dst_ref=recv.at[(me + parts - d) % parts],
            send_sem=send_sem.at[d - 1],
            recv_sem=recv_sem.at[d - 1],
            device_id=(row, (me + parts - d) % parts),
            device_id_type=MESH,
        ).wait_recv()
    total = recv[0]
    for s in range(1, parts):
        total = total + recv[s]
    o_ref[...] = total


def tp_reduce_scatter(term, parts):
    rows, width = term.shape
    cols = width // parts
    blocks = jnp.transpose(term.reshape(rows, parts, cols), (1, 0, 2))
    return pl.pallas_call(
        functools.partial(scatter_kernel, parts),
        out_shape=jax.ShapeDtypeStruct((rows, cols), jnp.float32),
        in_specs=[pl.BlockSpec(memory_space=pltpu.VMEM)],
        out_specs=pl.BlockSpec(memory_space=pltpu.VMEM),
        scratch_shapes=[
            pltpu.VMEM((parts, rows, cols), jnp.float32),
            pltpu.SemaphoreType.DMA(()),
            pltpu.SemaphoreType.DMA((parts - 1,)),
            pltpu.SemaphoreType.DMA((parts - 1,)),
        ],
        compiler_params=pltpu.CompilerParams(collective_id=1, has_side_effects=True),
        cost_estimate=pl.CostEstimate(
            flops=rows * width,
            transcendentals=0,
            bytes_accessed=3 * rows * width * 4,
        ),
    )(blocks)


def attention_kernel(with_fresh, len_ref, live_ref, off_ref, q_ref, k_ref, v_ref, *rest):
    tokens, width = q_ref.shape[1], q_ref.shape[2]
    positions = k_ref.shape[3]
    rows = (width // HEAD_DIM) * tokens
    request = pl.program_id(0)
    spot = lax.broadcasted_iota(jnp.int32, (1, positions), 1)
    usable = spot + off_ref[0] < len_ref[request]
    if not with_fresh:
        blocks = live_ref.shape[0]
        alive = spot < 0
        for b in range(blocks):
            alive = alive | (
                (spot // (positions // blocks) == b) & (live_ref[b, request] == 1)
            )
        usable = usable & alive
    pick = (
        lax.broadcasted_iota(jnp.int32, (rows, tokens), 0) % tokens
        == lax.broadcasted_iota(jnp.int32, (rows, tokens), 1)
    ).astype(jnp.bfloat16)
    head_lanes = (
        lax.broadcasted_iota(jnp.int32, (rows, width), 0) // tokens
        == lax.broadcasted_iota(jnp.int32, (rows, width), 1) // HEAD_DIM
    )
    spread = jnp.dot(pick, q_ref[0], preferred_element_type=jnp.float32)
    query = jnp.where(head_lanes, spread, 0.0).astype(jnp.bfloat16)
    contract = (((1,), (1,)), ((), ()))
    scale = 1.0 / math.sqrt(HEAD_DIM)
    scores = jnp.dot(query, k_ref[0, 0], preferred_element_type=jnp.float32) * scale
    scores = jnp.where(usable, scores, NEGATIVE)
    highest = jnp.max(scores, axis=1, keepdims=True)
    if with_fresh:
        fk_ref, fv_ref, o_ref = rest
        fresh_scores = lax.dot_general(
            query, fk_ref[0, 0], contract, preferred_element_type=jnp.float32
        ) * scale
        causal = lax.broadcasted_iota(jnp.int32, (rows, tokens), 1) <= (
            lax.broadcasted_iota(jnp.int32, (rows, tokens), 0) % tokens
        )
        fresh_scores = jnp.where(causal, fresh_scores, NEGATIVE)
        highest = jnp.maximum(highest, jnp.max(fresh_scores, axis=1, keepdims=True))
    expo = jnp.where(usable, jnp.exp(scores - highest), 0.0)
    totals = jnp.sum(expo, axis=1, keepdims=True)
    summed = lax.dot_general(
        expo.astype(jnp.bfloat16), v_ref[0, 0], contract, preferred_element_type=jnp.float32
    )
    if with_fresh:
        fresh_expo = jnp.where(causal, jnp.exp(fresh_scores - highest), 0.0)
        totals = totals + jnp.sum(fresh_expo, axis=1, keepdims=True)
        summed = summed + jnp.dot(
            fresh_expo.astype(jnp.bfloat16), fv_ref[0, 0], preferred_element_type=jnp.float32
        )
        normed = jnp.where(head_lanes, (summed / totals).astype(jnp.bfloat16), 0.0)
        gather = (
            lax.broadcasted_iota(jnp.int32, (tokens, rows), 1) % tokens
            == lax.broadcasted_iota(jnp.int32, (tokens, rows), 0)
        ).astype(jnp.bfloat16)
        o_ref[0] = jnp.dot(
            gather, normed.astype(jnp.bfloat16), preferred_element_type=jnp.float32
        ).astype(o_ref.dtype)
    else:
        (out_ref,) = rest
        masked = jnp.where(head_lanes, summed, 0.0)
        folded = masked[:, 0:HEAD_DIM]
        for g in range(1, width // HEAD_DIM):
            folded = folded + masked[:, g * HEAD_DIM : (g + 1) * HEAD_DIM]
        out_ref[0] = jnp.concatenate(
            [
                folded,
                highest,
                totals,
                jnp.zeros((rows, LANES - HEAD_DIM - 2), jnp.float32),
            ],
            axis=1,
        )


def attention(queries, cache, lengths, live, offset, fresh=None):
    count, tokens, width = queries.shape
    positions = cache.shape[2]
    rows = (width // HEAD_DIM) * tokens
    flipped = jnp.swapaxes(cache, 2, 3)
    specs = [
        pl.BlockSpec((1, tokens, width), lambda r, *_: (r, 0, 0)),
        pl.BlockSpec((1, 1, width, positions), lambda r, *_: (0, r, 0, 0)),
        pl.BlockSpec((1, 1, width, positions), lambda r, *_: (1, r, 0, 0)),
    ]
    operands = [lengths, live, offset, queries, flipped, flipped]
    if fresh is not None:
        specs += [
            pl.BlockSpec((1, 1, tokens, width), lambda r, *_: (0, r, 0, 0)),
            pl.BlockSpec((1, 1, tokens, width), lambda r, *_: (1, r, 0, 0)),
        ]
        operands += [fresh, fresh]
        out_shape = jax.ShapeDtypeStruct((count, tokens, width), jnp.bfloat16)
        out_specs = pl.BlockSpec((1, tokens, width), lambda r, *_: (r, 0, 0))
    else:
        out_shape = jax.ShapeDtypeStruct((count, rows, LANES), jnp.float32)
        out_specs = pl.BlockSpec((1, rows, LANES), lambda r, *_: (r, 0, 0))
    return pl.pallas_call(
        functools.partial(attention_kernel, fresh is not None),
        out_shape=out_shape,
        grid_spec=pltpu.PrefetchScalarGridSpec(
            num_scalar_prefetch=3, grid=(count,), in_specs=specs, out_specs=out_specs
        ),
        cost_estimate=pl.CostEstimate(
            flops=4 * count * rows * positions * width,
            transcendentals=count * rows * positions,
            bytes_accessed=2 * count * positions * width * 2,
        ),
    )(*operands)


def per_device(
    queries_short,
    cache_short,
    fresh_short,
    short_len,
    queries_long,
    cache_long,
    fresh_long,
    long_len,
    block_live,
    out_weight,
):
    request_count = queries_short.shape[0]
    token_count = queries_short.shape[1]
    local_len = cache_long.shape[2]
    packed = attention(
        queries_long,
        cache_long,
        long_len,
        block_live.T,
        (lax.axis_index("seq") * local_len).astype(jnp.int32).reshape(1),
    )
    heads = queries_long.shape[2] // HEAD_DIM
    shape = (queries_long.shape[0], heads, token_count)
    reduced, short_att = seq_allreduce(
        packed, lax.axis_size("seq"), short_len, queries_short, fresh_short, cache_short
    )
    merged = (
        reduced[..., HEAD_DIM].reshape(shape),
        reduced[..., HEAD_DIM + 1].reshape(shape),
        reduced[..., :HEAD_DIM].reshape(shape + (HEAD_DIM,)),
    )
    long_att = finish(combine_parts(merged, fresh_part(queries_long, fresh_long)))
    short_rows = short_att.reshape(-1, short_att.shape[2])
    both = jnp.concatenate([short_rows, long_att.reshape(-1, long_att.shape[2])], axis=0)
    term = jnp.dot(both, out_weight, preferred_element_type=jnp.float32)
    cols = tp_reduce_scatter(term, lax.axis_size("tp")).astype(jnp.bfloat16)
    short_out = cols[: short_rows.shape[0]].reshape(request_count, token_count, cols.shape[1])
    long_out = cols[short_rows.shape[0] :].reshape(
        long_att.shape[0], long_att.shape[1], cols.shape[1]
    )
    return (short_out, long_out)


def solution(mesh):
    in_specs = (
        P("seq", None, "tp"),
        P(None, "seq", None, "tp"),
        P(None, "seq", None, "tp"),
        P("seq"),
        P(None, None, "tp"),
        P(None, None, "seq", "tp"),
        P(None, None, None, "tp"),
        P(),
        P(None, "seq"),
        P("tp", None),
    )
    out_specs = (P("seq", None, "tp"), P(None, None, "tp"))
    return jax.shard_map(
        per_device, mesh=mesh, in_specs=in_specs, out_specs=out_specs, check_vma=False
    )
```

```python
import functools
import math

import jax
import jax.numpy as jnp
from jax import lax
from jax.experimental import pallas as pl
from jax.experimental.pallas import tpu as pltpu
from jax.sharding import PartitionSpec as P

HEAD_DIM = 64
MESH = pl.DeviceIdType.MESH
LANES = 128


NEGATIVE = -1e30


def split_heads(tensor):
    return tensor.reshape(tensor.shape[0], tensor.shape[1], tensor.shape[2] // HEAD_DIM, HEAD_DIM)


def partial_softmax(query_heads, key_heads, value_heads, usable):
    scores = jnp.einsum(
        "rjhd,rphd->rhjp", query_heads, key_heads, preferred_element_type=jnp.float32
    ) * (1.0 / math.sqrt(HEAD_DIM))
    scores = jnp.where(usable, scores, NEGATIVE)
    highest = jnp.max(scores, axis=-1)
    expo = jnp.where(usable, jnp.exp(scores - highest[..., None]), 0.0)
    totals = jnp.sum(expo, axis=-1)
    summed = jnp.einsum(
        "rhjp,rphd->rhjd",
        expo.astype(jnp.bfloat16),
        value_heads,
        preferred_element_type=jnp.float32,
    )
    return (highest, totals, summed)


def combine_parts(first, second):
    highest = jnp.maximum(first[0], second[0])
    scale_first = jnp.exp(first[0] - highest)
    scale_second = jnp.exp(second[0] - highest)
    totals = first[1] * scale_first + second[1] * scale_second
    summed = first[2] * scale_first[..., None] + second[2] * scale_second[..., None]
    return (highest, totals, summed)


def finish(parts):
    normed = (parts[2] / parts[1][..., None]).astype(jnp.bfloat16)
    normed = jnp.transpose(normed, (0, 2, 1, 3))
    return normed.reshape(normed.shape[0], normed.shape[1], normed.shape[2] * normed.shape[3])


def fresh_part(queries, fresh):
    count = queries.shape[1]
    causal = (jnp.arange(count)[:, None] >= jnp.arange(count)[None, :])[None, None]
    return partial_softmax(
        split_heads(queries), split_heads(fresh[0]), split_heads(fresh[1]), causal
    )


def merge_states(low, high):
    lane = lax.broadcasted_iota(jnp.int32, low.shape, low.ndim - 1)
    top_low = low[..., HEAD_DIM : HEAD_DIM + 1]
    top_high = high[..., HEAD_DIM : HEAD_DIM + 1]
    top = jnp.maximum(top_low, top_high)
    mixed = low * jnp.exp(top_low - top) + high * jnp.exp(top_high - top)
    return jnp.where(lane == HEAD_DIM, top, mixed)


def short_request(q, k_view, v_view, usable, fk, fv):
    tokens, width = q.shape
    rows = (width // HEAD_DIM) * tokens
    pick = (
        lax.broadcasted_iota(jnp.int32, (rows, tokens), 0) % tokens
        == lax.broadcasted_iota(jnp.int32, (rows, tokens), 1)
    ).astype(jnp.bfloat16)
    head_lanes = (
        lax.broadcasted_iota(jnp.int32, (rows, width), 0) // tokens
        == lax.broadcasted_iota(jnp.int32, (rows, width), 1) // HEAD_DIM
    )
    spread = jnp.dot(pick, q, preferred_element_type=jnp.float32)
    query = jnp.where(head_lanes, spread, 0.0).astype(jnp.bfloat16)
    contract = (((1,), (1,)), ((), ()))
    scale = 1.0 / math.sqrt(HEAD_DIM)
    scores = jnp.dot(query, k_view[...], preferred_element_type=jnp.float32) * scale
    scores = jnp.where(usable, scores, NEGATIVE)
    fresh_scores = lax.dot_general(query, fk, contract, preferred_element_type=jnp.float32) * scale
    causal = lax.broadcasted_iota(jnp.int32, (rows, tokens), 1) <= (
        lax.broadcasted_iota(jnp.int32, (rows, tokens), 0) % tokens
    )
    fresh_scores = jnp.where(causal, fresh_scores, NEGATIVE)
    highest = jnp.maximum(
        jnp.max(scores, axis=1, keepdims=True), jnp.max(fresh_scores, axis=1, keepdims=True)
    )
    expo = jnp.where(usable, jnp.exp(scores - highest), 0.0)
    fresh_expo = jnp.where(causal, jnp.exp(fresh_scores - highest), 0.0)
    totals = jnp.sum(expo, axis=1, keepdims=True) + jnp.sum(fresh_expo, axis=1, keepdims=True)
    summed = lax.dot_general(
        expo.astype(jnp.bfloat16), v_view[...], contract, preferred_element_type=jnp.float32
    ) + jnp.dot(fresh_expo.astype(jnp.bfloat16), fv, preferred_element_type=jnp.float32)
    normed = jnp.where(head_lanes, (summed / totals).astype(jnp.bfloat16), 0.0)
    gather = (
        lax.broadcasted_iota(jnp.int32, (tokens, rows), 1) % tokens
        == lax.broadcasted_iota(jnp.int32, (tokens, rows), 0)
    ).astype(jnp.bfloat16)
    return jnp.dot(gather, normed.astype(jnp.bfloat16), preferred_element_type=jnp.float32)


def butterfly_kernel(
    rounds, len_ref, x_ref, q_ref, f_ref, cache_ref, o_ref, att_ref,
    state, recv, send_sem, recv_sem, kv_buf, kv_sem,
):
    me = lax.axis_index("seq")
    column = lax.axis_index("tp")
    count = q_ref.shape[0]
    loads = []
    for r in range(count):
        pair = []
        for kv in range(2):
            load = pltpu.make_async_copy(
                cache_ref.at[kv, r], kv_buf.at[kv, r], kv_sem.at[kv, r]
            )
            load.start()
            pair.append(load)
        loads.append(pair)

    def short_step(r):
        for load in loads[r]:
            load.wait()
        spot = lax.broadcasted_iota(jnp.int32, (1, kv_buf.shape[3]), 1)
        att_ref[r] = short_request(
            q_ref[r], kv_buf.at[0, r], kv_buf.at[1, r], spot < len_ref[r],
            f_ref[0, r], f_ref[1, r],
        ).astype(att_ref.dtype)

    partners = []
    for k in range(rounds):
        step = 1 << k
        bit = (me // step) % 2
        partners.append((me + step - 2 * step * bit, bit))
    barrier = pltpu.get_barrier_semaphore()
    for partner, _ in partners:
        pl.semaphore_signal(
            barrier, inc=1, device_id=(partner, column), device_id_type=MESH
        )
    pl.semaphore_wait(barrier, rounds)
    for k in range(rounds):
        partner, bit = partners[k]
        source = x_ref if k == 0 else state.at[k - 1]
        copy = pltpu.make_async_remote_copy(
            src_ref=source,
            dst_ref=recv.at[k],
            send_sem=send_sem.at[k],
            recv_sem=recv_sem.at[k],
            device_id=(partner, column),
            device_id_type=MESH,
        )
        copy.start()
        if k < count:
            short_step(k)
        copy.wait()
        mine = source[...]
        theirs = recv[k]
        first = bit == 0
        merged = merge_states(
            jnp.where(first, mine, theirs), jnp.where(first, theirs, mine)
        )
        if k == rounds - 1:
            o_ref[...] = merged
        else:
            state[k] = merged
    for r in range(rounds, count):
        short_step(r)


def seq_allreduce(packed, devices, lengths, queries, fresh, cache):
    rounds = devices.bit_length() - 1
    rows = packed.size // LANES
    flipped = jnp.swapaxes(cache, 2, 3)
    vmem = pl.BlockSpec(memory_space=pltpu.VMEM)
    return pl.pallas_call(
        functools.partial(butterfly_kernel, rounds),
        out_shape=(
            jax.ShapeDtypeStruct(packed.shape, jnp.float32),
            jax.ShapeDtypeStruct(queries.shape, jnp.bfloat16),
        ),
        in_specs=[
            pl.BlockSpec(memory_space=pltpu.SMEM),
            vmem,
            vmem,
            vmem,
            pl.BlockSpec(memory_space=pl.ANY),
        ],
        out_specs=(vmem, vmem),
        scratch_shapes=[
            pltpu.VMEM((max(rounds - 1, 1),) + packed.shape, jnp.float32),
            pltpu.VMEM((rounds,) + packed.shape, jnp.float32),
            pltpu.SemaphoreType.DMA((rounds,)),
            pltpu.SemaphoreType.DMA((rounds,)),
            pltpu.VMEM(flipped.shape, flipped.dtype),
            pltpu.SemaphoreType.DMA(flipped.shape[:2]),
        ],
        compiler_params=pltpu.CompilerParams(collective_id=0, has_side_effects=True),
        cost_estimate=pl.CostEstimate(
            flops=8 * rows * LANES * rounds + 4 * 36 * queries.shape[0] * cache.size // 2,
            transcendentals=2 * rows * rounds,
            bytes_accessed=2 * rows * LANES * 4 * rounds + cache.size * 2,
        ),
    )(lengths, packed, queries, fresh, flipped)


def scatter_kernel(parts, x_ref, *rest):
    *out_refs, recv, local_sem, send_sem, recv_sem = rest
    me = lax.axis_index("tp")
    row = lax.axis_index("seq")
    barrier = pltpu.get_barrier_semaphore()
    for d in range(1, parts):
        pl.semaphore_signal(
            barrier, inc=1, device_id=(row, (me + d) % parts), device_id_type=MESH
        )
    pl.semaphore_wait(barrier, parts - 1)
    own = pltpu.make_async_copy(x_ref.at[me], recv.at[me], local_sem)
    own.start()
    copies = []
    for d in range(1, parts):
        copy = pltpu.make_async_remote_copy(
            src_ref=x_ref.at[(me + d) % parts],
            dst_ref=recv.at[me],
            send_sem=send_sem.at[d - 1],
            recv_sem=recv_sem.at[d - 1],
            device_id=(row, (me + d) % parts),
            device_id_type=MESH,
        )
        copy.start()
        copies.append(copy)
    own.wait()
    for d in range(1, parts):
        copies[d - 1].wait_send()
        pltpu.make_async_remote_copy(
            src_ref=x_ref.at[0],
            dst_ref=recv.at[(me + parts - d) % parts],
            send_sem=send_sem.at[d - 1],
            recv_sem=recv_sem.at[d - 1],
            device_id=(row, (me + parts - d) % parts),
            device_id_type=MESH,
        ).wait_recv()
    total = recv[0]
    for s in range(1, parts):
        total = total + recv[s]
    total = total.astype(jnp.bfloat16)
    start = 0
    for out_ref in out_refs:
        for r in range(out_ref.shape[0]):
            out_ref[r] = total[start : start + out_ref.shape[1]]
            start += out_ref.shape[1]


def tp_reduce_scatter(term, parts, shapes):
    rows, width = term.shape
    cols = width // parts
    blocks = jnp.transpose(term.reshape(rows, parts, cols), (1, 0, 2))
    vmem = pl.BlockSpec(memory_space=pltpu.VMEM)
    return pl.pallas_call(
        functools.partial(scatter_kernel, parts),
        out_shape=tuple(
            jax.ShapeDtypeStruct(shape + (cols,), jnp.bfloat16) for shape in shapes
        ),
        in_specs=[vmem],
        out_specs=tuple(vmem for _ in shapes),
        scratch_shapes=[
            pltpu.VMEM((parts, rows, cols), jnp.float32),
            pltpu.SemaphoreType.DMA(()),
            pltpu.SemaphoreType.DMA((parts - 1,)),
            pltpu.SemaphoreType.DMA((parts - 1,)),
        ],
        compiler_params=pltpu.CompilerParams(collective_id=1, has_side_effects=True),
        cost_estimate=pl.CostEstimate(
            flops=rows * width,
            transcendentals=0,
            bytes_accessed=3 * rows * width * 4,
        ),
    )(blocks)


def attention_kernel(with_fresh, len_ref, live_ref, off_ref, q_ref, k_ref, v_ref, *rest):
    tokens, width = q_ref.shape[1], q_ref.shape[2]
    positions = k_ref.shape[3]
    rows = (width // HEAD_DIM) * tokens
    request = pl.program_id(0)
    spot = lax.broadcasted_iota(jnp.int32, (1, positions), 1)
    usable = spot + off_ref[0] < len_ref[request]
    if not with_fresh:
        blocks = live_ref.shape[0]
        alive = spot < 0
        for b in range(blocks):
            alive = alive | (
                (spot // (positions // blocks) == b) & (live_ref[b, request] == 1)
            )
        usable = usable & alive
    pick = (
        lax.broadcasted_iota(jnp.int32, (rows, tokens), 0) % tokens
        == lax.broadcasted_iota(jnp.int32, (rows, tokens), 1)
    ).astype(jnp.bfloat16)
    head_lanes = (
        lax.broadcasted_iota(jnp.int32, (rows, width), 0) // tokens
        == lax.broadcasted_iota(jnp.int32, (rows, width), 1) // HEAD_DIM
    )
    spread = jnp.dot(pick, q_ref[0], preferred_element_type=jnp.float32)
    query = jnp.where(head_lanes, spread, 0.0).astype(jnp.bfloat16)
    contract = (((1,), (1,)), ((), ()))
    scale = 1.0 / math.sqrt(HEAD_DIM)
    scores = jnp.dot(query, k_ref[0, 0], preferred_element_type=jnp.float32) * scale
    scores = jnp.where(usable, scores, NEGATIVE)
    highest = jnp.max(scores, axis=1, keepdims=True)
    if with_fresh:
        fk_ref, fv_ref, o_ref = rest
        fresh_scores = lax.dot_general(
            query, fk_ref[0, 0], contract, preferred_element_type=jnp.float32
        ) * scale
        causal = lax.broadcasted_iota(jnp.int32, (rows, tokens), 1) <= (
            lax.broadcasted_iota(jnp.int32, (rows, tokens), 0) % tokens
        )
        fresh_scores = jnp.where(causal, fresh_scores, NEGATIVE)
        highest = jnp.maximum(highest, jnp.max(fresh_scores, axis=1, keepdims=True))
    expo = jnp.where(usable, jnp.exp(scores - highest), 0.0)
    totals = jnp.sum(expo, axis=1, keepdims=True)
    summed = lax.dot_general(
        expo.astype(jnp.bfloat16), v_ref[0, 0], contract, preferred_element_type=jnp.float32
    )
    if with_fresh:
        fresh_expo = jnp.where(causal, jnp.exp(fresh_scores - highest), 0.0)
        totals = totals + jnp.sum(fresh_expo, axis=1, keepdims=True)
        summed = summed + jnp.dot(
            fresh_expo.astype(jnp.bfloat16), fv_ref[0, 0], preferred_element_type=jnp.float32
        )
        normed = jnp.where(head_lanes, (summed / totals).astype(jnp.bfloat16), 0.0)
        gather = (
            lax.broadcasted_iota(jnp.int32, (tokens, rows), 1) % tokens
            == lax.broadcasted_iota(jnp.int32, (tokens, rows), 0)
        ).astype(jnp.bfloat16)
        o_ref[0] = jnp.dot(
            gather, normed.astype(jnp.bfloat16), preferred_element_type=jnp.float32
        ).astype(o_ref.dtype)
    else:
        (out_ref,) = rest
        masked = jnp.where(head_lanes, summed, 0.0)
        folded = masked[:, 0:HEAD_DIM]
        for g in range(1, width // HEAD_DIM):
            folded = folded + masked[:, g * HEAD_DIM : (g + 1) * HEAD_DIM]
        out_ref[0] = jnp.concatenate(
            [
                folded,
                highest,
                totals,
                jnp.zeros((rows, LANES - HEAD_DIM - 2), jnp.float32),
            ],
            axis=1,
        )


def attention(queries, cache, lengths, live, offset, fresh=None):
    count, tokens, width = queries.shape
    positions = cache.shape[2]
    rows = (width // HEAD_DIM) * tokens
    flipped = jnp.swapaxes(cache, 2, 3)
    specs = [
        pl.BlockSpec((1, tokens, width), lambda r, *_: (r, 0, 0)),
        pl.BlockSpec((1, 1, width, positions), lambda r, *_: (0, r, 0, 0)),
        pl.BlockSpec((1, 1, width, positions), lambda r, *_: (1, r, 0, 0)),
    ]
    operands = [lengths, live, offset, queries, flipped, flipped]
    if fresh is not None:
        specs += [
            pl.BlockSpec((1, 1, tokens, width), lambda r, *_: (0, r, 0, 0)),
            pl.BlockSpec((1, 1, tokens, width), lambda r, *_: (1, r, 0, 0)),
        ]
        operands += [fresh, fresh]
        out_shape = jax.ShapeDtypeStruct((count, tokens, width), jnp.bfloat16)
        out_specs = pl.BlockSpec((1, tokens, width), lambda r, *_: (r, 0, 0))
    else:
        out_shape = jax.ShapeDtypeStruct((count, rows, LANES), jnp.float32)
        out_specs = pl.BlockSpec((1, rows, LANES), lambda r, *_: (r, 0, 0))
    return pl.pallas_call(
        functools.partial(attention_kernel, fresh is not None),
        out_shape=out_shape,
        grid_spec=pltpu.PrefetchScalarGridSpec(
            num_scalar_prefetch=3, grid=(count,), in_specs=specs, out_specs=out_specs
        ),
        cost_estimate=pl.CostEstimate(
            flops=4 * count * rows * positions * width,
            transcendentals=count * rows * positions,
            bytes_accessed=2 * count * positions * width * 2,
        ),
    )(*operands)


def per_device(
    queries_short,
    cache_short,
    fresh_short,
    short_len,
    queries_long,
    cache_long,
    fresh_long,
    long_len,
    block_live,
    out_weight,
):
    request_count = queries_short.shape[0]
    token_count = queries_short.shape[1]
    local_len = cache_long.shape[2]
    packed = attention(
        queries_long,
        cache_long,
        long_len,
        block_live.T,
        (lax.axis_index("seq") * local_len).astype(jnp.int32).reshape(1),
    )
    heads = queries_long.shape[2] // HEAD_DIM
    shape = (queries_long.shape[0], heads, token_count)
    reduced, short_att = seq_allreduce(
        packed, lax.axis_size("seq"), short_len, queries_short, fresh_short, cache_short
    )
    merged = (
        reduced[..., HEAD_DIM].reshape(shape),
        reduced[..., HEAD_DIM + 1].reshape(shape),
        reduced[..., :HEAD_DIM].reshape(shape + (HEAD_DIM,)),
    )
    long_att = finish(combine_parts(merged, fresh_part(queries_long, fresh_long)))
    short_rows = short_att.reshape(-1, short_att.shape[2])
    both = jnp.concatenate([short_rows, long_att.reshape(-1, long_att.shape[2])], axis=0)
    term = jnp.dot(both, out_weight, preferred_element_type=jnp.float32)
    short_out, long_out = tp_reduce_scatter(
        term,
        lax.axis_size("tp"),
        ((request_count, token_count), (long_att.shape[0], long_att.shape[1])),
    )
    return (short_out, long_out)


def solution(mesh):
    in_specs = (
        P("seq", None, "tp"),
        P(None, "seq", None, "tp"),
        P(None, "seq", None, "tp"),
        P("seq"),
        P(None, None, "tp"),
        P(None, None, "seq", "tp"),
        P(None, None, None, "tp"),
        P(),
        P(None, "seq"),
        P("tp", None),
    )
    out_specs = (P("seq", None, "tp"), P(None, None, "tp"))
    return jax.shard_map(
        per_device, mesh=mesh, in_specs=in_specs, out_specs=out_specs, check_vma=False
    )
```

```python
import functools
import math

import jax
import jax.numpy as jnp
from jax import lax
from jax.experimental import pallas as pl
from jax.experimental.pallas import tpu as pltpu
from jax.sharding import PartitionSpec as P

HEAD_DIM = 64
MESH = pl.DeviceIdType.MESH
LANES = 128


NEGATIVE = -1e30


def split_heads(tensor):
    return tensor.reshape(tensor.shape[0], tensor.shape[1], tensor.shape[2] // HEAD_DIM, HEAD_DIM)


def partial_softmax(query_heads, key_heads, value_heads, usable):
    scores = jnp.einsum(
        "rjhd,rphd->rhjp", query_heads, key_heads, preferred_element_type=jnp.float32
    ) * (1.0 / math.sqrt(HEAD_DIM))
    scores = jnp.where(usable, scores, NEGATIVE)
    highest = jnp.max(scores, axis=-1)
    expo = jnp.where(usable, jnp.exp(scores - highest[..., None]), 0.0)
    totals = jnp.sum(expo, axis=-1)
    summed = jnp.einsum(
        "rhjp,rphd->rhjd",
        expo.astype(jnp.bfloat16),
        value_heads,
        preferred_element_type=jnp.float32,
    )
    return (highest, totals, summed)


def combine_parts(first, second):
    highest = jnp.maximum(first[0], second[0])
    scale_first = jnp.exp(first[0] - highest)
    scale_second = jnp.exp(second[0] - highest)
    totals = first[1] * scale_first + second[1] * scale_second
    summed = first[2] * scale_first[..., None] + second[2] * scale_second[..., None]
    return (highest, totals, summed)


def finish(parts):
    normed = (parts[2] / parts[1][..., None]).astype(jnp.bfloat16)
    normed = jnp.transpose(normed, (0, 2, 1, 3))
    return normed.reshape(normed.shape[0], normed.shape[1], normed.shape[2] * normed.shape[3])


def fresh_part(queries, fresh):
    count = queries.shape[1]
    causal = (jnp.arange(count)[:, None] >= jnp.arange(count)[None, :])[None, None]
    return partial_softmax(
        split_heads(queries), split_heads(fresh[0]), split_heads(fresh[1]), causal
    )


def merge_states(low, high):
    lane = lax.broadcasted_iota(jnp.int32, low.shape, low.ndim - 1)
    top_low = low[..., HEAD_DIM : HEAD_DIM + 1]
    top_high = high[..., HEAD_DIM : HEAD_DIM + 1]
    top = jnp.maximum(top_low, top_high)
    mixed = low * jnp.exp(top_low - top) + high * jnp.exp(top_high - top)
    return jnp.where(lane == HEAD_DIM, top, mixed)


def short_request(q, k_view, v_view, usable, fk, fv):
    tokens, width = q.shape
    rows = (width // HEAD_DIM) * tokens
    pick = (
        lax.broadcasted_iota(jnp.int32, (rows, tokens), 0) % tokens
        == lax.broadcasted_iota(jnp.int32, (rows, tokens), 1)
    ).astype(jnp.bfloat16)
    head_lanes = (
        lax.broadcasted_iota(jnp.int32, (rows, width), 0) // tokens
        == lax.broadcasted_iota(jnp.int32, (rows, width), 1) // HEAD_DIM
    )
    spread = jnp.dot(pick, q, preferred_element_type=jnp.float32)
    query = jnp.where(head_lanes, spread, 0.0).astype(jnp.bfloat16)
    contract = (((1,), (1,)), ((), ()))
    scale = 1.0 / math.sqrt(HEAD_DIM)
    scores = jnp.dot(query, k_view[...], preferred_element_type=jnp.float32) * scale
    scores = jnp.where(usable, scores, NEGATIVE)
    fresh_scores = lax.dot_general(query, fk, contract, preferred_element_type=jnp.float32) * scale
    causal = lax.broadcasted_iota(jnp.int32, (rows, tokens), 1) <= (
        lax.broadcasted_iota(jnp.int32, (rows, tokens), 0) % tokens
    )
    fresh_scores = jnp.where(causal, fresh_scores, NEGATIVE)
    highest = jnp.maximum(
        jnp.max(scores, axis=1, keepdims=True), jnp.max(fresh_scores, axis=1, keepdims=True)
    )
    expo = jnp.where(usable, jnp.exp(scores - highest), 0.0)
    fresh_expo = jnp.where(causal, jnp.exp(fresh_scores - highest), 0.0)
    totals = jnp.sum(expo, axis=1, keepdims=True) + jnp.sum(fresh_expo, axis=1, keepdims=True)
    summed = lax.dot_general(
        expo.astype(jnp.bfloat16), v_view[...], contract, preferred_element_type=jnp.float32
    ) + jnp.dot(fresh_expo.astype(jnp.bfloat16), fv, preferred_element_type=jnp.float32)
    normed = jnp.where(head_lanes, (summed / totals).astype(jnp.bfloat16), 0.0)
    gather = (
        lax.broadcasted_iota(jnp.int32, (tokens, rows), 1) % tokens
        == lax.broadcasted_iota(jnp.int32, (tokens, rows), 0)
    ).astype(jnp.bfloat16)
    return jnp.dot(gather, normed.astype(jnp.bfloat16), preferred_element_type=jnp.float32)


def finish_long(state, q, fk, fv):
    tokens, width = q.shape
    rows = (width // HEAD_DIM) * tokens
    pick = (
        lax.broadcasted_iota(jnp.int32, (rows, tokens), 0) % tokens
        == lax.broadcasted_iota(jnp.int32, (rows, tokens), 1)
    ).astype(jnp.bfloat16)
    head_lanes = (
        lax.broadcasted_iota(jnp.int32, (rows, width), 0) // tokens
        == lax.broadcasted_iota(jnp.int32, (rows, width), 1) // HEAD_DIM
    )
    spread = jnp.dot(pick, q, preferred_element_type=jnp.float32)
    query = jnp.where(head_lanes, spread, 0.0).astype(jnp.bfloat16)
    contract = (((1,), (1,)), ((), ()))
    fresh_scores = lax.dot_general(
        query, fk, contract, preferred_element_type=jnp.float32
    ) * (1.0 / math.sqrt(HEAD_DIM))
    causal = lax.broadcasted_iota(jnp.int32, (rows, tokens), 1) <= (
        lax.broadcasted_iota(jnp.int32, (rows, tokens), 0) % tokens
    )
    fresh_scores = jnp.where(causal, fresh_scores, NEGATIVE)
    top = state[:, HEAD_DIM : HEAD_DIM + 1]
    highest = jnp.maximum(top, jnp.max(fresh_scores, axis=1, keepdims=True))
    kept = jnp.exp(top - highest)
    fresh_expo = jnp.where(causal, jnp.exp(fresh_scores - highest), 0.0)
    totals = state[:, HEAD_DIM + 1 : HEAD_DIM + 2] * kept + jnp.sum(
        fresh_expo, axis=1, keepdims=True
    )
    fresh_sum = jnp.where(
        head_lanes,
        jnp.dot(fresh_expo.astype(jnp.bfloat16), fv, preferred_element_type=jnp.float32),
        0.0,
    )
    folded = fresh_sum[:, 0:HEAD_DIM]
    for g in range(1, width // HEAD_DIM):
        folded = folded + fresh_sum[:, g * HEAD_DIM : (g + 1) * HEAD_DIM]
    normed = ((state[:, :HEAD_DIM] * kept + folded) / totals).astype(jnp.float32)
    spread_back = jnp.concatenate([normed] * (width // HEAD_DIM), axis=1)
    placed = jnp.where(head_lanes, spread_back.astype(jnp.bfloat16), 0.0).astype(jnp.bfloat16)
    gather = (
        lax.broadcasted_iota(jnp.int32, (tokens, rows), 1) % tokens
        == lax.broadcasted_iota(jnp.int32, (tokens, rows), 0)
    ).astype(jnp.bfloat16)
    return jnp.dot(gather, placed, preferred_element_type=jnp.float32)


def butterfly_kernel(
    rounds, len_ref, x_ref, q_ref, f_ref, cache_ref, ql_ref, fl_ref, o_ref, att_ref,
    state, recv, send_sem, recv_sem, kv_buf, kv_sem,
):
    me = lax.axis_index("seq")
    column = lax.axis_index("tp")
    count = q_ref.shape[0]
    loads = []
    for r in range(count):
        pair = []
        for kv in range(2):
            load = pltpu.make_async_copy(
                cache_ref.at[kv, r], kv_buf.at[kv, r], kv_sem.at[kv, r]
            )
            load.start()
            pair.append(load)
        loads.append(pair)

    def short_step(r):
        for load in loads[r]:
            load.wait()
        spot = lax.broadcasted_iota(jnp.int32, (1, kv_buf.shape[3]), 1)
        att_ref[r] = short_request(
            q_ref[r], kv_buf.at[0, r], kv_buf.at[1, r], spot < len_ref[r],
            f_ref[0, r], f_ref[1, r],
        ).astype(att_ref.dtype)

    partners = []
    for k in range(rounds):
        step = 1 << k
        bit = (me // step) % 2
        partners.append((me + step - 2 * step * bit, bit))
    barrier = pltpu.get_barrier_semaphore()
    for partner, _ in partners:
        pl.semaphore_signal(
            barrier, inc=1, device_id=(partner, column), device_id_type=MESH
        )
    pl.semaphore_wait(barrier, rounds)
    for k in range(rounds):
        partner, bit = partners[k]
        source = x_ref if k == 0 else state.at[k - 1]
        copy = pltpu.make_async_remote_copy(
            src_ref=source,
            dst_ref=recv.at[k],
            send_sem=send_sem.at[k],
            recv_sem=recv_sem.at[k],
            device_id=(partner, column),
            device_id_type=MESH,
        )
        copy.start()
        if k < count:
            short_step(k)
        copy.wait()
        mine = source[...]
        theirs = recv[k]
        first = bit == 0
        merged = merge_states(
            jnp.where(first, mine, theirs), jnp.where(first, theirs, mine)
        )
        if k == rounds - 1:
            for r in range(o_ref.shape[0]):
                o_ref[r] = finish_long(
                    merged[r], ql_ref[r], fl_ref[0, r], fl_ref[1, r]
                ).astype(o_ref.dtype)
        else:
            state[k] = merged
    for r in range(rounds, count):
        short_step(r)


def seq_allreduce(packed, devices, lengths, queries, fresh, cache, queries_long, fresh_long):
    rounds = devices.bit_length() - 1
    rows = packed.size // LANES
    flipped = jnp.swapaxes(cache, 2, 3)
    vmem = pl.BlockSpec(memory_space=pltpu.VMEM)
    return pl.pallas_call(
        functools.partial(butterfly_kernel, rounds),
        out_shape=(
            jax.ShapeDtypeStruct(queries_long.shape, jnp.bfloat16),
            jax.ShapeDtypeStruct(queries.shape, jnp.bfloat16),
        ),
        in_specs=[
            pl.BlockSpec(memory_space=pltpu.SMEM),
            vmem,
            vmem,
            vmem,
            pl.BlockSpec(memory_space=pl.ANY),
            vmem,
            vmem,
        ],
        out_specs=(vmem, vmem),
        scratch_shapes=[
            pltpu.VMEM((max(rounds - 1, 1),) + packed.shape, jnp.float32),
            pltpu.VMEM((rounds,) + packed.shape, jnp.float32),
            pltpu.SemaphoreType.DMA((rounds,)),
            pltpu.SemaphoreType.DMA((rounds,)),
            pltpu.VMEM(flipped.shape, flipped.dtype),
            pltpu.SemaphoreType.DMA(flipped.shape[:2]),
        ],
        compiler_params=pltpu.CompilerParams(collective_id=0, has_side_effects=True),
        cost_estimate=pl.CostEstimate(
            flops=8 * rows * LANES * rounds + 4 * 36 * queries.shape[0] * cache.size // 2,
            transcendentals=2 * rows * rounds,
            bytes_accessed=2 * rows * LANES * 4 * rounds + cache.size * 2,
        ),
    )(lengths, packed, queries, fresh, flipped, queries_long, fresh_long)


def scatter_kernel(parts, x_ref, o_ref, recv, local_sem, send_sem, recv_sem):
    me = lax.axis_index("tp")
    row = lax.axis_index("seq")
    barrier = pltpu.get_barrier_semaphore()
    for d in range(1, parts):
        pl.semaphore_signal(
            barrier, inc=1, device_id=(row, (me + d) % parts), device_id_type=MESH
        )
    pl.semaphore_wait(barrier, parts - 1)
    own = pltpu.make_async_copy(x_ref.at[me], recv.at[me], local_sem)
    own.start()
    copies = []
    for d in range(1, parts):
        copy = pltpu.make_async_remote_copy(
            src_ref=x_ref.at[(me + d) % parts],
            dst_ref=recv.at[me],
            send_sem=send_sem.at[d - 1],
            recv_sem=recv_sem.at[d - 1],
            device_id=(row, (me + d) % parts),
            device_id_type=MESH,
        )
        copy.start()
        copies.append(copy)
    own.wait()
    for d in range(1, parts):
        copies[d - 1].wait_send()
        pltpu.make_async_remote_copy(
            src_ref=x_ref.at[0],
            dst_ref=recv.at[(me + parts - d) % parts],
            send_sem=send_sem.at[d - 1],
            recv_sem=recv_sem.at[d - 1],
            device_id=(row, (me + parts - d) % parts),
            device_id_type=MESH,
        ).wait_recv()
    total = recv[0]
    for s in range(1, parts):
        total = total + recv[s]
    o_ref[...] = total


def tp_reduce_scatter(term, parts):
    rows, width = term.shape
    cols = width // parts
    blocks = jnp.transpose(term.reshape(rows, parts, cols), (1, 0, 2))
    return pl.pallas_call(
        functools.partial(scatter_kernel, parts),
        out_shape=jax.ShapeDtypeStruct((rows, cols), jnp.float32),
        in_specs=[pl.BlockSpec(memory_space=pltpu.VMEM)],
        out_specs=pl.BlockSpec(memory_space=pltpu.VMEM),
        scratch_shapes=[
            pltpu.VMEM((parts, rows, cols), jnp.float32),
            pltpu.SemaphoreType.DMA(()),
            pltpu.SemaphoreType.DMA((parts - 1,)),
            pltpu.SemaphoreType.DMA((parts - 1,)),
        ],
        compiler_params=pltpu.CompilerParams(collective_id=1, has_side_effects=True),
        cost_estimate=pl.CostEstimate(
            flops=rows * width,
            transcendentals=0,
            bytes_accessed=3 * rows * width * 4,
        ),
    )(blocks)


def attention_kernel(with_fresh, len_ref, live_ref, off_ref, q_ref, k_ref, v_ref, *rest):
    tokens, width = q_ref.shape[1], q_ref.shape[2]
    positions = k_ref.shape[3]
    rows = (width // HEAD_DIM) * tokens
    request = pl.program_id(0)
    spot = lax.broadcasted_iota(jnp.int32, (1, positions), 1)
    usable = spot + off_ref[0] < len_ref[request]
    if not with_fresh:
        blocks = live_ref.shape[0]
        alive = spot < 0
        for b in range(blocks):
            alive = alive | (
                (spot // (positions // blocks) == b) & (live_ref[b, request] == 1)
            )
        usable = usable & alive
    pick = (
        lax.broadcasted_iota(jnp.int32, (rows, tokens), 0) % tokens
        == lax.broadcasted_iota(jnp.int32, (rows, tokens), 1)
    ).astype(jnp.bfloat16)
    head_lanes = (
        lax.broadcasted_iota(jnp.int32, (rows, width), 0) // tokens
        == lax.broadcasted_iota(jnp.int32, (rows, width), 1) // HEAD_DIM
    )
    spread = jnp.dot(pick, q_ref[0], preferred_element_type=jnp.float32)
    query = jnp.where(head_lanes, spread, 0.0).astype(jnp.bfloat16)
    contract = (((1,), (1,)), ((), ()))
    scale = 1.0 / math.sqrt(HEAD_DIM)
    scores = jnp.dot(query, k_ref[0, 0], preferred_element_type=jnp.float32) * scale
    scores = jnp.where(usable, scores, NEGATIVE)
    highest = jnp.max(scores, axis=1, keepdims=True)
    if with_fresh:
        fk_ref, fv_ref, o_ref = rest
        fresh_scores = lax.dot_general(
            query, fk_ref[0, 0], contract, preferred_element_type=jnp.float32
        ) * scale
        causal = lax.broadcasted_iota(jnp.int32, (rows, tokens), 1) <= (
            lax.broadcasted_iota(jnp.int32, (rows, tokens), 0) % tokens
        )
        fresh_scores = jnp.where(causal, fresh_scores, NEGATIVE)
        highest = jnp.maximum(highest, jnp.max(fresh_scores, axis=1, keepdims=True))
    expo = jnp.where(usable, jnp.exp(scores - highest), 0.0)
    totals = jnp.sum(expo, axis=1, keepdims=True)
    summed = lax.dot_general(
        expo.astype(jnp.bfloat16), v_ref[0, 0], contract, preferred_element_type=jnp.float32
    )
    if with_fresh:
        fresh_expo = jnp.where(causal, jnp.exp(fresh_scores - highest), 0.0)
        totals = totals + jnp.sum(fresh_expo, axis=1, keepdims=True)
        summed = summed + jnp.dot(
            fresh_expo.astype(jnp.bfloat16), fv_ref[0, 0], preferred_element_type=jnp.float32
        )
        normed = jnp.where(head_lanes, (summed / totals).astype(jnp.bfloat16), 0.0)
        gather = (
            lax.broadcasted_iota(jnp.int32, (tokens, rows), 1) % tokens
            == lax.broadcasted_iota(jnp.int32, (tokens, rows), 0)
        ).astype(jnp.bfloat16)
        o_ref[0] = jnp.dot(
            gather, normed.astype(jnp.bfloat16), preferred_element_type=jnp.float32
        ).astype(o_ref.dtype)
    else:
        (out_ref,) = rest
        masked = jnp.where(head_lanes, summed, 0.0)
        folded = masked[:, 0:HEAD_DIM]
        for g in range(1, width // HEAD_DIM):
            folded = folded + masked[:, g * HEAD_DIM : (g + 1) * HEAD_DIM]
        out_ref[0] = jnp.concatenate(
            [
                folded,
                highest,
                totals,
                jnp.zeros((rows, LANES - HEAD_DIM - 2), jnp.float32),
            ],
            axis=1,
        )


def attention(queries, cache, lengths, live, offset, fresh=None):
    count, tokens, width = queries.shape
    positions = cache.shape[2]
    rows = (width // HEAD_DIM) * tokens
    flipped = jnp.swapaxes(cache, 2, 3)
    specs = [
        pl.BlockSpec((1, tokens, width), lambda r, *_: (r, 0, 0)),
        pl.BlockSpec((1, 1, width, positions), lambda r, *_: (0, r, 0, 0)),
        pl.BlockSpec((1, 1, width, positions), lambda r, *_: (1, r, 0, 0)),
    ]
    operands = [lengths, live, offset, queries, flipped, flipped]
    if fresh is not None:
        specs += [
            pl.BlockSpec((1, 1, tokens, width), lambda r, *_: (0, r, 0, 0)),
            pl.BlockSpec((1, 1, tokens, width), lambda r, *_: (1, r, 0, 0)),
        ]
        operands += [fresh, fresh]
        out_shape = jax.ShapeDtypeStruct((count, tokens, width), jnp.bfloat16)
        out_specs = pl.BlockSpec((1, tokens, width), lambda r, *_: (r, 0, 0))
    else:
        out_shape = jax.ShapeDtypeStruct((count, rows, LANES), jnp.float32)
        out_specs = pl.BlockSpec((1, rows, LANES), lambda r, *_: (r, 0, 0))
    return pl.pallas_call(
        functools.partial(attention_kernel, fresh is not None),
        out_shape=out_shape,
        grid_spec=pltpu.PrefetchScalarGridSpec(
            num_scalar_prefetch=3, grid=(count,), in_specs=specs, out_specs=out_specs
        ),
        cost_estimate=pl.CostEstimate(
            flops=4 * count * rows * positions * width,
            transcendentals=count * rows * positions,
            bytes_accessed=2 * count * positions * width * 2,
        ),
    )(*operands)


def per_device(
    queries_short,
    cache_short,
    fresh_short,
    short_len,
    queries_long,
    cache_long,
    fresh_long,
    long_len,
    block_live,
    out_weight,
):
    request_count = queries_short.shape[0]
    token_count = queries_short.shape[1]
    local_len = cache_long.shape[2]
    packed = attention(
        queries_long,
        cache_long,
        long_len,
        block_live.T,
        (lax.axis_index("seq") * local_len).astype(jnp.int32).reshape(1),
    )
    heads = queries_long.shape[2] // HEAD_DIM
    shape = (queries_long.shape[0], heads, token_count)
    long_att, short_att = seq_allreduce(
        packed,
        lax.axis_size("seq"),
        short_len,
        queries_short,
        fresh_short,
        cache_short,
        queries_long,
        fresh_long,
    )
    short_rows = short_att.reshape(-1, short_att.shape[2])
    both = jnp.concatenate([short_rows, long_att.reshape(-1, long_att.shape[2])], axis=0)
    term = jnp.dot(both, out_weight, preferred_element_type=jnp.float32)
    cols = tp_reduce_scatter(term, lax.axis_size("tp")).astype(jnp.bfloat16)
    short_out = cols[: short_rows.shape[0]].reshape(request_count, token_count, cols.shape[1])
    long_out = cols[short_rows.shape[0] :].reshape(
        long_att.shape[0], long_att.shape[1], cols.shape[1]
    )
    return (short_out, long_out)


def solution(mesh):
    in_specs = (
        P("seq", None, "tp"),
        P(None, "seq", None, "tp"),
        P(None, "seq", None, "tp"),
        P("seq"),
        P(None, None, "tp"),
        P(None, None, "seq", "tp"),
        P(None, None, None, "tp"),
        P(),
        P(None, "seq"),
        P("tp", None),
    )
    out_specs = (P("seq", None, "tp"), P(None, None, "tp"))
    return jax.shard_map(
        per_device, mesh=mesh, in_specs=in_specs, out_specs=out_specs, check_vma=False
    )
```

```python
import functools
import math

import jax
import jax.numpy as jnp
from jax import lax
from jax.experimental import pallas as pl
from jax.experimental.pallas import tpu as pltpu
from jax.sharding import PartitionSpec as P

HEAD_DIM = 64
MESH = pl.DeviceIdType.MESH
LANES = 128


NEGATIVE = -1e30


def split_heads(tensor):
    return tensor.reshape(tensor.shape[0], tensor.shape[1], tensor.shape[2] // HEAD_DIM, HEAD_DIM)


def partial_softmax(query_heads, key_heads, value_heads, usable):
    scores = jnp.einsum(
        "rjhd,rphd->rhjp", query_heads, key_heads, preferred_element_type=jnp.float32
    ) * (1.0 / math.sqrt(HEAD_DIM))
    scores = jnp.where(usable, scores, NEGATIVE)
    highest = jnp.max(scores, axis=-1)
    expo = jnp.where(usable, jnp.exp(scores - highest[..., None]), 0.0)
    totals = jnp.sum(expo, axis=-1)
    summed = jnp.einsum(
        "rhjp,rphd->rhjd",
        expo.astype(jnp.bfloat16),
        value_heads,
        preferred_element_type=jnp.float32,
    )
    return (highest, totals, summed)


def combine_parts(first, second):
    highest = jnp.maximum(first[0], second[0])
    scale_first = jnp.exp(first[0] - highest)
    scale_second = jnp.exp(second[0] - highest)
    totals = first[1] * scale_first + second[1] * scale_second
    summed = first[2] * scale_first[..., None] + second[2] * scale_second[..., None]
    return (highest, totals, summed)


def finish(parts):
    normed = (parts[2] / parts[1][..., None]).astype(jnp.bfloat16)
    normed = jnp.transpose(normed, (0, 2, 1, 3))
    return normed.reshape(normed.shape[0], normed.shape[1], normed.shape[2] * normed.shape[3])


def fresh_part(queries, fresh):
    count = queries.shape[1]
    causal = (jnp.arange(count)[:, None] >= jnp.arange(count)[None, :])[None, None]
    return partial_softmax(
        split_heads(queries), split_heads(fresh[0]), split_heads(fresh[1]), causal
    )


def merge_states(low, high):
    lane = lax.broadcasted_iota(jnp.int32, low.shape, low.ndim - 1)
    top_low = low[..., HEAD_DIM : HEAD_DIM + 1]
    top_high = high[..., HEAD_DIM : HEAD_DIM + 1]
    top = jnp.maximum(top_low, top_high)
    mixed = low * jnp.exp(top_low - top) + high * jnp.exp(top_high - top)
    return jnp.where(lane == HEAD_DIM, top, mixed)


def short_request(q, k_view, v_view, usable, fk, fv):
    tokens, width = q.shape
    rows = (width // HEAD_DIM) * tokens
    pick = (
        lax.broadcasted_iota(jnp.int32, (rows, tokens), 0) % tokens
        == lax.broadcasted_iota(jnp.int32, (rows, tokens), 1)
    ).astype(jnp.bfloat16)
    head_lanes = (
        lax.broadcasted_iota(jnp.int32, (rows, width), 0) // tokens
        == lax.broadcasted_iota(jnp.int32, (rows, width), 1) // HEAD_DIM
    )
    spread = jnp.dot(pick, q, preferred_element_type=jnp.float32)
    query = jnp.where(head_lanes, spread, 0.0).astype(jnp.bfloat16)
    contract = (((1,), (1,)), ((), ()))
    scale = 1.0 / math.sqrt(HEAD_DIM)
    scores = jnp.dot(query, k_view[...], preferred_element_type=jnp.float32) * scale
    scores = jnp.where(usable, scores, NEGATIVE)
    fresh_scores = lax.dot_general(query, fk, contract, preferred_element_type=jnp.float32) * scale
    causal = lax.broadcasted_iota(jnp.int32, (rows, tokens), 1) <= (
        lax.broadcasted_iota(jnp.int32, (rows, tokens), 0) % tokens
    )
    fresh_scores = jnp.where(causal, fresh_scores, NEGATIVE)
    highest = jnp.maximum(
        jnp.max(scores, axis=1, keepdims=True), jnp.max(fresh_scores, axis=1, keepdims=True)
    )
    expo = jnp.where(usable, jnp.exp(scores - highest), 0.0)
    fresh_expo = jnp.where(causal, jnp.exp(fresh_scores - highest), 0.0)
    totals = jnp.sum(expo, axis=1, keepdims=True) + jnp.sum(fresh_expo, axis=1, keepdims=True)
    summed = lax.dot_general(
        expo.astype(jnp.bfloat16), v_view[...], contract, preferred_element_type=jnp.float32
    ) + jnp.dot(fresh_expo.astype(jnp.bfloat16), fv, preferred_element_type=jnp.float32)
    normed = jnp.where(head_lanes, (summed / totals).astype(jnp.bfloat16), 0.0)
    gather = (
        lax.broadcasted_iota(jnp.int32, (tokens, rows), 1) % tokens
        == lax.broadcasted_iota(jnp.int32, (tokens, rows), 0)
    ).astype(jnp.bfloat16)
    return jnp.dot(gather, normed.astype(jnp.bfloat16), preferred_element_type=jnp.float32)


def finish_long(state, q, fk, fv):
    tokens, width = q.shape
    rows = (width // HEAD_DIM) * tokens
    pick = (
        lax.broadcasted_iota(jnp.int32, (rows, tokens), 0) % tokens
        == lax.broadcasted_iota(jnp.int32, (rows, tokens), 1)
    ).astype(jnp.bfloat16)
    head_lanes = (
        lax.broadcasted_iota(jnp.int32, (rows, width), 0) // tokens
        == lax.broadcasted_iota(jnp.int32, (rows, width), 1) // HEAD_DIM
    )
    spread = jnp.dot(pick, q, preferred_element_type=jnp.float32)
    query = jnp.where(head_lanes, spread, 0.0).astype(jnp.bfloat16)
    contract = (((1,), (1,)), ((), ()))
    fresh_scores = lax.dot_general(
        query, fk, contract, preferred_element_type=jnp.float32
    ) * (1.0 / math.sqrt(HEAD_DIM))
    causal = lax.broadcasted_iota(jnp.int32, (rows, tokens), 1) <= (
        lax.broadcasted_iota(jnp.int32, (rows, tokens), 0) % tokens
    )
    fresh_scores = jnp.where(causal, fresh_scores, NEGATIVE)
    top = state[:, HEAD_DIM : HEAD_DIM + 1]
    highest = jnp.maximum(top, jnp.max(fresh_scores, axis=1, keepdims=True))
    kept = jnp.exp(top - highest)
    fresh_expo = jnp.where(causal, jnp.exp(fresh_scores - highest), 0.0)
    totals = state[:, HEAD_DIM + 1 : HEAD_DIM + 2] * kept + jnp.sum(
        fresh_expo, axis=1, keepdims=True
    )
    fresh_sum = jnp.where(
        head_lanes,
        jnp.dot(fresh_expo.astype(jnp.bfloat16), fv, preferred_element_type=jnp.float32),
        0.0,
    )
    folded = fresh_sum[:, 0:HEAD_DIM]
    for g in range(1, width // HEAD_DIM):
        folded = folded + fresh_sum[:, g * HEAD_DIM : (g + 1) * HEAD_DIM]
    normed = ((state[:, :HEAD_DIM] * kept + folded) / totals).astype(jnp.float32)
    spread_back = jnp.concatenate([normed] * (width // HEAD_DIM), axis=1)
    placed = jnp.where(head_lanes, spread_back.astype(jnp.bfloat16), 0.0).astype(jnp.bfloat16)
    gather = (
        lax.broadcasted_iota(jnp.int32, (tokens, rows), 1) % tokens
        == lax.broadcasted_iota(jnp.int32, (tokens, rows), 0)
    ).astype(jnp.bfloat16)
    return jnp.dot(gather, placed, preferred_element_type=jnp.float32)


def butterfly_kernel(
    rounds, len_ref, x_ref, q_ref, f_ref, cache_ref, ql_ref, fl_ref, att_ref,
    state, recv, send_sem, recv_sem, kv_buf, kv_sem,
):
    me = lax.axis_index("seq")
    column = lax.axis_index("tp")
    count, tokens = q_ref.shape[0], q_ref.shape[1]
    loads = []
    for r in range(count):
        pair = []
        for kv in range(2):
            load = pltpu.make_async_copy(
                cache_ref.at[kv, r], kv_buf.at[kv, r], kv_sem.at[kv, r]
            )
            load.start()
            pair.append(load)
        loads.append(pair)

    def short_step(r):
        for load in loads[r]:
            load.wait()
        spot = lax.broadcasted_iota(jnp.int32, (1, kv_buf.shape[3]), 1)
        att_ref[r * tokens : (r + 1) * tokens] = short_request(
            q_ref[r], kv_buf.at[0, r], kv_buf.at[1, r], spot < len_ref[r],
            f_ref[0, r], f_ref[1, r],
        ).astype(att_ref.dtype)

    partners = []
    for k in range(rounds):
        step = 1 << k
        bit = (me // step) % 2
        partners.append((me + step - 2 * step * bit, bit))
    barrier = pltpu.get_barrier_semaphore()
    for partner, _ in partners:
        pl.semaphore_signal(
            barrier, inc=1, device_id=(partner, column), device_id_type=MESH
        )
    pl.semaphore_wait(barrier, rounds)
    for k in range(rounds):
        partner, bit = partners[k]
        source = x_ref if k == 0 else state.at[k - 1]
        copy = pltpu.make_async_remote_copy(
            src_ref=source,
            dst_ref=recv.at[k],
            send_sem=send_sem.at[k],
            recv_sem=recv_sem.at[k],
            device_id=(partner, column),
            device_id_type=MESH,
        )
        copy.start()
        if k < count:
            short_step(k)
        copy.wait()
        mine = source[...]
        theirs = recv[k]
        first = bit == 0
        merged = merge_states(
            jnp.where(first, mine, theirs), jnp.where(first, theirs, mine)
        )
        if k == rounds - 1:
            for r in range(ql_ref.shape[0]):
                row = (count + r) * tokens
                att_ref[row : row + tokens] = finish_long(
                    merged[r], ql_ref[r], fl_ref[0, r], fl_ref[1, r]
                ).astype(att_ref.dtype)
        else:
            state[k] = merged
    for r in range(rounds, count):
        short_step(r)


def seq_allreduce(packed, devices, lengths, queries, fresh, cache, queries_long, fresh_long):
    rounds = devices.bit_length() - 1
    rows = packed.size // LANES
    flipped = jnp.swapaxes(cache, 2, 3)
    vmem = pl.BlockSpec(memory_space=pltpu.VMEM)
    return pl.pallas_call(
        functools.partial(butterfly_kernel, rounds),
        out_shape=jax.ShapeDtypeStruct(
            (
                (queries.shape[0] + queries_long.shape[0]) * queries.shape[1],
                queries.shape[2],
            ),
            jnp.bfloat16,
        ),
        in_specs=[
            pl.BlockSpec(memory_space=pltpu.SMEM),
            vmem,
            vmem,
            vmem,
            pl.BlockSpec(memory_space=pl.ANY),
            vmem,
            vmem,
        ],
        out_specs=vmem,
        scratch_shapes=[
            pltpu.VMEM((max(rounds - 1, 1),) + packed.shape, jnp.float32),
            pltpu.VMEM((rounds,) + packed.shape, jnp.float32),
            pltpu.SemaphoreType.DMA((rounds,)),
            pltpu.SemaphoreType.DMA((rounds,)),
            pltpu.VMEM(flipped.shape, flipped.dtype),
            pltpu.SemaphoreType.DMA(flipped.shape[:2]),
        ],
        compiler_params=pltpu.CompilerParams(collective_id=0, has_side_effects=True),
        cost_estimate=pl.CostEstimate(
            flops=8 * rows * LANES * rounds + 4 * 36 * queries.shape[0] * cache.size // 2,
            transcendentals=2 * rows * rounds,
            bytes_accessed=2 * rows * LANES * 4 * rounds + cache.size * 2,
        ),
    )(lengths, packed, queries, fresh, flipped, queries_long, fresh_long)


def scatter_kernel(parts, x_ref, o_ref, recv, local_sem, send_sem, recv_sem):
    me = lax.axis_index("tp")
    row = lax.axis_index("seq")
    barrier = pltpu.get_barrier_semaphore()
    for d in range(1, parts):
        pl.semaphore_signal(
            barrier, inc=1, device_id=(row, (me + d) % parts), device_id_type=MESH
        )
    pl.semaphore_wait(barrier, parts - 1)
    own = pltpu.make_async_copy(x_ref.at[me], recv.at[me], local_sem)
    own.start()
    copies = []
    for d in range(1, parts):
        copy = pltpu.make_async_remote_copy(
            src_ref=x_ref.at[(me + d) % parts],
            dst_ref=recv.at[me],
            send_sem=send_sem.at[d - 1],
            recv_sem=recv_sem.at[d - 1],
            device_id=(row, (me + d) % parts),
            device_id_type=MESH,
        )
        copy.start()
        copies.append(copy)
    own.wait()
    for d in range(1, parts):
        copies[d - 1].wait_send()
        pltpu.make_async_remote_copy(
            src_ref=x_ref.at[0],
            dst_ref=recv.at[(me + parts - d) % parts],
            send_sem=send_sem.at[d - 1],
            recv_sem=recv_sem.at[d - 1],
            device_id=(row, (me + parts - d) % parts),
            device_id_type=MESH,
        ).wait_recv()
    total = recv[0]
    for s in range(1, parts):
        total = total + recv[s]
    o_ref[...] = total


def tp_reduce_scatter(term, parts):
    rows, width = term.shape
    cols = width // parts
    blocks = jnp.transpose(term.reshape(rows, parts, cols), (1, 0, 2))
    return pl.pallas_call(
        functools.partial(scatter_kernel, parts),
        out_shape=jax.ShapeDtypeStruct((rows, cols), jnp.float32),
        in_specs=[pl.BlockSpec(memory_space=pltpu.VMEM)],
        out_specs=pl.BlockSpec(memory_space=pltpu.VMEM),
        scratch_shapes=[
            pltpu.VMEM((parts, rows, cols), jnp.float32),
            pltpu.SemaphoreType.DMA(()),
            pltpu.SemaphoreType.DMA((parts - 1,)),
            pltpu.SemaphoreType.DMA((parts - 1,)),
        ],
        compiler_params=pltpu.CompilerParams(collective_id=1, has_side_effects=True),
        cost_estimate=pl.CostEstimate(
            flops=rows * width,
            transcendentals=0,
            bytes_accessed=3 * rows * width * 4,
        ),
    )(blocks)


def attention_kernel(with_fresh, len_ref, live_ref, off_ref, q_ref, k_ref, v_ref, *rest):
    tokens, width = q_ref.shape[1], q_ref.shape[2]
    positions = k_ref.shape[3]
    rows = (width // HEAD_DIM) * tokens
    request = pl.program_id(0)
    spot = lax.broadcasted_iota(jnp.int32, (1, positions), 1)
    usable = spot + off_ref[0] < len_ref[request]
    if not with_fresh:
        blocks = live_ref.shape[0]
        alive = spot < 0
        for b in range(blocks):
            alive = alive | (
                (spot // (positions // blocks) == b) & (live_ref[b, request] == 1)
            )
        usable = usable & alive
    pick = (
        lax.broadcasted_iota(jnp.int32, (rows, tokens), 0) % tokens
        == lax.broadcasted_iota(jnp.int32, (rows, tokens), 1)
    ).astype(jnp.bfloat16)
    head_lanes = (
        lax.broadcasted_iota(jnp.int32, (rows, width), 0) // tokens
        == lax.broadcasted_iota(jnp.int32, (rows, width), 1) // HEAD_DIM
    )
    spread = jnp.dot(pick, q_ref[0], preferred_element_type=jnp.float32)
    query = jnp.where(head_lanes, spread, 0.0).astype(jnp.bfloat16)
    contract = (((1,), (1,)), ((), ()))
    scale = 1.0 / math.sqrt(HEAD_DIM)
    scores = jnp.dot(query, k_ref[0, 0], preferred_element_type=jnp.float32) * scale
    scores = jnp.where(usable, scores, NEGATIVE)
    highest = jnp.max(scores, axis=1, keepdims=True)
    if with_fresh:
        fk_ref, fv_ref, o_ref = rest
        fresh_scores = lax.dot_general(
            query, fk_ref[0, 0], contract, preferred_element_type=jnp.float32
        ) * scale
        causal = lax.broadcasted_iota(jnp.int32, (rows, tokens), 1) <= (
            lax.broadcasted_iota(jnp.int32, (rows, tokens), 0) % tokens
        )
        fresh_scores = jnp.where(causal, fresh_scores, NEGATIVE)
        highest = jnp.maximum(highest, jnp.max(fresh_scores, axis=1, keepdims=True))
    expo = jnp.where(usable, jnp.exp(scores - highest), 0.0)
    totals = jnp.sum(expo, axis=1, keepdims=True)
    summed = lax.dot_general(
        expo.astype(jnp.bfloat16), v_ref[0, 0], contract, preferred_element_type=jnp.float32
    )
    if with_fresh:
        fresh_expo = jnp.where(causal, jnp.exp(fresh_scores - highest), 0.0)
        totals = totals + jnp.sum(fresh_expo, axis=1, keepdims=True)
        summed = summed + jnp.dot(
            fresh_expo.astype(jnp.bfloat16), fv_ref[0, 0], preferred_element_type=jnp.float32
        )
        normed = jnp.where(head_lanes, (summed / totals).astype(jnp.bfloat16), 0.0)
        gather = (
            lax.broadcasted_iota(jnp.int32, (tokens, rows), 1) % tokens
            == lax.broadcasted_iota(jnp.int32, (tokens, rows), 0)
        ).astype(jnp.bfloat16)
        o_ref[0] = jnp.dot(
            gather, normed.astype(jnp.bfloat16), preferred_element_type=jnp.float32
        ).astype(o_ref.dtype)
    else:
        (out_ref,) = rest
        masked = jnp.where(head_lanes, summed, 0.0)
        folded = masked[:, 0:HEAD_DIM]
        for g in range(1, width // HEAD_DIM):
            folded = folded + masked[:, g * HEAD_DIM : (g + 1) * HEAD_DIM]
        out_ref[0] = jnp.concatenate(
            [
                folded,
                highest,
                totals,
                jnp.zeros((rows, LANES - HEAD_DIM - 2), jnp.float32),
            ],
            axis=1,
        )


def attention(queries, cache, lengths, live, offset, fresh=None):
    count, tokens, width = queries.shape
    positions = cache.shape[2]
    rows = (width // HEAD_DIM) * tokens
    flipped = jnp.swapaxes(cache, 2, 3)
    specs = [
        pl.BlockSpec((1, tokens, width), lambda r, *_: (r, 0, 0)),
        pl.BlockSpec((1, 1, width, positions), lambda r, *_: (0, r, 0, 0)),
        pl.BlockSpec((1, 1, width, positions), lambda r, *_: (1, r, 0, 0)),
    ]
    operands = [lengths, live, offset, queries, flipped, flipped]
    if fresh is not None:
        specs += [
            pl.BlockSpec((1, 1, tokens, width), lambda r, *_: (0, r, 0, 0)),
            pl.BlockSpec((1, 1, tokens, width), lambda r, *_: (1, r, 0, 0)),
        ]
        operands += [fresh, fresh]
        out_shape = jax.ShapeDtypeStruct((count, tokens, width), jnp.bfloat16)
        out_specs = pl.BlockSpec((1, tokens, width), lambda r, *_: (r, 0, 0))
    else:
        out_shape = jax.ShapeDtypeStruct((count, rows, LANES), jnp.float32)
        out_specs = pl.BlockSpec((1, rows, LANES), lambda r, *_: (r, 0, 0))
    return pl.pallas_call(
        functools.partial(attention_kernel, fresh is not None),
        out_shape=out_shape,
        grid_spec=pltpu.PrefetchScalarGridSpec(
            num_scalar_prefetch=3, grid=(count,), in_specs=specs, out_specs=out_specs
        ),
        cost_estimate=pl.CostEstimate(
            flops=4 * count * rows * positions * width,
            transcendentals=count * rows * positions,
            bytes_accessed=2 * count * positions * width * 2,
        ),
    )(*operands)


def per_device(
    queries_short,
    cache_short,
    fresh_short,
    short_len,
    queries_long,
    cache_long,
    fresh_long,
    long_len,
    block_live,
    out_weight,
):
    request_count = queries_short.shape[0]
    token_count = queries_short.shape[1]
    local_len = cache_long.shape[2]
    packed = attention(
        queries_long,
        cache_long,
        long_len,
        block_live.T,
        (lax.axis_index("seq") * local_len).astype(jnp.int32).reshape(1),
    )
    heads = queries_long.shape[2] // HEAD_DIM
    shape = (queries_long.shape[0], heads, token_count)
    both = seq_allreduce(
        packed,
        lax.axis_size("seq"),
        short_len,
        queries_short,
        fresh_short,
        cache_short,
        queries_long,
        fresh_long,
    )
    short_count = request_count * token_count
    term = jnp.dot(both, out_weight, preferred_element_type=jnp.float32)
    cols = tp_reduce_scatter(term, lax.axis_size("tp")).astype(jnp.bfloat16)
    short_out = cols[:short_count].reshape(request_count, token_count, cols.shape[1])
    long_out = cols[short_count:].reshape(
        queries_long.shape[0], queries_long.shape[1], cols.shape[1]
    )
    return (short_out, long_out)


def solution(mesh):
    in_specs = (
        P("seq", None, "tp"),
        P(None, "seq", None, "tp"),
        P(None, "seq", None, "tp"),
        P("seq"),
        P(None, None, "tp"),
        P(None, None, "seq", "tp"),
        P(None, None, None, "tp"),
        P(),
        P(None, "seq"),
        P("tp", None),
    )
    out_specs = (P("seq", None, "tp"), P(None, None, "tp"))
    return jax.shard_map(
        per_device, mesh=mesh, in_specs=in_specs, out_specs=out_specs, check_vma=False
    )
```

```python
import functools
import math

import jax
import jax.numpy as jnp
from jax import lax
from jax.experimental import pallas as pl
from jax.experimental.pallas import tpu as pltpu
from jax.sharding import PartitionSpec as P

HEAD_DIM = 64
MESH = pl.DeviceIdType.MESH
LANES = 128


NEGATIVE = -1e30


def split_heads(tensor):
    return tensor.reshape(tensor.shape[0], tensor.shape[1], tensor.shape[2] // HEAD_DIM, HEAD_DIM)


def partial_softmax(query_heads, key_heads, value_heads, usable):
    scores = jnp.einsum(
        "rjhd,rphd->rhjp", query_heads, key_heads, preferred_element_type=jnp.float32
    ) * (1.0 / math.sqrt(HEAD_DIM))
    scores = jnp.where(usable, scores, NEGATIVE)
    highest = jnp.max(scores, axis=-1)
    expo = jnp.where(usable, jnp.exp(scores - highest[..., None]), 0.0)
    totals = jnp.sum(expo, axis=-1)
    summed = jnp.einsum(
        "rhjp,rphd->rhjd",
        expo.astype(jnp.bfloat16),
        value_heads,
        preferred_element_type=jnp.float32,
    )
    return (highest, totals, summed)


def combine_parts(first, second):
    highest = jnp.maximum(first[0], second[0])
    scale_first = jnp.exp(first[0] - highest)
    scale_second = jnp.exp(second[0] - highest)
    totals = first[1] * scale_first + second[1] * scale_second
    summed = first[2] * scale_first[..., None] + second[2] * scale_second[..., None]
    return (highest, totals, summed)


def finish(parts):
    normed = (parts[2] / parts[1][..., None]).astype(jnp.bfloat16)
    normed = jnp.transpose(normed, (0, 2, 1, 3))
    return normed.reshape(normed.shape[0], normed.shape[1], normed.shape[2] * normed.shape[3])


def fresh_part(queries, fresh):
    count = queries.shape[1]
    causal = (jnp.arange(count)[:, None] >= jnp.arange(count)[None, :])[None, None]
    return partial_softmax(
        split_heads(queries), split_heads(fresh[0]), split_heads(fresh[1]), causal
    )


def merge_states(low, high):
    lane = lax.broadcasted_iota(jnp.int32, low.shape, low.ndim - 1)
    top_low = low[..., HEAD_DIM : HEAD_DIM + 1]
    top_high = high[..., HEAD_DIM : HEAD_DIM + 1]
    top = jnp.maximum(top_low, top_high)
    mixed = low * jnp.exp(top_low - top) + high * jnp.exp(top_high - top)
    return jnp.where(lane == HEAD_DIM, top, mixed)


def short_request(q, k_view, v_view, usable, fk, fv):
    tokens, width = q.shape
    rows = (width // HEAD_DIM) * tokens
    pick = (
        lax.broadcasted_iota(jnp.int32, (rows, tokens), 0) % tokens
        == lax.broadcasted_iota(jnp.int32, (rows, tokens), 1)
    ).astype(jnp.bfloat16)
    head_lanes = (
        lax.broadcasted_iota(jnp.int32, (rows, width), 0) // tokens
        == lax.broadcasted_iota(jnp.int32, (rows, width), 1) // HEAD_DIM
    )
    spread = jnp.dot(pick, q, preferred_element_type=jnp.float32)
    query = jnp.where(head_lanes, spread, 0.0).astype(jnp.bfloat16)
    contract = (((1,), (1,)), ((), ()))
    scale = 1.0 / math.sqrt(HEAD_DIM)
    scores = jnp.dot(query, k_view[...], preferred_element_type=jnp.float32) * scale
    scores = jnp.where(usable, scores, NEGATIVE)
    fresh_scores = lax.dot_general(query, fk, contract, preferred_element_type=jnp.float32) * scale
    causal = lax.broadcasted_iota(jnp.int32, (rows, tokens), 1) <= (
        lax.broadcasted_iota(jnp.int32, (rows, tokens), 0) % tokens
    )
    fresh_scores = jnp.where(causal, fresh_scores, NEGATIVE)
    highest = jnp.maximum(
        jnp.max(scores, axis=1, keepdims=True), jnp.max(fresh_scores, axis=1, keepdims=True)
    )
    expo = jnp.where(usable, jnp.exp(scores - highest), 0.0)
    fresh_expo = jnp.where(causal, jnp.exp(fresh_scores - highest), 0.0)
    totals = jnp.sum(expo, axis=1, keepdims=True) + jnp.sum(fresh_expo, axis=1, keepdims=True)
    summed = lax.dot_general(
        expo.astype(jnp.bfloat16), v_view[...], contract, preferred_element_type=jnp.float32
    ) + jnp.dot(fresh_expo.astype(jnp.bfloat16), fv, preferred_element_type=jnp.float32)
    normed = jnp.where(head_lanes, (summed / totals).astype(jnp.bfloat16), 0.0)
    gather = (
        lax.broadcasted_iota(jnp.int32, (tokens, rows), 1) % tokens
        == lax.broadcasted_iota(jnp.int32, (tokens, rows), 0)
    ).astype(jnp.bfloat16)
    return jnp.dot(gather, normed.astype(jnp.bfloat16), preferred_element_type=jnp.float32)


def finish_long(state, q, fk, fv):
    tokens, width = q.shape
    rows = (width // HEAD_DIM) * tokens
    pick = (
        lax.broadcasted_iota(jnp.int32, (rows, tokens), 0) % tokens
        == lax.broadcasted_iota(jnp.int32, (rows, tokens), 1)
    ).astype(jnp.bfloat16)
    head_lanes = (
        lax.broadcasted_iota(jnp.int32, (rows, width), 0) // tokens
        == lax.broadcasted_iota(jnp.int32, (rows, width), 1) // HEAD_DIM
    )
    spread = jnp.dot(pick, q, preferred_element_type=jnp.float32)
    query = jnp.where(head_lanes, spread, 0.0).astype(jnp.bfloat16)
    contract = (((1,), (1,)), ((), ()))
    fresh_scores = lax.dot_general(
        query, fk, contract, preferred_element_type=jnp.float32
    ) * (1.0 / math.sqrt(HEAD_DIM))
    causal = lax.broadcasted_iota(jnp.int32, (rows, tokens), 1) <= (
        lax.broadcasted_iota(jnp.int32, (rows, tokens), 0) % tokens
    )
    fresh_scores = jnp.where(causal, fresh_scores, NEGATIVE)
    top = state[:, HEAD_DIM : HEAD_DIM + 1]
    highest = jnp.maximum(top, jnp.max(fresh_scores, axis=1, keepdims=True))
    kept = jnp.exp(top - highest)
    fresh_expo = jnp.where(causal, jnp.exp(fresh_scores - highest), 0.0)
    totals = state[:, HEAD_DIM + 1 : HEAD_DIM + 2] * kept + jnp.sum(
        fresh_expo, axis=1, keepdims=True
    )
    fresh_sum = jnp.where(
        head_lanes,
        jnp.dot(fresh_expo.astype(jnp.bfloat16), fv, preferred_element_type=jnp.float32),
        0.0,
    )
    folded = fresh_sum[:, 0:HEAD_DIM]
    for g in range(1, width // HEAD_DIM):
        folded = folded + fresh_sum[:, g * HEAD_DIM : (g + 1) * HEAD_DIM]
    normed = ((state[:, :HEAD_DIM] * kept + folded) / totals).astype(jnp.float32)
    spread_back = jnp.concatenate([normed] * (width // HEAD_DIM), axis=1)
    placed = jnp.where(head_lanes, spread_back.astype(jnp.bfloat16), 0.0).astype(jnp.bfloat16)
    gather = (
        lax.broadcasted_iota(jnp.int32, (tokens, rows), 1) % tokens
        == lax.broadcasted_iota(jnp.int32, (tokens, rows), 0)
    ).astype(jnp.bfloat16)
    return jnp.dot(gather, placed, preferred_element_type=jnp.float32)


def long_request(q, k_view, v_view, usable):
    tokens, width = q.shape
    rows = (width // HEAD_DIM) * tokens
    pick = (
        lax.broadcasted_iota(jnp.int32, (rows, tokens), 0) % tokens
        == lax.broadcasted_iota(jnp.int32, (rows, tokens), 1)
    ).astype(jnp.bfloat16)
    head_lanes = (
        lax.broadcasted_iota(jnp.int32, (rows, width), 0) // tokens
        == lax.broadcasted_iota(jnp.int32, (rows, width), 1) // HEAD_DIM
    )
    spread = jnp.dot(pick, q, preferred_element_type=jnp.float32)
    query = jnp.where(head_lanes, spread, 0.0).astype(jnp.bfloat16)
    contract = (((1,), (1,)), ((), ()))
    scores = jnp.dot(query, k_view[...], preferred_element_type=jnp.float32) * (
        1.0 / math.sqrt(HEAD_DIM)
    )
    scores = jnp.where(usable, scores, NEGATIVE)
    highest = jnp.max(scores, axis=1, keepdims=True)
    expo = jnp.where(usable, jnp.exp(scores - highest), 0.0)
    totals = jnp.sum(expo, axis=1, keepdims=True)
    summed = lax.dot_general(
        expo.astype(jnp.bfloat16), v_view[...], contract, preferred_element_type=jnp.float32
    )
    masked = jnp.where(head_lanes, summed, 0.0)
    folded = masked[:, 0:HEAD_DIM]
    for g in range(1, width // HEAD_DIM):
        folded = folded + masked[:, g * HEAD_DIM : (g + 1) * HEAD_DIM]
    return jnp.concatenate(
        [folded, highest, totals, jnp.zeros((rows, LANES - HEAD_DIM - 2), jnp.float32)],
        axis=1,
    )


def butterfly_kernel(
    rounds, len_ref, llen_ref, live_ref, q_ref, f_ref, cache_ref, ql_ref, fl_ref,
    lcache_ref, att_ref, state, recv, send_sem, recv_sem, kv_buf, kv_sem, lkv_buf, lkv_sem,
):
    me = lax.axis_index("seq")
    column = lax.axis_index("tp")
    count, tokens = q_ref.shape[0], q_ref.shape[1]
    long_count = ql_ref.shape[0]
    long_loads = []
    for r in range(long_count):
        pair = []
        for kv in range(2):
            load = pltpu.make_async_copy(
                lcache_ref.at[kv, r], lkv_buf.at[kv, r], lkv_sem.at[kv, r]
            )
            load.start()
            pair.append(load)
        long_loads.append(pair)
    loads = []
    for r in range(count):
        pair = []
        for kv in range(2):
            load = pltpu.make_async_copy(
                cache_ref.at[kv, r], kv_buf.at[kv, r], kv_sem.at[kv, r]
            )
            load.start()
            pair.append(load)
        loads.append(pair)

    def short_step(r):
        for load in loads[r]:
            load.wait()
        spot = lax.broadcasted_iota(jnp.int32, (1, kv_buf.shape[3]), 1)
        att_ref[r * tokens : (r + 1) * tokens] = short_request(
            q_ref[r], kv_buf.at[0, r], kv_buf.at[1, r], spot < len_ref[r],
            f_ref[0, r], f_ref[1, r],
        ).astype(att_ref.dtype)

    partners = []
    for k in range(rounds):
        step = 1 << k
        bit = (me // step) % 2
        partners.append((me + step - 2 * step * bit, bit))
    barrier = pltpu.get_barrier_semaphore()
    for partner, _ in partners:
        pl.semaphore_signal(
            barrier, inc=1, device_id=(partner, column), device_id_type=MESH
        )
    positions = lkv_buf.shape[3]
    spot = lax.broadcasted_iota(jnp.int32, (1, positions), 1)
    blocks = live_ref.shape[0]
    for r in range(long_count):
        alive = spot < 0
        for b in range(blocks):
            alive = alive | (
                (spot // (positions // blocks) == b) & (live_ref[b, r] == 1)
            )
        usable = alive & (spot + me * positions < llen_ref[r])
        for load in long_loads[r]:
            load.wait()
        state[0, r] = long_request(ql_ref[r], lkv_buf.at[0, r], lkv_buf.at[1, r], usable)
    pl.semaphore_wait(barrier, rounds)
    for k in range(rounds):
        partner, bit = partners[k]
        source = state.at[k]
        copy = pltpu.make_async_remote_copy(
            src_ref=source,
            dst_ref=recv.at[k],
            send_sem=send_sem.at[k],
            recv_sem=recv_sem.at[k],
            device_id=(partner, column),
            device_id_type=MESH,
        )
        copy.start()
        if k < count:
            short_step(k)
        copy.wait()
        mine = source[...]
        theirs = recv[k]
        first = bit == 0
        merged = merge_states(
            jnp.where(first, mine, theirs), jnp.where(first, theirs, mine)
        )
        if k == rounds - 1:
            for r in range(ql_ref.shape[0]):
                row = (count + r) * tokens
                att_ref[row : row + tokens] = finish_long(
                    merged[r], ql_ref[r], fl_ref[0, r], fl_ref[1, r]
                ).astype(att_ref.dtype)
        else:
            state[k + 1] = merged
    for r in range(rounds, count):
        short_step(r)


def seq_allreduce(
    devices, lengths, queries, fresh, cache, long_len, live, queries_long, fresh_long, cache_long
):
    rounds = devices.bit_length() - 1
    tokens, width = queries.shape[1], queries.shape[2]
    rows = (width // HEAD_DIM) * tokens
    state_shape = (queries_long.shape[0], rows, LANES)
    flipped = jnp.swapaxes(cache, 2, 3)
    flipped_long = jnp.swapaxes(cache_long, 2, 3)
    vmem = pl.BlockSpec(memory_space=pltpu.VMEM)
    smem = pl.BlockSpec(memory_space=pltpu.SMEM)
    hbm = pl.BlockSpec(memory_space=pl.ANY)
    return pl.pallas_call(
        functools.partial(butterfly_kernel, rounds),
        out_shape=jax.ShapeDtypeStruct(
            ((queries.shape[0] + queries_long.shape[0]) * tokens, width), jnp.bfloat16
        ),
        in_specs=[smem, smem, smem, vmem, vmem, hbm, vmem, vmem, hbm],
        out_specs=vmem,
        scratch_shapes=[
            pltpu.VMEM((rounds,) + state_shape, jnp.float32),
            pltpu.VMEM((rounds,) + state_shape, jnp.float32),
            pltpu.SemaphoreType.DMA((rounds,)),
            pltpu.SemaphoreType.DMA((rounds,)),
            pltpu.VMEM(flipped.shape, flipped.dtype),
            pltpu.SemaphoreType.DMA(flipped.shape[:2]),
            pltpu.VMEM(flipped_long.shape, flipped_long.dtype),
            pltpu.SemaphoreType.DMA(flipped_long.shape[:2]),
        ],
        compiler_params=pltpu.CompilerParams(collective_id=0, has_side_effects=True),
        cost_estimate=pl.CostEstimate(
            flops=4 * rows * (queries.shape[0] * cache.size + queries_long.shape[0] * cache_long.size),
            transcendentals=rows * (cache.size + cache_long.size) // width,
            bytes_accessed=2 * (cache.size + cache_long.size),
        ),
    )(lengths, long_len, live, queries, fresh, flipped, queries_long, fresh_long, flipped_long)


def scatter_kernel(parts, x_ref, o_ref, recv, local_sem, send_sem, recv_sem):
    me = lax.axis_index("tp")
    row = lax.axis_index("seq")
    barrier = pltpu.get_barrier_semaphore()
    for d in range(1, parts):
        pl.semaphore_signal(
            barrier, inc=1, device_id=(row, (me + d) % parts), device_id_type=MESH
        )
    pl.semaphore_wait(barrier, parts - 1)
    own = pltpu.make_async_copy(x_ref.at[me], recv.at[me], local_sem)
    own.start()
    copies = []
    for d in range(1, parts):
        copy = pltpu.make_async_remote_copy(
            src_ref=x_ref.at[(me + d) % parts],
            dst_ref=recv.at[me],
            send_sem=send_sem.at[d - 1],
            recv_sem=recv_sem.at[d - 1],
            device_id=(row, (me + d) % parts),
            device_id_type=MESH,
        )
        copy.start()
        copies.append(copy)
    own.wait()
    for d in range(1, parts):
        copies[d - 1].wait_send()
        pltpu.make_async_remote_copy(
            src_ref=x_ref.at[0],
            dst_ref=recv.at[(me + parts - d) % parts],
            send_sem=send_sem.at[d - 1],
            recv_sem=recv_sem.at[d - 1],
            device_id=(row, (me + parts - d) % parts),
            device_id_type=MESH,
        ).wait_recv()
    total = recv[0]
    for s in range(1, parts):
        total = total + recv[s]
    o_ref[...] = total


def tp_reduce_scatter(term, parts):
    rows, width = term.shape
    cols = width // parts
    blocks = jnp.transpose(term.reshape(rows, parts, cols), (1, 0, 2))
    return pl.pallas_call(
        functools.partial(scatter_kernel, parts),
        out_shape=jax.ShapeDtypeStruct((rows, cols), jnp.float32),
        in_specs=[pl.BlockSpec(memory_space=pltpu.VMEM)],
        out_specs=pl.BlockSpec(memory_space=pltpu.VMEM),
        scratch_shapes=[
            pltpu.VMEM((parts, rows, cols), jnp.float32),
            pltpu.SemaphoreType.DMA(()),
            pltpu.SemaphoreType.DMA((parts - 1,)),
            pltpu.SemaphoreType.DMA((parts - 1,)),
        ],
        compiler_params=pltpu.CompilerParams(collective_id=1, has_side_effects=True),
        cost_estimate=pl.CostEstimate(
            flops=rows * width,
            transcendentals=0,
            bytes_accessed=3 * rows * width * 4,
        ),
    )(blocks)


def attention_kernel(with_fresh, len_ref, live_ref, off_ref, q_ref, k_ref, v_ref, *rest):
    tokens, width = q_ref.shape[1], q_ref.shape[2]
    positions = k_ref.shape[3]
    rows = (width // HEAD_DIM) * tokens
    request = pl.program_id(0)
    spot = lax.broadcasted_iota(jnp.int32, (1, positions), 1)
    usable = spot + off_ref[0] < len_ref[request]
    if not with_fresh:
        blocks = live_ref.shape[0]
        alive = spot < 0
        for b in range(blocks):
            alive = alive | (
                (spot // (positions // blocks) == b) & (live_ref[b, request] == 1)
            )
        usable = usable & alive
    pick = (
        lax.broadcasted_iota(jnp.int32, (rows, tokens), 0) % tokens
        == lax.broadcasted_iota(jnp.int32, (rows, tokens), 1)
    ).astype(jnp.bfloat16)
    head_lanes = (
        lax.broadcasted_iota(jnp.int32, (rows, width), 0) // tokens
        == lax.broadcasted_iota(jnp.int32, (rows, width), 1) // HEAD_DIM
    )
    spread = jnp.dot(pick, q_ref[0], preferred_element_type=jnp.float32)
    query = jnp.where(head_lanes, spread, 0.0).astype(jnp.bfloat16)
    contract = (((1,), (1,)), ((), ()))
    scale = 1.0 / math.sqrt(HEAD_DIM)
    scores = jnp.dot(query, k_ref[0, 0], preferred_element_type=jnp.float32) * scale
    scores = jnp.where(usable, scores, NEGATIVE)
    highest = jnp.max(scores, axis=1, keepdims=True)
    if with_fresh:
        fk_ref, fv_ref, o_ref = rest
        fresh_scores = lax.dot_general(
            query, fk_ref[0, 0], contract, preferred_element_type=jnp.float32
        ) * scale
        causal = lax.broadcasted_iota(jnp.int32, (rows, tokens), 1) <= (
            lax.broadcasted_iota(jnp.int32, (rows, tokens), 0) % tokens
        )
        fresh_scores = jnp.where(causal, fresh_scores, NEGATIVE)
        highest = jnp.maximum(highest, jnp.max(fresh_scores, axis=1, keepdims=True))
    expo = jnp.where(usable, jnp.exp(scores - highest), 0.0)
    totals = jnp.sum(expo, axis=1, keepdims=True)
    summed = lax.dot_general(
        expo.astype(jnp.bfloat16), v_ref[0, 0], contract, preferred_element_type=jnp.float32
    )
    if with_fresh:
        fresh_expo = jnp.where(causal, jnp.exp(fresh_scores - highest), 0.0)
        totals = totals + jnp.sum(fresh_expo, axis=1, keepdims=True)
        summed = summed + jnp.dot(
            fresh_expo.astype(jnp.bfloat16), fv_ref[0, 0], preferred_element_type=jnp.float32
        )
        normed = jnp.where(head_lanes, (summed / totals).astype(jnp.bfloat16), 0.0)
        gather = (
            lax.broadcasted_iota(jnp.int32, (tokens, rows), 1) % tokens
            == lax.broadcasted_iota(jnp.int32, (tokens, rows), 0)
        ).astype(jnp.bfloat16)
        o_ref[0] = jnp.dot(
            gather, normed.astype(jnp.bfloat16), preferred_element_type=jnp.float32
        ).astype(o_ref.dtype)
    else:
        (out_ref,) = rest
        masked = jnp.where(head_lanes, summed, 0.0)
        folded = masked[:, 0:HEAD_DIM]
        for g in range(1, width // HEAD_DIM):
            folded = folded + masked[:, g * HEAD_DIM : (g + 1) * HEAD_DIM]
        out_ref[0] = jnp.concatenate(
            [
                folded,
                highest,
                totals,
                jnp.zeros((rows, LANES - HEAD_DIM - 2), jnp.float32),
            ],
            axis=1,
        )


def attention(queries, cache, lengths, live, offset, fresh=None):
    count, tokens, width = queries.shape
    positions = cache.shape[2]
    rows = (width // HEAD_DIM) * tokens
    flipped = jnp.swapaxes(cache, 2, 3)
    specs = [
        pl.BlockSpec((1, tokens, width), lambda r, *_: (r, 0, 0)),
        pl.BlockSpec((1, 1, width, positions), lambda r, *_: (0, r, 0, 0)),
        pl.BlockSpec((1, 1, width, positions), lambda r, *_: (1, r, 0, 0)),
    ]
    operands = [lengths, live, offset, queries, flipped, flipped]
    if fresh is not None:
        specs += [
            pl.BlockSpec((1, 1, tokens, width), lambda r, *_: (0, r, 0, 0)),
            pl.BlockSpec((1, 1, tokens, width), lambda r, *_: (1, r, 0, 0)),
        ]
        operands += [fresh, fresh]
        out_shape = jax.ShapeDtypeStruct((count, tokens, width), jnp.bfloat16)
        out_specs = pl.BlockSpec((1, tokens, width), lambda r, *_: (r, 0, 0))
    else:
        out_shape = jax.ShapeDtypeStruct((count, rows, LANES), jnp.float32)
        out_specs = pl.BlockSpec((1, rows, LANES), lambda r, *_: (r, 0, 0))
    return pl.pallas_call(
        functools.partial(attention_kernel, fresh is not None),
        out_shape=out_shape,
        grid_spec=pltpu.PrefetchScalarGridSpec(
            num_scalar_prefetch=3, grid=(count,), in_specs=specs, out_specs=out_specs
        ),
        cost_estimate=pl.CostEstimate(
            flops=4 * count * rows * positions * width,
            transcendentals=count * rows * positions,
            bytes_accessed=2 * count * positions * width * 2,
        ),
    )(*operands)


def per_device(
    queries_short,
    cache_short,
    fresh_short,
    short_len,
    queries_long,
    cache_long,
    fresh_long,
    long_len,
    block_live,
    out_weight,
):
    request_count = queries_short.shape[0]
    token_count = queries_short.shape[1]
    both = seq_allreduce(
        lax.axis_size("seq"),
        short_len,
        queries_short,
        fresh_short,
        cache_short,
        long_len,
        block_live.T,
        queries_long,
        fresh_long,
        cache_long,
    )
    short_count = request_count * token_count
    term = jnp.dot(both, out_weight, preferred_element_type=jnp.float32)
    cols = tp_reduce_scatter(term, lax.axis_size("tp")).astype(jnp.bfloat16)
    short_out = cols[:short_count].reshape(request_count, token_count, cols.shape[1])
    long_out = cols[short_count:].reshape(
        queries_long.shape[0], queries_long.shape[1], cols.shape[1]
    )
    return (short_out, long_out)


def solution(mesh):
    in_specs = (
        P("seq", None, "tp"),
        P(None, "seq", None, "tp"),
        P(None, "seq", None, "tp"),
        P("seq"),
        P(None, None, "tp"),
        P(None, None, "seq", "tp"),
        P(None, None, None, "tp"),
        P(),
        P(None, "seq"),
        P("tp", None),
    )
    out_specs = (P("seq", None, "tp"), P(None, None, "tp"))
    return jax.shard_map(
        per_device, mesh=mesh, in_specs=in_specs, out_specs=out_specs, check_vma=False
    )
```

```python
import functools
import math

import jax
import jax.numpy as jnp
from jax import lax
from jax.experimental import pallas as pl
from jax.experimental.pallas import tpu as pltpu
from jax.sharding import PartitionSpec as P

HEAD_DIM = 64
MESH = pl.DeviceIdType.MESH
LANES = 128


NEGATIVE = -1e30


def split_heads(tensor):
    return tensor.reshape(tensor.shape[0], tensor.shape[1], tensor.shape[2] // HEAD_DIM, HEAD_DIM)


def partial_softmax(query_heads, key_heads, value_heads, usable):
    scores = jnp.einsum(
        "rjhd,rphd->rhjp", query_heads, key_heads, preferred_element_type=jnp.float32
    ) * (1.0 / math.sqrt(HEAD_DIM))
    scores = jnp.where(usable, scores, NEGATIVE)
    highest = jnp.max(scores, axis=-1)
    expo = jnp.where(usable, jnp.exp(scores - highest[..., None]), 0.0)
    totals = jnp.sum(expo, axis=-1)
    summed = jnp.einsum(
        "rhjp,rphd->rhjd",
        expo.astype(jnp.bfloat16),
        value_heads,
        preferred_element_type=jnp.float32,
    )
    return (highest, totals, summed)


def combine_parts(first, second):
    highest = jnp.maximum(first[0], second[0])
    scale_first = jnp.exp(first[0] - highest)
    scale_second = jnp.exp(second[0] - highest)
    totals = first[1] * scale_first + second[1] * scale_second
    summed = first[2] * scale_first[..., None] + second[2] * scale_second[..., None]
    return (highest, totals, summed)


def finish(parts):
    normed = (parts[2] / parts[1][..., None]).astype(jnp.bfloat16)
    normed = jnp.transpose(normed, (0, 2, 1, 3))
    return normed.reshape(normed.shape[0], normed.shape[1], normed.shape[2] * normed.shape[3])


def fresh_part(queries, fresh):
    count = queries.shape[1]
    causal = (jnp.arange(count)[:, None] >= jnp.arange(count)[None, :])[None, None]
    return partial_softmax(
        split_heads(queries), split_heads(fresh[0]), split_heads(fresh[1]), causal
    )


def merge_states(low, high):
    lane = lax.broadcasted_iota(jnp.int32, low.shape, low.ndim - 1)
    top_low = low[..., HEAD_DIM : HEAD_DIM + 1]
    top_high = high[..., HEAD_DIM : HEAD_DIM + 1]
    top = jnp.maximum(top_low, top_high)
    mixed = low * jnp.exp(top_low - top) + high * jnp.exp(top_high - top)
    return jnp.where(lane == HEAD_DIM, top, mixed)


def short_request(q, k_view, v_view, usable, fk, fv):
    tokens, width = q.shape
    rows = (width // HEAD_DIM) * tokens
    pick = (
        lax.broadcasted_iota(jnp.int32, (rows, tokens), 0) % tokens
        == lax.broadcasted_iota(jnp.int32, (rows, tokens), 1)
    ).astype(jnp.bfloat16)
    head_lanes = (
        lax.broadcasted_iota(jnp.int32, (rows, width), 0) // tokens
        == lax.broadcasted_iota(jnp.int32, (rows, width), 1) // HEAD_DIM
    )
    spread = jnp.dot(pick, q, preferred_element_type=jnp.float32)
    query = jnp.where(head_lanes, spread, 0.0).astype(jnp.bfloat16)
    contract = (((1,), (1,)), ((), ()))
    scale = 1.0 / math.sqrt(HEAD_DIM)
    scores = jnp.dot(query, k_view[...], preferred_element_type=jnp.float32) * scale
    scores = jnp.where(usable, scores, NEGATIVE)
    fresh_scores = lax.dot_general(query, fk, contract, preferred_element_type=jnp.float32) * scale
    causal = lax.broadcasted_iota(jnp.int32, (rows, tokens), 1) <= (
        lax.broadcasted_iota(jnp.int32, (rows, tokens), 0) % tokens
    )
    fresh_scores = jnp.where(causal, fresh_scores, NEGATIVE)
    highest = jnp.maximum(
        jnp.max(scores, axis=1, keepdims=True), jnp.max(fresh_scores, axis=1, keepdims=True)
    )
    expo = jnp.where(usable, jnp.exp(scores - highest), 0.0)
    fresh_expo = jnp.where(causal, jnp.exp(fresh_scores - highest), 0.0)
    totals = jnp.sum(expo, axis=1, keepdims=True) + jnp.sum(fresh_expo, axis=1, keepdims=True)
    summed = lax.dot_general(
        expo.astype(jnp.bfloat16), v_view[...], contract, preferred_element_type=jnp.float32
    ) + jnp.dot(fresh_expo.astype(jnp.bfloat16), fv, preferred_element_type=jnp.float32)
    normed = jnp.where(head_lanes, (summed / totals).astype(jnp.bfloat16), 0.0)
    gather = (
        lax.broadcasted_iota(jnp.int32, (tokens, rows), 1) % tokens
        == lax.broadcasted_iota(jnp.int32, (tokens, rows), 0)
    ).astype(jnp.bfloat16)
    return jnp.dot(gather, normed.astype(jnp.bfloat16), preferred_element_type=jnp.float32)


def finish_long(state, q, fk, fv):
    tokens, width = q.shape
    rows = (width // HEAD_DIM) * tokens
    pick = (
        lax.broadcasted_iota(jnp.int32, (rows, tokens), 0) % tokens
        == lax.broadcasted_iota(jnp.int32, (rows, tokens), 1)
    ).astype(jnp.bfloat16)
    head_lanes = (
        lax.broadcasted_iota(jnp.int32, (rows, width), 0) // tokens
        == lax.broadcasted_iota(jnp.int32, (rows, width), 1) // HEAD_DIM
    )
    spread = jnp.dot(pick, q, preferred_element_type=jnp.float32)
    query = jnp.where(head_lanes, spread, 0.0).astype(jnp.bfloat16)
    contract = (((1,), (1,)), ((), ()))
    fresh_scores = lax.dot_general(
        query, fk, contract, preferred_element_type=jnp.float32
    ) * (1.0 / math.sqrt(HEAD_DIM))
    causal = lax.broadcasted_iota(jnp.int32, (rows, tokens), 1) <= (
        lax.broadcasted_iota(jnp.int32, (rows, tokens), 0) % tokens
    )
    fresh_scores = jnp.where(causal, fresh_scores, NEGATIVE)
    top = state[:, HEAD_DIM : HEAD_DIM + 1]
    highest = jnp.maximum(top, jnp.max(fresh_scores, axis=1, keepdims=True))
    kept = jnp.exp(top - highest)
    fresh_expo = jnp.where(causal, jnp.exp(fresh_scores - highest), 0.0)
    totals = state[:, HEAD_DIM + 1 : HEAD_DIM + 2] * kept + jnp.sum(
        fresh_expo, axis=1, keepdims=True
    )
    fresh_sum = jnp.where(
        head_lanes,
        jnp.dot(fresh_expo.astype(jnp.bfloat16), fv, preferred_element_type=jnp.float32),
        0.0,
    )
    folded = fresh_sum[:, 0:HEAD_DIM]
    for g in range(1, width // HEAD_DIM):
        folded = folded + fresh_sum[:, g * HEAD_DIM : (g + 1) * HEAD_DIM]
    normed = ((state[:, :HEAD_DIM] * kept + folded) / totals).astype(jnp.float32)
    spread_back = jnp.concatenate([normed] * (width // HEAD_DIM), axis=1)
    placed = jnp.where(head_lanes, spread_back.astype(jnp.bfloat16), 0.0).astype(jnp.bfloat16)
    gather = (
        lax.broadcasted_iota(jnp.int32, (tokens, rows), 1) % tokens
        == lax.broadcasted_iota(jnp.int32, (tokens, rows), 0)
    ).astype(jnp.bfloat16)
    return jnp.dot(gather, placed, preferred_element_type=jnp.float32)


def long_request(q, k_view, v_view, usable):
    tokens, width = q.shape
    rows = (width // HEAD_DIM) * tokens
    pick = (
        lax.broadcasted_iota(jnp.int32, (rows, tokens), 0) % tokens
        == lax.broadcasted_iota(jnp.int32, (rows, tokens), 1)
    ).astype(jnp.bfloat16)
    head_lanes = (
        lax.broadcasted_iota(jnp.int32, (rows, width), 0) // tokens
        == lax.broadcasted_iota(jnp.int32, (rows, width), 1) // HEAD_DIM
    )
    spread = jnp.dot(pick, q, preferred_element_type=jnp.float32)
    query = jnp.where(head_lanes, spread, 0.0).astype(jnp.bfloat16)
    contract = (((1,), (1,)), ((), ()))
    scores = jnp.dot(query, k_view[...], preferred_element_type=jnp.float32) * (
        1.0 / math.sqrt(HEAD_DIM)
    )
    scores = jnp.where(usable, scores, NEGATIVE)
    highest = jnp.max(scores, axis=1, keepdims=True)
    expo = jnp.where(usable, jnp.exp(scores - highest), 0.0)
    totals = jnp.sum(expo, axis=1, keepdims=True)
    summed = lax.dot_general(
        expo.astype(jnp.bfloat16), v_view[...], contract, preferred_element_type=jnp.float32
    )
    masked = jnp.where(head_lanes, summed, 0.0)
    folded = masked[:, 0:HEAD_DIM]
    for g in range(1, width // HEAD_DIM):
        folded = folded + masked[:, g * HEAD_DIM : (g + 1) * HEAD_DIM]
    return jnp.concatenate(
        [folded, highest, totals, jnp.zeros((rows, LANES - HEAD_DIM - 2), jnp.float32)],
        axis=1,
    )


def butterfly_kernel(
    rounds, parts, len_ref, llen_ref, live_ref, q_ref, f_ref, cache_ref, ql_ref, fl_ref,
    lcache_ref, w_ref, out_ref, att_ref, state, recv, send_sem, recv_sem, kv_buf, kv_sem, lkv_buf, lkv_sem,
):
    me = lax.axis_index("seq")
    column = lax.axis_index("tp")
    count, tokens = q_ref.shape[0], q_ref.shape[1]
    long_count = ql_ref.shape[0]
    long_loads = []
    for r in range(long_count):
        pair = []
        for kv in range(2):
            load = pltpu.make_async_copy(
                lcache_ref.at[kv, r], lkv_buf.at[kv, r], lkv_sem.at[kv, r]
            )
            load.start()
            pair.append(load)
        long_loads.append(pair)
    loads = []
    for r in range(count):
        pair = []
        for kv in range(2):
            load = pltpu.make_async_copy(
                cache_ref.at[kv, r], kv_buf.at[kv, r], kv_sem.at[kv, r]
            )
            load.start()
            pair.append(load)
        loads.append(pair)

    def short_step(r):
        for load in loads[r]:
            load.wait()
        spot = lax.broadcasted_iota(jnp.int32, (1, kv_buf.shape[3]), 1)
        att_ref[r * tokens : (r + 1) * tokens] = short_request(
            q_ref[r], kv_buf.at[0, r], kv_buf.at[1, r], spot < len_ref[r],
            f_ref[0, r], f_ref[1, r],
        ).astype(att_ref.dtype)

    partners = []
    for k in range(rounds):
        step = 1 << k
        bit = (me // step) % 2
        partners.append((me + step - 2 * step * bit, bit))
    barrier = pltpu.get_barrier_semaphore()
    for partner, _ in partners:
        pl.semaphore_signal(
            barrier, inc=1, device_id=(partner, column), device_id_type=MESH
        )
    positions = lkv_buf.shape[3]
    spot = lax.broadcasted_iota(jnp.int32, (1, positions), 1)
    blocks = live_ref.shape[0]
    for r in range(long_count):
        alive = spot < 0
        for b in range(blocks):
            alive = alive | (
                (spot // (positions // blocks) == b) & (live_ref[b, r] == 1)
            )
        usable = alive & (spot + me * positions < llen_ref[r])
        for load in long_loads[r]:
            load.wait()
        state[0, r] = long_request(ql_ref[r], lkv_buf.at[0, r], lkv_buf.at[1, r], usable)
    pl.semaphore_wait(barrier, rounds)
    for k in range(rounds):
        partner, bit = partners[k]
        source = state.at[k]
        copy = pltpu.make_async_remote_copy(
            src_ref=source,
            dst_ref=recv.at[k],
            send_sem=send_sem.at[k],
            recv_sem=recv_sem.at[k],
            device_id=(partner, column),
            device_id_type=MESH,
        )
        copy.start()
        if k < count:
            short_step(k)
        copy.wait()
        mine = source[...]
        theirs = recv[k]
        first = bit == 0
        merged = merge_states(
            jnp.where(first, mine, theirs), jnp.where(first, theirs, mine)
        )
        if k == rounds - 1:
            for r in range(ql_ref.shape[0]):
                row = (count + r) * tokens
                att_ref[row : row + tokens] = finish_long(
                    merged[r], ql_ref[r], fl_ref[0, r], fl_ref[1, r]
                ).astype(att_ref.dtype)
        else:
            state[k + 1] = merged
    for r in range(rounds, count):
        short_step(r)
    term = jnp.dot(att_ref[...], w_ref[...], preferred_element_type=jnp.float32)
    cols = w_ref.shape[1] // parts
    for q in range(parts):
        out_ref[q] = term[:, q * cols : (q + 1) * cols]


def seq_allreduce(
    devices, lengths, queries, fresh, cache, long_len, live, queries_long, fresh_long, cache_long,
    weight, parts,
):
    rounds = devices.bit_length() - 1
    tokens, width = queries.shape[1], queries.shape[2]
    rows = (width // HEAD_DIM) * tokens
    state_shape = (queries_long.shape[0], rows, LANES)
    flipped = jnp.swapaxes(cache, 2, 3)
    flipped_long = jnp.swapaxes(cache_long, 2, 3)
    vmem = pl.BlockSpec(memory_space=pltpu.VMEM)
    smem = pl.BlockSpec(memory_space=pltpu.SMEM)
    hbm = pl.BlockSpec(memory_space=pl.ANY)
    return pl.pallas_call(
        functools.partial(butterfly_kernel, rounds, parts),
        out_shape=jax.ShapeDtypeStruct(
            (parts, (queries.shape[0] + queries_long.shape[0]) * tokens, weight.shape[1] // parts),
            jnp.float32,
        ),
        in_specs=[smem, smem, smem, vmem, vmem, hbm, vmem, vmem, hbm, vmem],
        out_specs=vmem,
        scratch_shapes=[
            pltpu.VMEM(((queries.shape[0] + queries_long.shape[0]) * tokens, width), jnp.bfloat16),
            pltpu.VMEM((rounds,) + state_shape, jnp.float32),
            pltpu.VMEM((rounds,) + state_shape, jnp.float32),
            pltpu.SemaphoreType.DMA((rounds,)),
            pltpu.SemaphoreType.DMA((rounds,)),
            pltpu.VMEM(flipped.shape, flipped.dtype),
            pltpu.SemaphoreType.DMA(flipped.shape[:2]),
            pltpu.VMEM(flipped_long.shape, flipped_long.dtype),
            pltpu.SemaphoreType.DMA(flipped_long.shape[:2]),
        ],
        compiler_params=pltpu.CompilerParams(collective_id=0, has_side_effects=True),
        cost_estimate=pl.CostEstimate(
            flops=4 * rows * (queries.shape[0] * cache.size + queries_long.shape[0] * cache_long.size),
            transcendentals=rows * (cache.size + cache_long.size) // width,
            bytes_accessed=2 * (cache.size + cache_long.size),
        ),
    )(lengths, long_len, live, queries, fresh, flipped, queries_long, fresh_long, flipped_long, weight)


def scatter_kernel(parts, x_ref, o_ref, recv, local_sem, send_sem, recv_sem):
    me = lax.axis_index("tp")
    row = lax.axis_index("seq")
    barrier = pltpu.get_barrier_semaphore()
    for d in range(1, parts):
        pl.semaphore_signal(
            barrier, inc=1, device_id=(row, (me + d) % parts), device_id_type=MESH
        )
    pl.semaphore_wait(barrier, parts - 1)
    own = pltpu.make_async_copy(x_ref.at[me], recv.at[me], local_sem)
    own.start()
    copies = []
    for d in range(1, parts):
        copy = pltpu.make_async_remote_copy(
            src_ref=x_ref.at[(me + d) % parts],
            dst_ref=recv.at[me],
            send_sem=send_sem.at[d - 1],
            recv_sem=recv_sem.at[d - 1],
            device_id=(row, (me + d) % parts),
            device_id_type=MESH,
        )
        copy.start()
        copies.append(copy)
    own.wait()
    for d in range(1, parts):
        copies[d - 1].wait_send()
        pltpu.make_async_remote_copy(
            src_ref=x_ref.at[0],
            dst_ref=recv.at[(me + parts - d) % parts],
            send_sem=send_sem.at[d - 1],
            recv_sem=recv_sem.at[d - 1],
            device_id=(row, (me + parts - d) % parts),
            device_id_type=MESH,
        ).wait_recv()
    total = recv[0]
    for s in range(1, parts):
        total = total + recv[s]
    o_ref[...] = total


def tp_reduce_scatter(blocks):
    parts, rows, cols = blocks.shape
    return pl.pallas_call(
        functools.partial(scatter_kernel, parts),
        out_shape=jax.ShapeDtypeStruct((rows, cols), jnp.float32),
        in_specs=[pl.BlockSpec(memory_space=pltpu.VMEM)],
        out_specs=pl.BlockSpec(memory_space=pltpu.VMEM),
        scratch_shapes=[
            pltpu.VMEM((parts, rows, cols), jnp.float32),
            pltpu.SemaphoreType.DMA(()),
            pltpu.SemaphoreType.DMA((parts - 1,)),
            pltpu.SemaphoreType.DMA((parts - 1,)),
        ],
        compiler_params=pltpu.CompilerParams(collective_id=1, has_side_effects=True),
        cost_estimate=pl.CostEstimate(
            flops=rows * cols * parts,
            transcendentals=0,
            bytes_accessed=3 * rows * cols * parts * 4,
        ),
    )(blocks)


def attention_kernel(with_fresh, len_ref, live_ref, off_ref, q_ref, k_ref, v_ref, *rest):
    tokens, width = q_ref.shape[1], q_ref.shape[2]
    positions = k_ref.shape[3]
    rows = (width // HEAD_DIM) * tokens
    request = pl.program_id(0)
    spot = lax.broadcasted_iota(jnp.int32, (1, positions), 1)
    usable = spot + off_ref[0] < len_ref[request]
    if not with_fresh:
        blocks = live_ref.shape[0]
        alive = spot < 0
        for b in range(blocks):
            alive = alive | (
                (spot // (positions // blocks) == b) & (live_ref[b, request] == 1)
            )
        usable = usable & alive
    pick = (
        lax.broadcasted_iota(jnp.int32, (rows, tokens), 0) % tokens
        == lax.broadcasted_iota(jnp.int32, (rows, tokens), 1)
    ).astype(jnp.bfloat16)
    head_lanes = (
        lax.broadcasted_iota(jnp.int32, (rows, width), 0) // tokens
        == lax.broadcasted_iota(jnp.int32, (rows, width), 1) // HEAD_DIM
    )
    spread = jnp.dot(pick, q_ref[0], preferred_element_type=jnp.float32)
    query = jnp.where(head_lanes, spread, 0.0).astype(jnp.bfloat16)
    contract = (((1,), (1,)), ((), ()))
    scale = 1.0 / math.sqrt(HEAD_DIM)
    scores = jnp.dot(query, k_ref[0, 0], preferred_element_type=jnp.float32) * scale
    scores = jnp.where(usable, scores, NEGATIVE)
    highest = jnp.max(scores, axis=1, keepdims=True)
    if with_fresh:
        fk_ref, fv_ref, o_ref = rest
        fresh_scores = lax.dot_general(
            query, fk_ref[0, 0], contract, preferred_element_type=jnp.float32
        ) * scale
        causal = lax.broadcasted_iota(jnp.int32, (rows, tokens), 1) <= (
            lax.broadcasted_iota(jnp.int32, (rows, tokens), 0) % tokens
        )
        fresh_scores = jnp.where(causal, fresh_scores, NEGATIVE)
        highest = jnp.maximum(highest, jnp.max(fresh_scores, axis=1, keepdims=True))
    expo = jnp.where(usable, jnp.exp(scores - highest), 0.0)
    totals = jnp.sum(expo, axis=1, keepdims=True)
    summed = lax.dot_general(
        expo.astype(jnp.bfloat16), v_ref[0, 0], contract, preferred_element_type=jnp.float32
    )
    if with_fresh:
        fresh_expo = jnp.where(causal, jnp.exp(fresh_scores - highest), 0.0)
        totals = totals + jnp.sum(fresh_expo, axis=1, keepdims=True)
        summed = summed + jnp.dot(
            fresh_expo.astype(jnp.bfloat16), fv_ref[0, 0], preferred_element_type=jnp.float32
        )
        normed = jnp.where(head_lanes, (summed / totals).astype(jnp.bfloat16), 0.0)
        gather = (
            lax.broadcasted_iota(jnp.int32, (tokens, rows), 1) % tokens
            == lax.broadcasted_iota(jnp.int32, (tokens, rows), 0)
        ).astype(jnp.bfloat16)
        o_ref[0] = jnp.dot(
            gather, normed.astype(jnp.bfloat16), preferred_element_type=jnp.float32
        ).astype(o_ref.dtype)
    else:
        (out_ref,) = rest
        masked = jnp.where(head_lanes, summed, 0.0)
        folded = masked[:, 0:HEAD_DIM]
        for g in range(1, width // HEAD_DIM):
            folded = folded + masked[:, g * HEAD_DIM : (g + 1) * HEAD_DIM]
        out_ref[0] = jnp.concatenate(
            [
                folded,
                highest,
                totals,
                jnp.zeros((rows, LANES - HEAD_DIM - 2), jnp.float32),
            ],
            axis=1,
        )


def attention(queries, cache, lengths, live, offset, fresh=None):
    count, tokens, width = queries.shape
    positions = cache.shape[2]
    rows = (width // HEAD_DIM) * tokens
    flipped = jnp.swapaxes(cache, 2, 3)
    specs = [
        pl.BlockSpec((1, tokens, width), lambda r, *_: (r, 0, 0)),
        pl.BlockSpec((1, 1, width, positions), lambda r, *_: (0, r, 0, 0)),
        pl.BlockSpec((1, 1, width, positions), lambda r, *_: (1, r, 0, 0)),
    ]
    operands = [lengths, live, offset, queries, flipped, flipped]
    if fresh is not None:
        specs += [
            pl.BlockSpec((1, 1, tokens, width), lambda r, *_: (0, r, 0, 0)),
            pl.BlockSpec((1, 1, tokens, width), lambda r, *_: (1, r, 0, 0)),
        ]
        operands += [fresh, fresh]
        out_shape = jax.ShapeDtypeStruct((count, tokens, width), jnp.bfloat16)
        out_specs = pl.BlockSpec((1, tokens, width), lambda r, *_: (r, 0, 0))
    else:
        out_shape = jax.ShapeDtypeStruct((count, rows, LANES), jnp.float32)
        out_specs = pl.BlockSpec((1, rows, LANES), lambda r, *_: (r, 0, 0))
    return pl.pallas_call(
        functools.partial(attention_kernel, fresh is not None),
        out_shape=out_shape,
        grid_spec=pltpu.PrefetchScalarGridSpec(
            num_scalar_prefetch=3, grid=(count,), in_specs=specs, out_specs=out_specs
        ),
        cost_estimate=pl.CostEstimate(
            flops=4 * count * rows * positions * width,
            transcendentals=count * rows * positions,
            bytes_accessed=2 * count * positions * width * 2,
        ),
    )(*operands)


def per_device(
    queries_short,
    cache_short,
    fresh_short,
    short_len,
    queries_long,
    cache_long,
    fresh_long,
    long_len,
    block_live,
    out_weight,
):
    request_count = queries_short.shape[0]
    token_count = queries_short.shape[1]
    blocks = seq_allreduce(
        lax.axis_size("seq"),
        short_len,
        queries_short,
        fresh_short,
        cache_short,
        long_len,
        block_live.T,
        queries_long,
        fresh_long,
        cache_long,
        out_weight,
        lax.axis_size("tp"),
    )
    short_count = request_count * token_count
    cols = tp_reduce_scatter(blocks).astype(jnp.bfloat16)
    short_out = cols[:short_count].reshape(request_count, token_count, cols.shape[1])
    long_out = cols[short_count:].reshape(
        queries_long.shape[0], queries_long.shape[1], cols.shape[1]
    )
    return (short_out, long_out)


def solution(mesh):
    in_specs = (
        P("seq", None, "tp"),
        P(None, "seq", None, "tp"),
        P(None, "seq", None, "tp"),
        P("seq"),
        P(None, None, "tp"),
        P(None, None, "seq", "tp"),
        P(None, None, None, "tp"),
        P(),
        P(None, "seq"),
        P("tp", None),
    )
    out_specs = (P("seq", None, "tp"), P(None, None, "tp"))
    return jax.shard_map(
        per_device, mesh=mesh, in_specs=in_specs, out_specs=out_specs, check_vma=False
    )
```

```python
import functools
import math

import jax
import jax.numpy as jnp
from jax import lax
from jax.experimental import pallas as pl
from jax.experimental.pallas import tpu as pltpu
from jax.sharding import PartitionSpec as P

HEAD_DIM = 64
MESH = pl.DeviceIdType.MESH
LANES = 128


NEGATIVE = -1e30


def split_heads(tensor):
    return tensor.reshape(tensor.shape[0], tensor.shape[1], tensor.shape[2] // HEAD_DIM, HEAD_DIM)


def partial_softmax(query_heads, key_heads, value_heads, usable):
    scores = jnp.einsum(
        "rjhd,rphd->rhjp", query_heads, key_heads, preferred_element_type=jnp.float32
    ) * (1.0 / math.sqrt(HEAD_DIM))
    scores = jnp.where(usable, scores, NEGATIVE)
    highest = jnp.max(scores, axis=-1)
    expo = jnp.where(usable, jnp.exp(scores - highest[..., None]), 0.0)
    totals = jnp.sum(expo, axis=-1)
    summed = jnp.einsum(
        "rhjp,rphd->rhjd",
        expo.astype(jnp.bfloat16),
        value_heads,
        preferred_element_type=jnp.float32,
    )
    return (highest, totals, summed)


def combine_parts(first, second):
    highest = jnp.maximum(first[0], second[0])
    scale_first = jnp.exp(first[0] - highest)
    scale_second = jnp.exp(second[0] - highest)
    totals = first[1] * scale_first + second[1] * scale_second
    summed = first[2] * scale_first[..., None] + second[2] * scale_second[..., None]
    return (highest, totals, summed)


def finish(parts):
    normed = (parts[2] / parts[1][..., None]).astype(jnp.bfloat16)
    normed = jnp.transpose(normed, (0, 2, 1, 3))
    return normed.reshape(normed.shape[0], normed.shape[1], normed.shape[2] * normed.shape[3])


def fresh_part(queries, fresh):
    count = queries.shape[1]
    causal = (jnp.arange(count)[:, None] >= jnp.arange(count)[None, :])[None, None]
    return partial_softmax(
        split_heads(queries), split_heads(fresh[0]), split_heads(fresh[1]), causal
    )


def merge_states(low, high):
    lane = lax.broadcasted_iota(jnp.int32, low.shape, low.ndim - 1)
    top_low = low[..., HEAD_DIM : HEAD_DIM + 1]
    top_high = high[..., HEAD_DIM : HEAD_DIM + 1]
    top = jnp.maximum(top_low, top_high)
    mixed = low * jnp.exp(top_low - top) + high * jnp.exp(top_high - top)
    return jnp.where(lane == HEAD_DIM, top, mixed)


def short_request(q, k_view, v_view, usable, fk, fv):
    tokens, width = q.shape
    rows = (width // HEAD_DIM) * tokens
    pick = (
        lax.broadcasted_iota(jnp.int32, (rows, tokens), 0) % tokens
        == lax.broadcasted_iota(jnp.int32, (rows, tokens), 1)
    ).astype(jnp.bfloat16)
    head_lanes = (
        lax.broadcasted_iota(jnp.int32, (rows, width), 0) // tokens
        == lax.broadcasted_iota(jnp.int32, (rows, width), 1) // HEAD_DIM
    )
    spread = jnp.dot(pick, q, preferred_element_type=jnp.float32)
    query = jnp.where(head_lanes, spread, 0.0).astype(jnp.bfloat16)
    contract = (((1,), (1,)), ((), ()))
    scale = 1.0 / math.sqrt(HEAD_DIM)
    scores = jnp.dot(query, k_view[...], preferred_element_type=jnp.float32) * scale
    scores = jnp.where(usable, scores, NEGATIVE)
    fresh_scores = lax.dot_general(query, fk, contract, preferred_element_type=jnp.float32) * scale
    causal = lax.broadcasted_iota(jnp.int32, (rows, tokens), 1) <= (
        lax.broadcasted_iota(jnp.int32, (rows, tokens), 0) % tokens
    )
    fresh_scores = jnp.where(causal, fresh_scores, NEGATIVE)
    highest = jnp.maximum(
        jnp.max(scores, axis=1, keepdims=True), jnp.max(fresh_scores, axis=1, keepdims=True)
    )
    expo = jnp.where(usable, jnp.exp(scores - highest), 0.0)
    fresh_expo = jnp.where(causal, jnp.exp(fresh_scores - highest), 0.0)
    totals = jnp.sum(expo, axis=1, keepdims=True) + jnp.sum(fresh_expo, axis=1, keepdims=True)
    summed = lax.dot_general(
        expo.astype(jnp.bfloat16), v_view[...], contract, preferred_element_type=jnp.float32
    ) + jnp.dot(fresh_expo.astype(jnp.bfloat16), fv, preferred_element_type=jnp.float32)
    normed = jnp.where(head_lanes, (summed / totals).astype(jnp.bfloat16), 0.0)
    gather = (
        lax.broadcasted_iota(jnp.int32, (tokens, rows), 1) % tokens
        == lax.broadcasted_iota(jnp.int32, (tokens, rows), 0)
    ).astype(jnp.bfloat16)
    return jnp.dot(gather, normed.astype(jnp.bfloat16), preferred_element_type=jnp.float32)


def finish_long(state, q, fk, fv):
    tokens, width = q.shape
    rows = (width // HEAD_DIM) * tokens
    pick = (
        lax.broadcasted_iota(jnp.int32, (rows, tokens), 0) % tokens
        == lax.broadcasted_iota(jnp.int32, (rows, tokens), 1)
    ).astype(jnp.bfloat16)
    head_lanes = (
        lax.broadcasted_iota(jnp.int32, (rows, width), 0) // tokens
        == lax.broadcasted_iota(jnp.int32, (rows, width), 1) // HEAD_DIM
    )
    spread = jnp.dot(pick, q, preferred_element_type=jnp.float32)
    query = jnp.where(head_lanes, spread, 0.0).astype(jnp.bfloat16)
    contract = (((1,), (1,)), ((), ()))
    fresh_scores = lax.dot_general(
        query, fk, contract, preferred_element_type=jnp.float32
    ) * (1.0 / math.sqrt(HEAD_DIM))
    causal = lax.broadcasted_iota(jnp.int32, (rows, tokens), 1) <= (
        lax.broadcasted_iota(jnp.int32, (rows, tokens), 0) % tokens
    )
    fresh_scores = jnp.where(causal, fresh_scores, NEGATIVE)
    top = state[:, HEAD_DIM : HEAD_DIM + 1]
    highest = jnp.maximum(top, jnp.max(fresh_scores, axis=1, keepdims=True))
    kept = jnp.exp(top - highest)
    fresh_expo = jnp.where(causal, jnp.exp(fresh_scores - highest), 0.0)
    totals = state[:, HEAD_DIM + 1 : HEAD_DIM + 2] * kept + jnp.sum(
        fresh_expo, axis=1, keepdims=True
    )
    fresh_sum = jnp.where(
        head_lanes,
        jnp.dot(fresh_expo.astype(jnp.bfloat16), fv, preferred_element_type=jnp.float32),
        0.0,
    )
    folded = fresh_sum[:, 0:HEAD_DIM]
    for g in range(1, width // HEAD_DIM):
        folded = folded + fresh_sum[:, g * HEAD_DIM : (g + 1) * HEAD_DIM]
    normed = ((state[:, :HEAD_DIM] * kept + folded) / totals).astype(jnp.float32)
    spread_back = jnp.concatenate([normed] * (width // HEAD_DIM), axis=1)
    placed = jnp.where(head_lanes, spread_back.astype(jnp.bfloat16), 0.0).astype(jnp.bfloat16)
    gather = (
        lax.broadcasted_iota(jnp.int32, (tokens, rows), 1) % tokens
        == lax.broadcasted_iota(jnp.int32, (tokens, rows), 0)
    ).astype(jnp.bfloat16)
    return jnp.dot(gather, placed, preferred_element_type=jnp.float32)


def long_request(q, k_view, v_view, usable):
    tokens, width = q.shape
    rows = (width // HEAD_DIM) * tokens
    pick = (
        lax.broadcasted_iota(jnp.int32, (rows, tokens), 0) % tokens
        == lax.broadcasted_iota(jnp.int32, (rows, tokens), 1)
    ).astype(jnp.bfloat16)
    head_lanes = (
        lax.broadcasted_iota(jnp.int32, (rows, width), 0) // tokens
        == lax.broadcasted_iota(jnp.int32, (rows, width), 1) // HEAD_DIM
    )
    spread = jnp.dot(pick, q, preferred_element_type=jnp.float32)
    query = jnp.where(head_lanes, spread, 0.0).astype(jnp.bfloat16)
    contract = (((1,), (1,)), ((), ()))
    scores = jnp.dot(query, k_view[...], preferred_element_type=jnp.float32) * (
        1.0 / math.sqrt(HEAD_DIM)
    )
    scores = jnp.where(usable, scores, NEGATIVE)
    highest = jnp.max(scores, axis=1, keepdims=True)
    expo = jnp.where(usable, jnp.exp(scores - highest), 0.0)
    totals = jnp.sum(expo, axis=1, keepdims=True)
    summed = lax.dot_general(
        expo.astype(jnp.bfloat16), v_view[...], contract, preferred_element_type=jnp.float32
    )
    masked = jnp.where(head_lanes, summed, 0.0)
    folded = masked[:, 0:HEAD_DIM]
    for g in range(1, width // HEAD_DIM):
        folded = folded + masked[:, g * HEAD_DIM : (g + 1) * HEAD_DIM]
    return jnp.concatenate(
        [folded, highest, totals, jnp.zeros((rows, LANES - HEAD_DIM - 2), jnp.float32)],
        axis=1,
    )


def butterfly_kernel(
    rounds, parts, len_ref, llen_ref, live_ref, q_ref, f_ref, cache_ref, ql_ref, fl_ref,
    lcache_ref, w_ref, out_ref, att_ref, state, recv, send_sem, recv_sem, kv_buf, kv_sem, lkv_buf, lkv_sem,
    blk, tp_recv, tp_local, tp_send, tp_sem,
):
    me = lax.axis_index("seq")
    column = lax.axis_index("tp")
    count, tokens = q_ref.shape[0], q_ref.shape[1]
    long_count = ql_ref.shape[0]
    long_loads = []
    for r in range(long_count):
        pair = []
        for kv in range(2):
            load = pltpu.make_async_copy(
                lcache_ref.at[kv, r], lkv_buf.at[kv, r], lkv_sem.at[kv, r]
            )
            load.start()
            pair.append(load)
        long_loads.append(pair)
    loads = []
    for r in range(count):
        pair = []
        for kv in range(2):
            load = pltpu.make_async_copy(
                cache_ref.at[kv, r], kv_buf.at[kv, r], kv_sem.at[kv, r]
            )
            load.start()
            pair.append(load)
        loads.append(pair)

    def short_step(r):
        for load in loads[r]:
            load.wait()
        spot = lax.broadcasted_iota(jnp.int32, (1, kv_buf.shape[3]), 1)
        att_ref[r * tokens : (r + 1) * tokens] = short_request(
            q_ref[r], kv_buf.at[0, r], kv_buf.at[1, r], spot < len_ref[r],
            f_ref[0, r], f_ref[1, r],
        ).astype(att_ref.dtype)

    partners = []
    for k in range(rounds):
        step = 1 << k
        bit = (me // step) % 2
        partners.append((me + step - 2 * step * bit, bit))
    barrier = pltpu.get_barrier_semaphore()
    for partner, _ in partners:
        pl.semaphore_signal(
            barrier, inc=1, device_id=(partner, column), device_id_type=MESH
        )
    for d in range(1, parts):
        pl.semaphore_signal(
            barrier, inc=1, device_id=(me, (column + d) % parts), device_id_type=MESH
        )
    positions = lkv_buf.shape[3]
    spot = lax.broadcasted_iota(jnp.int32, (1, positions), 1)
    blocks = live_ref.shape[0]
    for r in range(long_count):
        alive = spot < 0
        for b in range(blocks):
            alive = alive | (
                (spot // (positions // blocks) == b) & (live_ref[b, r] == 1)
            )
        usable = alive & (spot + me * positions < llen_ref[r])
        for load in long_loads[r]:
            load.wait()
        state[0, r] = long_request(ql_ref[r], lkv_buf.at[0, r], lkv_buf.at[1, r], usable)
    pl.semaphore_wait(barrier, rounds + parts - 1)
    for k in range(rounds):
        partner, bit = partners[k]
        source = state.at[k]
        copy = pltpu.make_async_remote_copy(
            src_ref=source,
            dst_ref=recv.at[k],
            send_sem=send_sem.at[k],
            recv_sem=recv_sem.at[k],
            device_id=(partner, column),
            device_id_type=MESH,
        )
        copy.start()
        if k < count:
            short_step(k)
        copy.wait()
        mine = source[...]
        theirs = recv[k]
        first = bit == 0
        merged = merge_states(
            jnp.where(first, mine, theirs), jnp.where(first, theirs, mine)
        )
        if k == rounds - 1:
            for r in range(ql_ref.shape[0]):
                row = (count + r) * tokens
                att_ref[row : row + tokens] = finish_long(
                    merged[r], ql_ref[r], fl_ref[0, r], fl_ref[1, r]
                ).astype(att_ref.dtype)
        else:
            state[k + 1] = merged
    for r in range(rounds, count):
        short_step(r)
    term = jnp.dot(att_ref[...], w_ref[...], preferred_element_type=jnp.float32)
    cols = w_ref.shape[1] // parts
    for q in range(parts):
        blk[q] = term[:, q * cols : (q + 1) * cols]
    own = pltpu.make_async_copy(blk.at[column], tp_recv.at[column], tp_local)
    own.start()
    sends = []
    for d in range(1, parts):
        send = pltpu.make_async_remote_copy(
            src_ref=blk.at[(column + d) % parts],
            dst_ref=tp_recv.at[column],
            send_sem=tp_send.at[d - 1],
            recv_sem=tp_sem.at[d - 1],
            device_id=(me, (column + d) % parts),
            device_id_type=MESH,
        )
        send.start()
        sends.append(send)
    own.wait()
    for d in range(1, parts):
        sends[d - 1].wait_send()
        pltpu.make_async_remote_copy(
            src_ref=blk.at[0],
            dst_ref=tp_recv.at[(column + parts - d) % parts],
            send_sem=tp_send.at[d - 1],
            recv_sem=tp_sem.at[d - 1],
            device_id=(me, (column + parts - d) % parts),
            device_id_type=MESH,
        ).wait_recv()
    total = tp_recv[0]
    for s in range(1, parts):
        total = total + tp_recv[s]
    out_ref[...] = total


def seq_allreduce(
    devices, lengths, queries, fresh, cache, long_len, live, queries_long, fresh_long, cache_long,
    weight, parts,
):
    rounds = devices.bit_length() - 1
    tokens, width = queries.shape[1], queries.shape[2]
    rows = (width // HEAD_DIM) * tokens
    state_shape = (queries_long.shape[0], rows, LANES)
    block_shape = (
        parts,
        (queries.shape[0] + queries_long.shape[0]) * tokens,
        weight.shape[1] // parts,
    )
    flipped = jnp.swapaxes(cache, 2, 3)
    flipped_long = jnp.swapaxes(cache_long, 2, 3)
    vmem = pl.BlockSpec(memory_space=pltpu.VMEM)
    smem = pl.BlockSpec(memory_space=pltpu.SMEM)
    hbm = pl.BlockSpec(memory_space=pl.ANY)
    return pl.pallas_call(
        functools.partial(butterfly_kernel, rounds, parts),
        out_shape=jax.ShapeDtypeStruct(
            ((queries.shape[0] + queries_long.shape[0]) * tokens, weight.shape[1] // parts),
            jnp.float32,
        ),
        in_specs=[smem, smem, smem, vmem, vmem, hbm, vmem, vmem, hbm, vmem],
        out_specs=vmem,
        scratch_shapes=[
            pltpu.VMEM(((queries.shape[0] + queries_long.shape[0]) * tokens, width), jnp.bfloat16),
            pltpu.VMEM((rounds,) + state_shape, jnp.float32),
            pltpu.VMEM((rounds,) + state_shape, jnp.float32),
            pltpu.SemaphoreType.DMA((rounds,)),
            pltpu.SemaphoreType.DMA((rounds,)),
            pltpu.VMEM(flipped.shape, flipped.dtype),
            pltpu.SemaphoreType.DMA(flipped.shape[:2]),
            pltpu.VMEM(flipped_long.shape, flipped_long.dtype),
            pltpu.SemaphoreType.DMA(flipped_long.shape[:2]),
            pltpu.VMEM(block_shape, jnp.float32),
            pltpu.VMEM(block_shape, jnp.float32),
            pltpu.SemaphoreType.DMA(()),
            pltpu.SemaphoreType.DMA((parts - 1,)),
            pltpu.SemaphoreType.DMA((parts - 1,)),
        ],
        compiler_params=pltpu.CompilerParams(collective_id=0, has_side_effects=True),
        cost_estimate=pl.CostEstimate(
            flops=4 * rows * (queries.shape[0] * cache.size + queries_long.shape[0] * cache_long.size),
            transcendentals=rows * (cache.size + cache_long.size) // width,
            bytes_accessed=2 * (cache.size + cache_long.size),
        ),
    )(lengths, long_len, live, queries, fresh, flipped, queries_long, fresh_long, flipped_long, weight)


def scatter_kernel(parts, x_ref, o_ref, recv, local_sem, send_sem, recv_sem):
    me = lax.axis_index("tp")
    row = lax.axis_index("seq")
    barrier = pltpu.get_barrier_semaphore()
    for d in range(1, parts):
        pl.semaphore_signal(
            barrier, inc=1, device_id=(row, (me + d) % parts), device_id_type=MESH
        )
    pl.semaphore_wait(barrier, parts - 1)
    own = pltpu.make_async_copy(x_ref.at[me], recv.at[me], local_sem)
    own.start()
    copies = []
    for d in range(1, parts):
        copy = pltpu.make_async_remote_copy(
            src_ref=x_ref.at[(me + d) % parts],
            dst_ref=recv.at[me],
            send_sem=send_sem.at[d - 1],
            recv_sem=recv_sem.at[d - 1],
            device_id=(row, (me + d) % parts),
            device_id_type=MESH,
        )
        copy.start()
        copies.append(copy)
    own.wait()
    for d in range(1, parts):
        copies[d - 1].wait_send()
        pltpu.make_async_remote_copy(
            src_ref=x_ref.at[0],
            dst_ref=recv.at[(me + parts - d) % parts],
            send_sem=send_sem.at[d - 1],
            recv_sem=recv_sem.at[d - 1],
            device_id=(row, (me + parts - d) % parts),
            device_id_type=MESH,
        ).wait_recv()
    total = recv[0]
    for s in range(1, parts):
        total = total + recv[s]
    o_ref[...] = total


def tp_reduce_scatter(blocks):
    parts, rows, cols = blocks.shape
    return pl.pallas_call(
        functools.partial(scatter_kernel, parts),
        out_shape=jax.ShapeDtypeStruct((rows, cols), jnp.float32),
        in_specs=[pl.BlockSpec(memory_space=pltpu.VMEM)],
        out_specs=pl.BlockSpec(memory_space=pltpu.VMEM),
        scratch_shapes=[
            pltpu.VMEM((parts, rows, cols), jnp.float32),
            pltpu.SemaphoreType.DMA(()),
            pltpu.SemaphoreType.DMA((parts - 1,)),
            pltpu.SemaphoreType.DMA((parts - 1,)),
        ],
        compiler_params=pltpu.CompilerParams(collective_id=1, has_side_effects=True),
        cost_estimate=pl.CostEstimate(
            flops=rows * cols * parts,
            transcendentals=0,
            bytes_accessed=3 * rows * cols * parts * 4,
        ),
    )(blocks)


def attention_kernel(with_fresh, len_ref, live_ref, off_ref, q_ref, k_ref, v_ref, *rest):
    tokens, width = q_ref.shape[1], q_ref.shape[2]
    positions = k_ref.shape[3]
    rows = (width // HEAD_DIM) * tokens
    request = pl.program_id(0)
    spot = lax.broadcasted_iota(jnp.int32, (1, positions), 1)
    usable = spot + off_ref[0] < len_ref[request]
    if not with_fresh:
        blocks = live_ref.shape[0]
        alive = spot < 0
        for b in range(blocks):
            alive = alive | (
                (spot // (positions // blocks) == b) & (live_ref[b, request] == 1)
            )
        usable = usable & alive
    pick = (
        lax.broadcasted_iota(jnp.int32, (rows, tokens), 0) % tokens
        == lax.broadcasted_iota(jnp.int32, (rows, tokens), 1)
    ).astype(jnp.bfloat16)
    head_lanes = (
        lax.broadcasted_iota(jnp.int32, (rows, width), 0) // tokens
        == lax.broadcasted_iota(jnp.int32, (rows, width), 1) // HEAD_DIM
    )
    spread = jnp.dot(pick, q_ref[0], preferred_element_type=jnp.float32)
    query = jnp.where(head_lanes, spread, 0.0).astype(jnp.bfloat16)
    contract = (((1,), (1,)), ((), ()))
    scale = 1.0 / math.sqrt(HEAD_DIM)
    scores = jnp.dot(query, k_ref[0, 0], preferred_element_type=jnp.float32) * scale
    scores = jnp.where(usable, scores, NEGATIVE)
    highest = jnp.max(scores, axis=1, keepdims=True)
    if with_fresh:
        fk_ref, fv_ref, o_ref = rest
        fresh_scores = lax.dot_general(
            query, fk_ref[0, 0], contract, preferred_element_type=jnp.float32
        ) * scale
        causal = lax.broadcasted_iota(jnp.int32, (rows, tokens), 1) <= (
            lax.broadcasted_iota(jnp.int32, (rows, tokens), 0) % tokens
        )
        fresh_scores = jnp.where(causal, fresh_scores, NEGATIVE)
        highest = jnp.maximum(highest, jnp.max(fresh_scores, axis=1, keepdims=True))
    expo = jnp.where(usable, jnp.exp(scores - highest), 0.0)
    totals = jnp.sum(expo, axis=1, keepdims=True)
    summed = lax.dot_general(
        expo.astype(jnp.bfloat16), v_ref[0, 0], contract, preferred_element_type=jnp.float32
    )
    if with_fresh:
        fresh_expo = jnp.where(causal, jnp.exp(fresh_scores - highest), 0.0)
        totals = totals + jnp.sum(fresh_expo, axis=1, keepdims=True)
        summed = summed + jnp.dot(
            fresh_expo.astype(jnp.bfloat16), fv_ref[0, 0], preferred_element_type=jnp.float32
        )
        normed = jnp.where(head_lanes, (summed / totals).astype(jnp.bfloat16), 0.0)
        gather = (
            lax.broadcasted_iota(jnp.int32, (tokens, rows), 1) % tokens
            == lax.broadcasted_iota(jnp.int32, (tokens, rows), 0)
        ).astype(jnp.bfloat16)
        o_ref[0] = jnp.dot(
            gather, normed.astype(jnp.bfloat16), preferred_element_type=jnp.float32
        ).astype(o_ref.dtype)
    else:
        (out_ref,) = rest
        masked = jnp.where(head_lanes, summed, 0.0)
        folded = masked[:, 0:HEAD_DIM]
        for g in range(1, width // HEAD_DIM):
            folded = folded + masked[:, g * HEAD_DIM : (g + 1) * HEAD_DIM]
        out_ref[0] = jnp.concatenate(
            [
                folded,
                highest,
                totals,
                jnp.zeros((rows, LANES - HEAD_DIM - 2), jnp.float32),
            ],
            axis=1,
        )


def attention(queries, cache, lengths, live, offset, fresh=None):
    count, tokens, width = queries.shape
    positions = cache.shape[2]
    rows = (width // HEAD_DIM) * tokens
    flipped = jnp.swapaxes(cache, 2, 3)
    specs = [
        pl.BlockSpec((1, tokens, width), lambda r, *_: (r, 0, 0)),
        pl.BlockSpec((1, 1, width, positions), lambda r, *_: (0, r, 0, 0)),
        pl.BlockSpec((1, 1, width, positions), lambda r, *_: (1, r, 0, 0)),
    ]
    operands = [lengths, live, offset, queries, flipped, flipped]
    if fresh is not None:
        specs += [
            pl.BlockSpec((1, 1, tokens, width), lambda r, *_: (0, r, 0, 0)),
            pl.BlockSpec((1, 1, tokens, width), lambda r, *_: (1, r, 0, 0)),
        ]
        operands += [fresh, fresh]
        out_shape = jax.ShapeDtypeStruct((count, tokens, width), jnp.bfloat16)
        out_specs = pl.BlockSpec((1, tokens, width), lambda r, *_: (r, 0, 0))
    else:
        out_shape = jax.ShapeDtypeStruct((count, rows, LANES), jnp.float32)
        out_specs = pl.BlockSpec((1, rows, LANES), lambda r, *_: (r, 0, 0))
    return pl.pallas_call(
        functools.partial(attention_kernel, fresh is not None),
        out_shape=out_shape,
        grid_spec=pltpu.PrefetchScalarGridSpec(
            num_scalar_prefetch=3, grid=(count,), in_specs=specs, out_specs=out_specs
        ),
        cost_estimate=pl.CostEstimate(
            flops=4 * count * rows * positions * width,
            transcendentals=count * rows * positions,
            bytes_accessed=2 * count * positions * width * 2,
        ),
    )(*operands)


def per_device(
    queries_short,
    cache_short,
    fresh_short,
    short_len,
    queries_long,
    cache_long,
    fresh_long,
    long_len,
    block_live,
    out_weight,
):
    request_count = queries_short.shape[0]
    token_count = queries_short.shape[1]
    blocks = seq_allreduce(
        lax.axis_size("seq"),
        short_len,
        queries_short,
        fresh_short,
        cache_short,
        long_len,
        block_live.T,
        queries_long,
        fresh_long,
        cache_long,
        out_weight,
        lax.axis_size("tp"),
    )
    short_count = request_count * token_count
    cols = blocks.astype(jnp.bfloat16)
    short_out = cols[:short_count].reshape(request_count, token_count, cols.shape[1])
    long_out = cols[short_count:].reshape(
        queries_long.shape[0], queries_long.shape[1], cols.shape[1]
    )
    return (short_out, long_out)


def solution(mesh):
    in_specs = (
        P("seq", None, "tp"),
        P(None, "seq", None, "tp"),
        P(None, "seq", None, "tp"),
        P("seq"),
        P(None, None, "tp"),
        P(None, None, "seq", "tp"),
        P(None, None, None, "tp"),
        P(),
        P(None, "seq"),
        P("tp", None),
    )
    out_specs = (P("seq", None, "tp"), P(None, None, "tp"))
    return jax.shard_map(
        per_device, mesh=mesh, in_specs=in_specs, out_specs=out_specs, check_vma=False
    )
```

```python
import functools
import math

import jax
import jax.numpy as jnp
from jax import lax
from jax.experimental import pallas as pl
from jax.experimental.pallas import tpu as pltpu
from jax.sharding import PartitionSpec as P

HEAD_DIM = 64
MESH = pl.DeviceIdType.MESH
LANES = 128


NEGATIVE = -1e30


def split_heads(tensor):
    return tensor.reshape(tensor.shape[0], tensor.shape[1], tensor.shape[2] // HEAD_DIM, HEAD_DIM)


def partial_softmax(query_heads, key_heads, value_heads, usable):
    scores = jnp.einsum(
        "rjhd,rphd->rhjp", query_heads, key_heads, preferred_element_type=jnp.float32
    ) * (1.0 / math.sqrt(HEAD_DIM))
    scores = jnp.where(usable, scores, NEGATIVE)
    highest = jnp.max(scores, axis=-1)
    expo = jnp.where(usable, jnp.exp(scores - highest[..., None]), 0.0)
    totals = jnp.sum(expo, axis=-1)
    summed = jnp.einsum(
        "rhjp,rphd->rhjd",
        expo.astype(jnp.bfloat16),
        value_heads,
        preferred_element_type=jnp.float32,
    )
    return (highest, totals, summed)


def combine_parts(first, second):
    highest = jnp.maximum(first[0], second[0])
    scale_first = jnp.exp(first[0] - highest)
    scale_second = jnp.exp(second[0] - highest)
    totals = first[1] * scale_first + second[1] * scale_second
    summed = first[2] * scale_first[..., None] + second[2] * scale_second[..., None]
    return (highest, totals, summed)


def finish(parts):
    normed = (parts[2] / parts[1][..., None]).astype(jnp.bfloat16)
    normed = jnp.transpose(normed, (0, 2, 1, 3))
    return normed.reshape(normed.shape[0], normed.shape[1], normed.shape[2] * normed.shape[3])


def fresh_part(queries, fresh):
    count = queries.shape[1]
    causal = (jnp.arange(count)[:, None] >= jnp.arange(count)[None, :])[None, None]
    return partial_softmax(
        split_heads(queries), split_heads(fresh[0]), split_heads(fresh[1]), causal
    )


def merge_states(low, high):
    lane = lax.broadcasted_iota(jnp.int32, low.shape, low.ndim - 1)
    top_low = low[..., HEAD_DIM : HEAD_DIM + 1]
    top_high = high[..., HEAD_DIM : HEAD_DIM + 1]
    top = jnp.maximum(top_low, top_high)
    mixed = low * jnp.exp(top_low - top) + high * jnp.exp(top_high - top)
    return jnp.where(lane == HEAD_DIM, top, mixed)


def short_request(q, k_view, v_view, usable, fk, fv):
    tokens, width = q.shape
    rows = (width // HEAD_DIM) * tokens
    pick = (
        lax.broadcasted_iota(jnp.int32, (rows, tokens), 0) % tokens
        == lax.broadcasted_iota(jnp.int32, (rows, tokens), 1)
    ).astype(jnp.bfloat16)
    head_lanes = (
        lax.broadcasted_iota(jnp.int32, (rows, width), 0) // tokens
        == lax.broadcasted_iota(jnp.int32, (rows, width), 1) // HEAD_DIM
    )
    spread = jnp.dot(pick, q, preferred_element_type=jnp.float32)
    query = jnp.where(head_lanes, spread, 0.0).astype(jnp.bfloat16)
    contract = (((1,), (1,)), ((), ()))
    scale = 1.0 / math.sqrt(HEAD_DIM)
    scores = jnp.dot(query, k_view[...], preferred_element_type=jnp.float32) * scale
    scores = jnp.where(usable, scores, NEGATIVE)
    fresh_scores = lax.dot_general(query, fk, contract, preferred_element_type=jnp.float32) * scale
    causal = lax.broadcasted_iota(jnp.int32, (rows, tokens), 1) <= (
        lax.broadcasted_iota(jnp.int32, (rows, tokens), 0) % tokens
    )
    fresh_scores = jnp.where(causal, fresh_scores, NEGATIVE)
    highest = jnp.maximum(
        jnp.max(scores, axis=1, keepdims=True), jnp.max(fresh_scores, axis=1, keepdims=True)
    )
    expo = jnp.where(usable, jnp.exp(scores - highest), 0.0)
    fresh_expo = jnp.where(causal, jnp.exp(fresh_scores - highest), 0.0)
    totals = jnp.sum(expo, axis=1, keepdims=True) + jnp.sum(fresh_expo, axis=1, keepdims=True)
    summed = lax.dot_general(
        expo.astype(jnp.bfloat16), v_view[...], contract, preferred_element_type=jnp.float32
    ) + jnp.dot(fresh_expo.astype(jnp.bfloat16), fv, preferred_element_type=jnp.float32)
    normed = jnp.where(head_lanes, (summed / totals).astype(jnp.bfloat16), 0.0)
    gather = (
        lax.broadcasted_iota(jnp.int32, (tokens, rows), 1) % tokens
        == lax.broadcasted_iota(jnp.int32, (tokens, rows), 0)
    ).astype(jnp.bfloat16)
    return jnp.dot(gather, normed.astype(jnp.bfloat16), preferred_element_type=jnp.float32)


def finish_long(state, q, fk, fv):
    tokens, width = q.shape
    rows = (width // HEAD_DIM) * tokens
    pick = (
        lax.broadcasted_iota(jnp.int32, (rows, tokens), 0) % tokens
        == lax.broadcasted_iota(jnp.int32, (rows, tokens), 1)
    ).astype(jnp.bfloat16)
    head_lanes = (
        lax.broadcasted_iota(jnp.int32, (rows, width), 0) // tokens
        == lax.broadcasted_iota(jnp.int32, (rows, width), 1) // HEAD_DIM
    )
    spread = jnp.dot(pick, q, preferred_element_type=jnp.float32)
    query = jnp.where(head_lanes, spread, 0.0).astype(jnp.bfloat16)
    contract = (((1,), (1,)), ((), ()))
    fresh_scores = lax.dot_general(
        query, fk, contract, preferred_element_type=jnp.float32
    ) * (1.0 / math.sqrt(HEAD_DIM))
    causal = lax.broadcasted_iota(jnp.int32, (rows, tokens), 1) <= (
        lax.broadcasted_iota(jnp.int32, (rows, tokens), 0) % tokens
    )
    fresh_scores = jnp.where(causal, fresh_scores, NEGATIVE)
    top = state[:, HEAD_DIM : HEAD_DIM + 1]
    highest = jnp.maximum(top, jnp.max(fresh_scores, axis=1, keepdims=True))
    kept = jnp.exp(top - highest)
    fresh_expo = jnp.where(causal, jnp.exp(fresh_scores - highest), 0.0)
    totals = state[:, HEAD_DIM + 1 : HEAD_DIM + 2] * kept + jnp.sum(
        fresh_expo, axis=1, keepdims=True
    )
    fresh_sum = jnp.where(
        head_lanes,
        jnp.dot(fresh_expo.astype(jnp.bfloat16), fv, preferred_element_type=jnp.float32),
        0.0,
    )
    folded = fresh_sum[:, 0:HEAD_DIM]
    for g in range(1, width // HEAD_DIM):
        folded = folded + fresh_sum[:, g * HEAD_DIM : (g + 1) * HEAD_DIM]
    normed = ((state[:, :HEAD_DIM] * kept + folded) / totals).astype(jnp.float32)
    spread_back = jnp.concatenate([normed] * (width // HEAD_DIM), axis=1)
    placed = jnp.where(head_lanes, spread_back.astype(jnp.bfloat16), 0.0).astype(jnp.bfloat16)
    gather = (
        lax.broadcasted_iota(jnp.int32, (tokens, rows), 1) % tokens
        == lax.broadcasted_iota(jnp.int32, (tokens, rows), 0)
    ).astype(jnp.bfloat16)
    return jnp.dot(gather, placed, preferred_element_type=jnp.float32)


def long_request(q, k_view, v_view, usable):
    tokens, width = q.shape
    rows = (width // HEAD_DIM) * tokens
    pick = (
        lax.broadcasted_iota(jnp.int32, (rows, tokens), 0) % tokens
        == lax.broadcasted_iota(jnp.int32, (rows, tokens), 1)
    ).astype(jnp.bfloat16)
    head_lanes = (
        lax.broadcasted_iota(jnp.int32, (rows, width), 0) // tokens
        == lax.broadcasted_iota(jnp.int32, (rows, width), 1) // HEAD_DIM
    )
    spread = jnp.dot(pick, q, preferred_element_type=jnp.float32)
    query = jnp.where(head_lanes, spread, 0.0).astype(jnp.bfloat16)
    contract = (((1,), (1,)), ((), ()))
    scores = jnp.dot(query, k_view[...], preferred_element_type=jnp.float32) * (
        1.0 / math.sqrt(HEAD_DIM)
    )
    scores = jnp.where(usable, scores, NEGATIVE)
    highest = jnp.max(scores, axis=1, keepdims=True)
    expo = jnp.where(usable, jnp.exp(scores - highest), 0.0)
    totals = jnp.sum(expo, axis=1, keepdims=True)
    summed = lax.dot_general(
        expo.astype(jnp.bfloat16), v_view[...], contract, preferred_element_type=jnp.float32
    )
    masked = jnp.where(head_lanes, summed, 0.0)
    folded = masked[:, 0:HEAD_DIM]
    for g in range(1, width // HEAD_DIM):
        folded = folded + masked[:, g * HEAD_DIM : (g + 1) * HEAD_DIM]
    return jnp.concatenate(
        [folded, highest, totals, jnp.zeros((rows, LANES - HEAD_DIM - 2), jnp.float32)],
        axis=1,
    )


def butterfly_kernel(
    rounds, parts, len_ref, llen_ref, live_ref, q_ref, f_ref, cache_ref, ql_ref, fl_ref,
    lcache_ref, w_ref, out_ref, att_ref, state, recv, send_sem, recv_sem, kv_buf, kv_sem, lkv_buf, lkv_sem,
    blk, tp_recv, tp_local, tp_send, tp_sem,
):
    me = lax.axis_index("seq")
    column = lax.axis_index("tp")
    count, tokens = q_ref.shape[0], q_ref.shape[1]
    long_count = ql_ref.shape[0]
    long_loads = []
    for r in range(long_count):
        pair = []
        for kv in range(2):
            load = pltpu.make_async_copy(
                lcache_ref.at[kv, r], lkv_buf.at[kv, r], lkv_sem.at[kv, r]
            )
            load.start()
            pair.append(load)
        long_loads.append(pair)
    loads = []
    for r in range(count):
        pair = []
        for kv in range(2):
            load = pltpu.make_async_copy(
                cache_ref.at[kv, r], kv_buf.at[kv, r], kv_sem.at[kv, r]
            )
            load.start()
            pair.append(load)
        loads.append(pair)

    def short_step(r):
        for load in loads[r]:
            load.wait()
        spot = lax.broadcasted_iota(jnp.int32, (1, kv_buf.shape[3]), 1)
        att_ref[r * tokens : (r + 1) * tokens] = short_request(
            q_ref[r], kv_buf.at[0, r], kv_buf.at[1, r], spot < len_ref[r],
            f_ref[0, r], f_ref[1, r],
        ).astype(att_ref.dtype)

    partners = []
    for k in range(rounds):
        step = 1 << k
        bit = (me // step) % 2
        partners.append((me + step - 2 * step * bit, bit))
    barrier = pltpu.get_barrier_semaphore()
    for partner, _ in partners:
        pl.semaphore_signal(
            barrier, inc=1, device_id=(partner, column), device_id_type=MESH
        )
    for d in range(1, parts):
        pl.semaphore_signal(
            barrier, inc=1, device_id=(me, (column + d) % parts), device_id_type=MESH
        )
    positions = lkv_buf.shape[3]
    spot = lax.broadcasted_iota(jnp.int32, (1, positions), 1)
    blocks = live_ref.shape[0]
    for r in range(long_count):
        alive = spot < 0
        for b in range(blocks):
            alive = alive | (
                (spot // (positions // blocks) == b) & (live_ref[b, r] == 1)
            )
        usable = alive & (spot + me * positions < llen_ref[r])
        for load in long_loads[r]:
            load.wait()
        state[0, r] = long_request(ql_ref[r], lkv_buf.at[0, r], lkv_buf.at[1, r], usable)
    pl.semaphore_wait(barrier, rounds + parts - 1)
    for k in range(rounds):
        partner, bit = partners[k]
        source = state.at[k]
        copy = pltpu.make_async_remote_copy(
            src_ref=source,
            dst_ref=recv.at[k],
            send_sem=send_sem.at[k],
            recv_sem=recv_sem.at[k],
            device_id=(partner, column),
            device_id_type=MESH,
        )
        copy.start()
        if k < count:
            short_step(k)
        copy.wait()
        mine = source[...]
        theirs = recv[k]
        first = bit == 0
        merged = merge_states(
            jnp.where(first, mine, theirs), jnp.where(first, theirs, mine)
        )
        if k == rounds - 1:
            for r in range(ql_ref.shape[0]):
                row = (count + r) * tokens
                att_ref[row : row + tokens] = finish_long(
                    merged[r], ql_ref[r], fl_ref[0, r], fl_ref[1, r]
                ).astype(att_ref.dtype)
        else:
            state[k + 1] = merged
    for r in range(rounds, count):
        short_step(r)
    term = jnp.dot(att_ref[...], w_ref[...], preferred_element_type=jnp.float32)
    cols = w_ref.shape[1] // parts
    for q in range(parts):
        blk[q] = term[:, q * cols : (q + 1) * cols]
    own = pltpu.make_async_copy(blk.at[column], tp_recv.at[column], tp_local)
    own.start()
    sends = []
    for d in range(1, parts):
        send = pltpu.make_async_remote_copy(
            src_ref=blk.at[(column + d) % parts],
            dst_ref=tp_recv.at[column],
            send_sem=tp_send.at[d - 1],
            recv_sem=tp_sem.at[d - 1],
            device_id=(me, (column + d) % parts),
            device_id_type=MESH,
        )
        send.start()
        sends.append(send)
    own.wait()
    for d in range(1, parts):
        sends[d - 1].wait_send()
        pltpu.make_async_remote_copy(
            src_ref=blk.at[0],
            dst_ref=tp_recv.at[(column + parts - d) % parts],
            send_sem=tp_send.at[d - 1],
            recv_sem=tp_sem.at[d - 1],
            device_id=(me, (column + parts - d) % parts),
            device_id_type=MESH,
        ).wait_recv()
    total = tp_recv[0]
    for s in range(1, parts):
        total = total + tp_recv[s]
    out_ref[...] = total.astype(out_ref.dtype)


def seq_allreduce(
    devices, lengths, queries, fresh, cache, long_len, live, queries_long, fresh_long, cache_long,
    weight, parts,
):
    rounds = devices.bit_length() - 1
    tokens, width = queries.shape[1], queries.shape[2]
    rows = (width // HEAD_DIM) * tokens
    state_shape = (queries_long.shape[0], rows, LANES)
    block_shape = (
        parts,
        (queries.shape[0] + queries_long.shape[0]) * tokens,
        weight.shape[1] // parts,
    )
    flipped = jnp.swapaxes(cache, 2, 3)
    flipped_long = jnp.swapaxes(cache_long, 2, 3)
    vmem = pl.BlockSpec(memory_space=pltpu.VMEM)
    smem = pl.BlockSpec(memory_space=pltpu.SMEM)
    hbm = pl.BlockSpec(memory_space=pl.ANY)
    return pl.pallas_call(
        functools.partial(butterfly_kernel, rounds, parts),
        out_shape=jax.ShapeDtypeStruct(
            ((queries.shape[0] + queries_long.shape[0]) * tokens, weight.shape[1] // parts),
            jnp.bfloat16,
        ),
        in_specs=[smem, smem, smem, vmem, vmem, hbm, vmem, vmem, hbm, vmem],
        out_specs=vmem,
        scratch_shapes=[
            pltpu.VMEM(((queries.shape[0] + queries_long.shape[0]) * tokens, width), jnp.bfloat16),
            pltpu.VMEM((rounds,) + state_shape, jnp.float32),
            pltpu.VMEM((rounds,) + state_shape, jnp.float32),
            pltpu.SemaphoreType.DMA((rounds,)),
            pltpu.SemaphoreType.DMA((rounds,)),
            pltpu.VMEM(flipped.shape, flipped.dtype),
            pltpu.SemaphoreType.DMA(flipped.shape[:2]),
            pltpu.VMEM(flipped_long.shape, flipped_long.dtype),
            pltpu.SemaphoreType.DMA(flipped_long.shape[:2]),
            pltpu.VMEM(block_shape, jnp.float32),
            pltpu.VMEM(block_shape, jnp.float32),
            pltpu.SemaphoreType.DMA(()),
            pltpu.SemaphoreType.DMA((parts - 1,)),
            pltpu.SemaphoreType.DMA((parts - 1,)),
        ],
        compiler_params=pltpu.CompilerParams(collective_id=0, has_side_effects=True),
        cost_estimate=pl.CostEstimate(
            flops=4 * rows * (queries.shape[0] * cache.size + queries_long.shape[0] * cache_long.size),
            transcendentals=rows * (cache.size + cache_long.size) // width,
            bytes_accessed=2 * (cache.size + cache_long.size),
        ),
    )(lengths, long_len, live, queries, fresh, flipped, queries_long, fresh_long, flipped_long, weight)


def scatter_kernel(parts, x_ref, o_ref, recv, local_sem, send_sem, recv_sem):
    me = lax.axis_index("tp")
    row = lax.axis_index("seq")
    barrier = pltpu.get_barrier_semaphore()
    for d in range(1, parts):
        pl.semaphore_signal(
            barrier, inc=1, device_id=(row, (me + d) % parts), device_id_type=MESH
        )
    pl.semaphore_wait(barrier, parts - 1)
    own = pltpu.make_async_copy(x_ref.at[me], recv.at[me], local_sem)
    own.start()
    copies = []
    for d in range(1, parts):
        copy = pltpu.make_async_remote_copy(
            src_ref=x_ref.at[(me + d) % parts],
            dst_ref=recv.at[me],
            send_sem=send_sem.at[d - 1],
            recv_sem=recv_sem.at[d - 1],
            device_id=(row, (me + d) % parts),
            device_id_type=MESH,
        )
        copy.start()
        copies.append(copy)
    own.wait()
    for d in range(1, parts):
        copies[d - 1].wait_send()
        pltpu.make_async_remote_copy(
            src_ref=x_ref.at[0],
            dst_ref=recv.at[(me + parts - d) % parts],
            send_sem=send_sem.at[d - 1],
            recv_sem=recv_sem.at[d - 1],
            device_id=(row, (me + parts - d) % parts),
            device_id_type=MESH,
        ).wait_recv()
    total = recv[0]
    for s in range(1, parts):
        total = total + recv[s]
    o_ref[...] = total


def tp_reduce_scatter(blocks):
    parts, rows, cols = blocks.shape
    return pl.pallas_call(
        functools.partial(scatter_kernel, parts),
        out_shape=jax.ShapeDtypeStruct((rows, cols), jnp.float32),
        in_specs=[pl.BlockSpec(memory_space=pltpu.VMEM)],
        out_specs=pl.BlockSpec(memory_space=pltpu.VMEM),
        scratch_shapes=[
            pltpu.VMEM((parts, rows, cols), jnp.float32),
            pltpu.SemaphoreType.DMA(()),
            pltpu.SemaphoreType.DMA((parts - 1,)),
            pltpu.SemaphoreType.DMA((parts - 1,)),
        ],
        compiler_params=pltpu.CompilerParams(collective_id=1, has_side_effects=True),
        cost_estimate=pl.CostEstimate(
            flops=rows * cols * parts,
            transcendentals=0,
            bytes_accessed=3 * rows * cols * parts * 4,
        ),
    )(blocks)


def attention_kernel(with_fresh, len_ref, live_ref, off_ref, q_ref, k_ref, v_ref, *rest):
    tokens, width = q_ref.shape[1], q_ref.shape[2]
    positions = k_ref.shape[3]
    rows = (width // HEAD_DIM) * tokens
    request = pl.program_id(0)
    spot = lax.broadcasted_iota(jnp.int32, (1, positions), 1)
    usable = spot + off_ref[0] < len_ref[request]
    if not with_fresh:
        blocks = live_ref.shape[0]
        alive = spot < 0
        for b in range(blocks):
            alive = alive | (
                (spot // (positions // blocks) == b) & (live_ref[b, request] == 1)
            )
        usable = usable & alive
    pick = (
        lax.broadcasted_iota(jnp.int32, (rows, tokens), 0) % tokens
        == lax.broadcasted_iota(jnp.int32, (rows, tokens), 1)
    ).astype(jnp.bfloat16)
    head_lanes = (
        lax.broadcasted_iota(jnp.int32, (rows, width), 0) // tokens
        == lax.broadcasted_iota(jnp.int32, (rows, width), 1) // HEAD_DIM
    )
    spread = jnp.dot(pick, q_ref[0], preferred_element_type=jnp.float32)
    query = jnp.where(head_lanes, spread, 0.0).astype(jnp.bfloat16)
    contract = (((1,), (1,)), ((), ()))
    scale = 1.0 / math.sqrt(HEAD_DIM)
    scores = jnp.dot(query, k_ref[0, 0], preferred_element_type=jnp.float32) * scale
    scores = jnp.where(usable, scores, NEGATIVE)
    highest = jnp.max(scores, axis=1, keepdims=True)
    if with_fresh:
        fk_ref, fv_ref, o_ref = rest
        fresh_scores = lax.dot_general(
            query, fk_ref[0, 0], contract, preferred_element_type=jnp.float32
        ) * scale
        causal = lax.broadcasted_iota(jnp.int32, (rows, tokens), 1) <= (
            lax.broadcasted_iota(jnp.int32, (rows, tokens), 0) % tokens
        )
        fresh_scores = jnp.where(causal, fresh_scores, NEGATIVE)
        highest = jnp.maximum(highest, jnp.max(fresh_scores, axis=1, keepdims=True))
    expo = jnp.where(usable, jnp.exp(scores - highest), 0.0)
    totals = jnp.sum(expo, axis=1, keepdims=True)
    summed = lax.dot_general(
        expo.astype(jnp.bfloat16), v_ref[0, 0], contract, preferred_element_type=jnp.float32
    )
    if with_fresh:
        fresh_expo = jnp.where(causal, jnp.exp(fresh_scores - highest), 0.0)
        totals = totals + jnp.sum(fresh_expo, axis=1, keepdims=True)
        summed = summed + jnp.dot(
            fresh_expo.astype(jnp.bfloat16), fv_ref[0, 0], preferred_element_type=jnp.float32
        )
        normed = jnp.where(head_lanes, (summed / totals).astype(jnp.bfloat16), 0.0)
        gather = (
            lax.broadcasted_iota(jnp.int32, (tokens, rows), 1) % tokens
            == lax.broadcasted_iota(jnp.int32, (tokens, rows), 0)
        ).astype(jnp.bfloat16)
        o_ref[0] = jnp.dot(
            gather, normed.astype(jnp.bfloat16), preferred_element_type=jnp.float32
        ).astype(o_ref.dtype)
    else:
        (out_ref,) = rest
        masked = jnp.where(head_lanes, summed, 0.0)
        folded = masked[:, 0:HEAD_DIM]
        for g in range(1, width // HEAD_DIM):
            folded = folded + masked[:, g * HEAD_DIM : (g + 1) * HEAD_DIM]
        out_ref[0] = jnp.concatenate(
            [
                folded,
                highest,
                totals,
                jnp.zeros((rows, LANES - HEAD_DIM - 2), jnp.float32),
            ],
            axis=1,
        )


def attention(queries, cache, lengths, live, offset, fresh=None):
    count, tokens, width = queries.shape
    positions = cache.shape[2]
    rows = (width // HEAD_DIM) * tokens
    flipped = jnp.swapaxes(cache, 2, 3)
    specs = [
        pl.BlockSpec((1, tokens, width), lambda r, *_: (r, 0, 0)),
        pl.BlockSpec((1, 1, width, positions), lambda r, *_: (0, r, 0, 0)),
        pl.BlockSpec((1, 1, width, positions), lambda r, *_: (1, r, 0, 0)),
    ]
    operands = [lengths, live, offset, queries, flipped, flipped]
    if fresh is not None:
        specs += [
            pl.BlockSpec((1, 1, tokens, width), lambda r, *_: (0, r, 0, 0)),
            pl.BlockSpec((1, 1, tokens, width), lambda r, *_: (1, r, 0, 0)),
        ]
        operands += [fresh, fresh]
        out_shape = jax.ShapeDtypeStruct((count, tokens, width), jnp.bfloat16)
        out_specs = pl.BlockSpec((1, tokens, width), lambda r, *_: (r, 0, 0))
    else:
        out_shape = jax.ShapeDtypeStruct((count, rows, LANES), jnp.float32)
        out_specs = pl.BlockSpec((1, rows, LANES), lambda r, *_: (r, 0, 0))
    return pl.pallas_call(
        functools.partial(attention_kernel, fresh is not None),
        out_shape=out_shape,
        grid_spec=pltpu.PrefetchScalarGridSpec(
            num_scalar_prefetch=3, grid=(count,), in_specs=specs, out_specs=out_specs
        ),
        cost_estimate=pl.CostEstimate(
            flops=4 * count * rows * positions * width,
            transcendentals=count * rows * positions,
            bytes_accessed=2 * count * positions * width * 2,
        ),
    )(*operands)


def per_device(
    queries_short,
    cache_short,
    fresh_short,
    short_len,
    queries_long,
    cache_long,
    fresh_long,
    long_len,
    block_live,
    out_weight,
):
    request_count = queries_short.shape[0]
    token_count = queries_short.shape[1]
    blocks = seq_allreduce(
        lax.axis_size("seq"),
        short_len,
        queries_short,
        fresh_short,
        cache_short,
        long_len,
        block_live.T,
        queries_long,
        fresh_long,
        cache_long,
        out_weight,
        lax.axis_size("tp"),
    )
    short_count = request_count * token_count
    cols = blocks
    short_out = cols[:short_count].reshape(request_count, token_count, cols.shape[1])
    long_out = cols[short_count:].reshape(
        queries_long.shape[0], queries_long.shape[1], cols.shape[1]
    )
    return (short_out, long_out)


def solution(mesh):
    in_specs = (
        P("seq", None, "tp"),
        P(None, "seq", None, "tp"),
        P(None, "seq", None, "tp"),
        P("seq"),
        P(None, None, "tp"),
        P(None, None, "seq", "tp"),
        P(None, None, None, "tp"),
        P(),
        P(None, "seq"),
        P("tp", None),
    )
    out_specs = (P("seq", None, "tp"), P(None, None, "tp"))
    return jax.shard_map(
        per_device, mesh=mesh, in_specs=in_specs, out_specs=out_specs, check_vma=False
    )
```

```python
import functools
import math

import jax
import jax.numpy as jnp
from jax import lax
from jax.experimental import pallas as pl
from jax.experimental.pallas import tpu as pltpu
from jax.sharding import PartitionSpec as P

HEAD_DIM = 64
MESH = pl.DeviceIdType.MESH
LANES = 128


NEGATIVE = -1e30


def split_heads(tensor):
    return tensor.reshape(tensor.shape[0], tensor.shape[1], tensor.shape[2] // HEAD_DIM, HEAD_DIM)


def partial_softmax(query_heads, key_heads, value_heads, usable):
    scores = jnp.einsum(
        "rjhd,rphd->rhjp", query_heads, key_heads, preferred_element_type=jnp.float32
    ) * (1.0 / math.sqrt(HEAD_DIM))
    scores = jnp.where(usable, scores, NEGATIVE)
    highest = jnp.max(scores, axis=-1)
    expo = jnp.where(usable, jnp.exp(scores - highest[..., None]), 0.0)
    totals = jnp.sum(expo, axis=-1)
    summed = jnp.einsum(
        "rhjp,rphd->rhjd",
        expo.astype(jnp.bfloat16),
        value_heads,
        preferred_element_type=jnp.float32,
    )
    return (highest, totals, summed)


def combine_parts(first, second):
    highest = jnp.maximum(first[0], second[0])
    scale_first = jnp.exp(first[0] - highest)
    scale_second = jnp.exp(second[0] - highest)
    totals = first[1] * scale_first + second[1] * scale_second
    summed = first[2] * scale_first[..., None] + second[2] * scale_second[..., None]
    return (highest, totals, summed)


def finish(parts):
    normed = (parts[2] / parts[1][..., None]).astype(jnp.bfloat16)
    normed = jnp.transpose(normed, (0, 2, 1, 3))
    return normed.reshape(normed.shape[0], normed.shape[1], normed.shape[2] * normed.shape[3])


def fresh_part(queries, fresh):
    count = queries.shape[1]
    causal = (jnp.arange(count)[:, None] >= jnp.arange(count)[None, :])[None, None]
    return partial_softmax(
        split_heads(queries), split_heads(fresh[0]), split_heads(fresh[1]), causal
    )


def merge_states(low, high):
    lane = lax.broadcasted_iota(jnp.int32, low.shape, low.ndim - 1)
    top_low = low[..., HEAD_DIM : HEAD_DIM + 1]
    top_high = high[..., HEAD_DIM : HEAD_DIM + 1]
    top = jnp.maximum(top_low, top_high)
    mixed = low * jnp.exp(top_low - top) + high * jnp.exp(top_high - top)
    return jnp.where(lane == HEAD_DIM, top, mixed)


def short_request(q, k_view, v_view, usable, fk, fv):
    tokens, width = q.shape
    rows = (width // HEAD_DIM) * tokens
    pick = (
        lax.broadcasted_iota(jnp.int32, (rows, tokens), 0) % tokens
        == lax.broadcasted_iota(jnp.int32, (rows, tokens), 1)
    ).astype(jnp.bfloat16)
    head_lanes = (
        lax.broadcasted_iota(jnp.int32, (rows, width), 0) // tokens
        == lax.broadcasted_iota(jnp.int32, (rows, width), 1) // HEAD_DIM
    )
    spread = jnp.dot(pick, q, preferred_element_type=jnp.float32)
    query = jnp.where(head_lanes, spread, 0.0).astype(jnp.bfloat16)
    contract = (((1,), (1,)), ((), ()))
    scale = 1.0 / math.sqrt(HEAD_DIM)
    scores = jnp.dot(query, k_view[...], preferred_element_type=jnp.float32) * scale
    scores = jnp.where(usable, scores, NEGATIVE)
    fresh_scores = lax.dot_general(query, fk, contract, preferred_element_type=jnp.float32) * scale
    causal = lax.broadcasted_iota(jnp.int32, (rows, tokens), 1) <= (
        lax.broadcasted_iota(jnp.int32, (rows, tokens), 0) % tokens
    )
    fresh_scores = jnp.where(causal, fresh_scores, NEGATIVE)
    highest = jnp.maximum(
        jnp.max(scores, axis=1, keepdims=True), jnp.max(fresh_scores, axis=1, keepdims=True)
    )
    expo = jnp.where(usable, jnp.exp(scores - highest), 0.0)
    fresh_expo = jnp.where(causal, jnp.exp(fresh_scores - highest), 0.0)
    totals = jnp.sum(expo, axis=1, keepdims=True) + jnp.sum(fresh_expo, axis=1, keepdims=True)
    summed = lax.dot_general(
        expo.astype(jnp.bfloat16), v_view[...], contract, preferred_element_type=jnp.float32
    ) + jnp.dot(fresh_expo.astype(jnp.bfloat16), fv, preferred_element_type=jnp.float32)
    normed = jnp.where(head_lanes, (summed / totals).astype(jnp.bfloat16), 0.0)
    gather = (
        lax.broadcasted_iota(jnp.int32, (tokens, rows), 1) % tokens
        == lax.broadcasted_iota(jnp.int32, (tokens, rows), 0)
    ).astype(jnp.bfloat16)
    return jnp.dot(gather, normed.astype(jnp.bfloat16), preferred_element_type=jnp.float32)


def finish_long(state, q, fk, fv):
    tokens, width = q.shape
    rows = (width // HEAD_DIM) * tokens
    pick = (
        lax.broadcasted_iota(jnp.int32, (rows, tokens), 0) % tokens
        == lax.broadcasted_iota(jnp.int32, (rows, tokens), 1)
    ).astype(jnp.bfloat16)
    head_lanes = (
        lax.broadcasted_iota(jnp.int32, (rows, width), 0) // tokens
        == lax.broadcasted_iota(jnp.int32, (rows, width), 1) // HEAD_DIM
    )
    spread = jnp.dot(pick, q, preferred_element_type=jnp.float32)
    query = jnp.where(head_lanes, spread, 0.0).astype(jnp.bfloat16)
    contract = (((1,), (1,)), ((), ()))
    fresh_scores = lax.dot_general(
        query, fk, contract, preferred_element_type=jnp.float32
    ) * (1.0 / math.sqrt(HEAD_DIM))
    causal = lax.broadcasted_iota(jnp.int32, (rows, tokens), 1) <= (
        lax.broadcasted_iota(jnp.int32, (rows, tokens), 0) % tokens
    )
    fresh_scores = jnp.where(causal, fresh_scores, NEGATIVE)
    top = state[:, HEAD_DIM : HEAD_DIM + 1]
    highest = jnp.maximum(top, jnp.max(fresh_scores, axis=1, keepdims=True))
    kept = jnp.exp(top - highest)
    fresh_expo = jnp.where(causal, jnp.exp(fresh_scores - highest), 0.0)
    totals = state[:, HEAD_DIM + 1 : HEAD_DIM + 2] * kept + jnp.sum(
        fresh_expo, axis=1, keepdims=True
    )
    fresh_sum = jnp.where(
        head_lanes,
        jnp.dot(fresh_expo.astype(jnp.bfloat16), fv, preferred_element_type=jnp.float32),
        0.0,
    )
    folded = fresh_sum[:, 0:HEAD_DIM]
    for g in range(1, width // HEAD_DIM):
        folded = folded + fresh_sum[:, g * HEAD_DIM : (g + 1) * HEAD_DIM]
    normed = ((state[:, :HEAD_DIM] * kept + folded) / totals).astype(jnp.float32)
    spread_back = jnp.concatenate([normed] * (width // HEAD_DIM), axis=1)
    placed = jnp.where(head_lanes, spread_back.astype(jnp.bfloat16), 0.0).astype(jnp.bfloat16)
    gather = (
        lax.broadcasted_iota(jnp.int32, (tokens, rows), 1) % tokens
        == lax.broadcasted_iota(jnp.int32, (tokens, rows), 0)
    ).astype(jnp.bfloat16)
    return jnp.dot(gather, placed, preferred_element_type=jnp.float32)


def long_request(q, k_view, v_view, usable):
    tokens, width = q.shape
    rows = (width // HEAD_DIM) * tokens
    pick = (
        lax.broadcasted_iota(jnp.int32, (rows, tokens), 0) % tokens
        == lax.broadcasted_iota(jnp.int32, (rows, tokens), 1)
    ).astype(jnp.bfloat16)
    head_lanes = (
        lax.broadcasted_iota(jnp.int32, (rows, width), 0) // tokens
        == lax.broadcasted_iota(jnp.int32, (rows, width), 1) // HEAD_DIM
    )
    spread = jnp.dot(pick, q, preferred_element_type=jnp.float32)
    query = jnp.where(head_lanes, spread, 0.0).astype(jnp.bfloat16)
    contract = (((1,), (1,)), ((), ()))
    scores = jnp.dot(query, k_view[...], preferred_element_type=jnp.float32) * (
        1.0 / math.sqrt(HEAD_DIM)
    )
    scores = jnp.where(usable, scores, NEGATIVE)
    highest = jnp.max(scores, axis=1, keepdims=True)
    expo = jnp.where(usable, jnp.exp(scores - highest), 0.0)
    totals = jnp.sum(expo, axis=1, keepdims=True)
    summed = lax.dot_general(
        expo.astype(jnp.bfloat16), v_view[...], contract, preferred_element_type=jnp.float32
    )
    masked = jnp.where(head_lanes, summed, 0.0)
    folded = masked[:, 0:HEAD_DIM]
    for g in range(1, width // HEAD_DIM):
        folded = folded + masked[:, g * HEAD_DIM : (g + 1) * HEAD_DIM]
    return jnp.concatenate(
        [folded, highest, totals, jnp.zeros((rows, LANES - HEAD_DIM - 2), jnp.float32)],
        axis=1,
    )


def butterfly_kernel(
    rounds, parts, len_ref, llen_ref, live_ref, q_ref, f_ref, cache_ref, ql_ref, fl_ref,
    lcache_ref, w_ref, out_ref, att_ref, state, recv, send_sem, recv_sem, kv_buf, kv_sem, lkv_buf, lkv_sem,
    blk, tp_recv, tp_local, tp_send, tp_sem,
):
    me = lax.axis_index("seq")
    column = lax.axis_index("tp")
    count, tokens = q_ref.shape[0], q_ref.shape[1]
    long_count = ql_ref.shape[0]
    long_loads = []
    for r in range(long_count):
        pair = []
        for kv in range(2):
            load = pltpu.make_async_copy(
                lcache_ref.at[kv, r], lkv_buf.at[kv, r], lkv_sem.at[kv, r]
            )
            load.start()
            pair.append(load)
        long_loads.append(pair)
    loads = []
    for r in range(count):
        pair = []
        for kv in range(2):
            load = pltpu.make_async_copy(
                cache_ref.at[kv, r], kv_buf.at[kv, r], kv_sem.at[kv, r]
            )
            load.start()
            pair.append(load)
        loads.append(pair)

    def short_step(r):
        for load in loads[r]:
            load.wait()
        spot = lax.broadcasted_iota(jnp.int32, (1, kv_buf.shape[3]), 1)
        att_ref[r * tokens : (r + 1) * tokens] = short_request(
            q_ref[r], kv_buf.at[0, r], kv_buf.at[1, r], spot < len_ref[r],
            f_ref[0, r], f_ref[1, r],
        ).astype(att_ref.dtype)

    def project(lo, hi):
        term = jnp.dot(att_ref[lo:hi], w_ref[...], preferred_element_type=jnp.float32)
        cols = w_ref.shape[1] // parts
        for q in range(parts):
            blk[q, lo:hi] = term[:, q * cols : (q + 1) * cols]

    partners = []
    for k in range(rounds):
        step = 1 << k
        bit = (me // step) % 2
        partners.append((me + step - 2 * step * bit, bit))
    barrier = pltpu.get_barrier_semaphore()
    for partner, _ in partners:
        pl.semaphore_signal(
            barrier, inc=1, device_id=(partner, column), device_id_type=MESH
        )
    for d in range(1, parts):
        pl.semaphore_signal(
            barrier, inc=1, device_id=(me, (column + d) % parts), device_id_type=MESH
        )
    positions = lkv_buf.shape[3]
    spot = lax.broadcasted_iota(jnp.int32, (1, positions), 1)
    blocks = live_ref.shape[0]
    for r in range(long_count):
        alive = spot < 0
        for b in range(blocks):
            alive = alive | (
                (spot // (positions // blocks) == b) & (live_ref[b, r] == 1)
            )
        usable = alive & (spot + me * positions < llen_ref[r])
        for load in long_loads[r]:
            load.wait()
        state[0, r] = long_request(ql_ref[r], lkv_buf.at[0, r], lkv_buf.at[1, r], usable)
    pl.semaphore_wait(barrier, rounds + parts - 1)
    for k in range(rounds):
        partner, bit = partners[k]
        source = state.at[k]
        copy = pltpu.make_async_remote_copy(
            src_ref=source,
            dst_ref=recv.at[k],
            send_sem=send_sem.at[k],
            recv_sem=recv_sem.at[k],
            device_id=(partner, column),
            device_id_type=MESH,
        )
        copy.start()
        if k < count:
            short_step(k)
        if k == count:
            project(0, count * tokens)
        copy.wait()
        mine = source[...]
        theirs = recv[k]
        first = bit == 0
        merged = merge_states(
            jnp.where(first, mine, theirs), jnp.where(first, theirs, mine)
        )
        if k == rounds - 1:
            for r in range(ql_ref.shape[0]):
                row = (count + r) * tokens
                att_ref[row : row + tokens] = finish_long(
                    merged[r], ql_ref[r], fl_ref[0, r], fl_ref[1, r]
                ).astype(att_ref.dtype)
        else:
            state[k + 1] = merged
    for r in range(rounds, count):
        short_step(r)
    if count >= rounds:
        project(0, count * tokens)
    project(count * tokens, att_ref.shape[0])
    own = pltpu.make_async_copy(blk.at[column], tp_recv.at[column], tp_local)
    own.start()
    sends = []
    for d in range(1, parts):
        send = pltpu.make_async_remote_copy(
            src_ref=blk.at[(column + d) % parts],
            dst_ref=tp_recv.at[column],
            send_sem=tp_send.at[d - 1],
            recv_sem=tp_sem.at[d - 1],
            device_id=(me, (column + d) % parts),
            device_id_type=MESH,
        )
        send.start()
        sends.append(send)
    own.wait()
    for d in range(1, parts):
        sends[d - 1].wait_send()
        pltpu.make_async_remote_copy(
            src_ref=blk.at[0],
            dst_ref=tp_recv.at[(column + parts - d) % parts],
            send_sem=tp_send.at[d - 1],
            recv_sem=tp_sem.at[d - 1],
            device_id=(me, (column + parts - d) % parts),
            device_id_type=MESH,
        ).wait_recv()
    total = tp_recv[0]
    for s in range(1, parts):
        total = total + tp_recv[s]
    out_ref[...] = total


def seq_allreduce(
    devices, lengths, queries, fresh, cache, long_len, live, queries_long, fresh_long, cache_long,
    weight, parts,
):
    rounds = devices.bit_length() - 1
    tokens, width = queries.shape[1], queries.shape[2]
    rows = (width // HEAD_DIM) * tokens
    state_shape = (queries_long.shape[0], rows, LANES)
    block_shape = (
        parts,
        (queries.shape[0] + queries_long.shape[0]) * tokens,
        weight.shape[1] // parts,
    )
    flipped = jnp.swapaxes(cache, 2, 3)
    flipped_long = jnp.swapaxes(cache_long, 2, 3)
    vmem = pl.BlockSpec(memory_space=pltpu.VMEM)
    smem = pl.BlockSpec(memory_space=pltpu.SMEM)
    hbm = pl.BlockSpec(memory_space=pl.ANY)
    return pl.pallas_call(
        functools.partial(butterfly_kernel, rounds, parts),
        out_shape=jax.ShapeDtypeStruct(
            ((queries.shape[0] + queries_long.shape[0]) * tokens, weight.shape[1] // parts),
            jnp.float32,
        ),
        in_specs=[smem, smem, smem, vmem, vmem, hbm, vmem, vmem, hbm, vmem],
        out_specs=vmem,
        scratch_shapes=[
            pltpu.VMEM(((queries.shape[0] + queries_long.shape[0]) * tokens, width), jnp.bfloat16),
            pltpu.VMEM((rounds,) + state_shape, jnp.float32),
            pltpu.VMEM((rounds,) + state_shape, jnp.float32),
            pltpu.SemaphoreType.DMA((rounds,)),
            pltpu.SemaphoreType.DMA((rounds,)),
            pltpu.VMEM(flipped.shape, flipped.dtype),
            pltpu.SemaphoreType.DMA(flipped.shape[:2]),
            pltpu.VMEM(flipped_long.shape, flipped_long.dtype),
            pltpu.SemaphoreType.DMA(flipped_long.shape[:2]),
            pltpu.VMEM(block_shape, jnp.float32),
            pltpu.VMEM(block_shape, jnp.float32),
            pltpu.SemaphoreType.DMA(()),
            pltpu.SemaphoreType.DMA((parts - 1,)),
            pltpu.SemaphoreType.DMA((parts - 1,)),
        ],
        compiler_params=pltpu.CompilerParams(collective_id=0, has_side_effects=True),
        cost_estimate=pl.CostEstimate(
            flops=4 * rows * (queries.shape[0] * cache.size + queries_long.shape[0] * cache_long.size),
            transcendentals=rows * (cache.size + cache_long.size) // width,
            bytes_accessed=2 * (cache.size + cache_long.size),
        ),
    )(lengths, long_len, live, queries, fresh, flipped, queries_long, fresh_long, flipped_long, weight)


def scatter_kernel(parts, x_ref, o_ref, recv, local_sem, send_sem, recv_sem):
    me = lax.axis_index("tp")
    row = lax.axis_index("seq")
    barrier = pltpu.get_barrier_semaphore()
    for d in range(1, parts):
        pl.semaphore_signal(
            barrier, inc=1, device_id=(row, (me + d) % parts), device_id_type=MESH
        )
    pl.semaphore_wait(barrier, parts - 1)
    own = pltpu.make_async_copy(x_ref.at[me], recv.at[me], local_sem)
    own.start()
    copies = []
    for d in range(1, parts):
        copy = pltpu.make_async_remote_copy(
            src_ref=x_ref.at[(me + d) % parts],
            dst_ref=recv.at[me],
            send_sem=send_sem.at[d - 1],
            recv_sem=recv_sem.at[d - 1],
            device_id=(row, (me + d) % parts),
            device_id_type=MESH,
        )
        copy.start()
        copies.append(copy)
    own.wait()
    for d in range(1, parts):
        copies[d - 1].wait_send()
        pltpu.make_async_remote_copy(
            src_ref=x_ref.at[0],
            dst_ref=recv.at[(me + parts - d) % parts],
            send_sem=send_sem.at[d - 1],
            recv_sem=recv_sem.at[d - 1],
            device_id=(row, (me + parts - d) % parts),
            device_id_type=MESH,
        ).wait_recv()
    total = recv[0]
    for s in range(1, parts):
        total = total + recv[s]
    o_ref[...] = total


def tp_reduce_scatter(blocks):
    parts, rows, cols = blocks.shape
    return pl.pallas_call(
        functools.partial(scatter_kernel, parts),
        out_shape=jax.ShapeDtypeStruct((rows, cols), jnp.float32),
        in_specs=[pl.BlockSpec(memory_space=pltpu.VMEM)],
        out_specs=pl.BlockSpec(memory_space=pltpu.VMEM),
        scratch_shapes=[
            pltpu.VMEM((parts, rows, cols), jnp.float32),
            pltpu.SemaphoreType.DMA(()),
            pltpu.SemaphoreType.DMA((parts - 1,)),
            pltpu.SemaphoreType.DMA((parts - 1,)),
        ],
        compiler_params=pltpu.CompilerParams(collective_id=1, has_side_effects=True),
        cost_estimate=pl.CostEstimate(
            flops=rows * cols * parts,
            transcendentals=0,
            bytes_accessed=3 * rows * cols * parts * 4,
        ),
    )(blocks)


def attention_kernel(with_fresh, len_ref, live_ref, off_ref, q_ref, k_ref, v_ref, *rest):
    tokens, width = q_ref.shape[1], q_ref.shape[2]
    positions = k_ref.shape[3]
    rows = (width // HEAD_DIM) * tokens
    request = pl.program_id(0)
    spot = lax.broadcasted_iota(jnp.int32, (1, positions), 1)
    usable = spot + off_ref[0] < len_ref[request]
    if not with_fresh:
        blocks = live_ref.shape[0]
        alive = spot < 0
        for b in range(blocks):
            alive = alive | (
                (spot // (positions // blocks) == b) & (live_ref[b, request] == 1)
            )
        usable = usable & alive
    pick = (
        lax.broadcasted_iota(jnp.int32, (rows, tokens), 0) % tokens
        == lax.broadcasted_iota(jnp.int32, (rows, tokens), 1)
    ).astype(jnp.bfloat16)
    head_lanes = (
        lax.broadcasted_iota(jnp.int32, (rows, width), 0) // tokens
        == lax.broadcasted_iota(jnp.int32, (rows, width), 1) // HEAD_DIM
    )
    spread = jnp.dot(pick, q_ref[0], preferred_element_type=jnp.float32)
    query = jnp.where(head_lanes, spread, 0.0).astype(jnp.bfloat16)
    contract = (((1,), (1,)), ((), ()))
    scale = 1.0 / math.sqrt(HEAD_DIM)
    scores = jnp.dot(query, k_ref[0, 0], preferred_element_type=jnp.float32) * scale
    scores = jnp.where(usable, scores, NEGATIVE)
    highest = jnp.max(scores, axis=1, keepdims=True)
    if with_fresh:
        fk_ref, fv_ref, o_ref = rest
        fresh_scores = lax.dot_general(
            query, fk_ref[0, 0], contract, preferred_element_type=jnp.float32
        ) * scale
        causal = lax.broadcasted_iota(jnp.int32, (rows, tokens), 1) <= (
            lax.broadcasted_iota(jnp.int32, (rows, tokens), 0) % tokens
        )
        fresh_scores = jnp.where(causal, fresh_scores, NEGATIVE)
        highest = jnp.maximum(highest, jnp.max(fresh_scores, axis=1, keepdims=True))
    expo = jnp.where(usable, jnp.exp(scores - highest), 0.0)
    totals = jnp.sum(expo, axis=1, keepdims=True)
    summed = lax.dot_general(
        expo.astype(jnp.bfloat16), v_ref[0, 0], contract, preferred_element_type=jnp.float32
    )
    if with_fresh:
        fresh_expo = jnp.where(causal, jnp.exp(fresh_scores - highest), 0.0)
        totals = totals + jnp.sum(fresh_expo, axis=1, keepdims=True)
        summed = summed + jnp.dot(
            fresh_expo.astype(jnp.bfloat16), fv_ref[0, 0], preferred_element_type=jnp.float32
        )
        normed = jnp.where(head_lanes, (summed / totals).astype(jnp.bfloat16), 0.0)
        gather = (
            lax.broadcasted_iota(jnp.int32, (tokens, rows), 1) % tokens
            == lax.broadcasted_iota(jnp.int32, (tokens, rows), 0)
        ).astype(jnp.bfloat16)
        o_ref[0] = jnp.dot(
            gather, normed.astype(jnp.bfloat16), preferred_element_type=jnp.float32
        ).astype(o_ref.dtype)
    else:
        (out_ref,) = rest
        masked = jnp.where(head_lanes, summed, 0.0)
        folded = masked[:, 0:HEAD_DIM]
        for g in range(1, width // HEAD_DIM):
            folded = folded + masked[:, g * HEAD_DIM : (g + 1) * HEAD_DIM]
        out_ref[0] = jnp.concatenate(
            [
                folded,
                highest,
                totals,
                jnp.zeros((rows, LANES - HEAD_DIM - 2), jnp.float32),
            ],
            axis=1,
        )


def attention(queries, cache, lengths, live, offset, fresh=None):
    count, tokens, width = queries.shape
    positions = cache.shape[2]
    rows = (width // HEAD_DIM) * tokens
    flipped = jnp.swapaxes(cache, 2, 3)
    specs = [
        pl.BlockSpec((1, tokens, width), lambda r, *_: (r, 0, 0)),
        pl.BlockSpec((1, 1, width, positions), lambda r, *_: (0, r, 0, 0)),
        pl.BlockSpec((1, 1, width, positions), lambda r, *_: (1, r, 0, 0)),
    ]
    operands = [lengths, live, offset, queries, flipped, flipped]
    if fresh is not None:
        specs += [
            pl.BlockSpec((1, 1, tokens, width), lambda r, *_: (0, r, 0, 0)),
            pl.BlockSpec((1, 1, tokens, width), lambda r, *_: (1, r, 0, 0)),
        ]
        operands += [fresh, fresh]
        out_shape = jax.ShapeDtypeStruct((count, tokens, width), jnp.bfloat16)
        out_specs = pl.BlockSpec((1, tokens, width), lambda r, *_: (r, 0, 0))
    else:
        out_shape = jax.ShapeDtypeStruct((count, rows, LANES), jnp.float32)
        out_specs = pl.BlockSpec((1, rows, LANES), lambda r, *_: (r, 0, 0))
    return pl.pallas_call(
        functools.partial(attention_kernel, fresh is not None),
        out_shape=out_shape,
        grid_spec=pltpu.PrefetchScalarGridSpec(
            num_scalar_prefetch=3, grid=(count,), in_specs=specs, out_specs=out_specs
        ),
        cost_estimate=pl.CostEstimate(
            flops=4 * count * rows * positions * width,
            transcendentals=count * rows * positions,
            bytes_accessed=2 * count * positions * width * 2,
        ),
    )(*operands)


def per_device(
    queries_short,
    cache_short,
    fresh_short,
    short_len,
    queries_long,
    cache_long,
    fresh_long,
    long_len,
    block_live,
    out_weight,
):
    request_count = queries_short.shape[0]
    token_count = queries_short.shape[1]
    blocks = seq_allreduce(
        lax.axis_size("seq"),
        short_len,
        queries_short,
        fresh_short,
        cache_short,
        long_len,
        block_live.T,
        queries_long,
        fresh_long,
        cache_long,
        out_weight,
        lax.axis_size("tp"),
    )
    short_count = request_count * token_count
    cols = blocks.astype(jnp.bfloat16)
    short_out = cols[:short_count].reshape(request_count, token_count, cols.shape[1])
    long_out = cols[short_count:].reshape(
        queries_long.shape[0], queries_long.shape[1], cols.shape[1]
    )
    return (short_out, long_out)


def solution(mesh):
    in_specs = (
        P("seq", None, "tp"),
        P(None, "seq", None, "tp"),
        P(None, "seq", None, "tp"),
        P("seq"),
        P(None, None, "tp"),
        P(None, None, "seq", "tp"),
        P(None, None, None, "tp"),
        P(),
        P(None, "seq"),
        P("tp", None),
    )
    out_specs = (P("seq", None, "tp"), P(None, None, "tp"))
    return jax.shard_map(
        per_device, mesh=mesh, in_specs=in_specs, out_specs=out_specs, check_vma=False
    )
```
